128 devices in a mesh: fsdp: 16 (over x_lo, y, core), tp: 8 (over x_hi, z).
Axes of the slice: x: 4 (x_hi: 2, x_lo: 2; x = x_hi * 2 + x_lo), y: 4, z: 4, core: 2. Of those that a mesh axis runs over, the one named last changes fastest.
Arguments:
- tokens: bfloat16 [16384, 2048], P(('fsdp', 'tp')), may hold values from -6 to 6
- grad_out: bfloat16 [16384, 2048], P(('fsdp', 'tp')), may hold values from -6 to 6
- adapter_ids: int32 [16], P('fsdp'), may hold values from 0 to 7
- first_gain: float32 [2048], replicated, may hold values from 0.1 to 1.9
- first_shift: float32 [2048], replicated, may hold values from -4 to 4
- joined_weight: bfloat16 [2048, 6144], P('fsdp', 'tp'), may hold values from -0.125 to 0.125
- joined_bias: float32 [6144], P('tp'), may hold values from -4 to 4
- dense_weight: bfloat16 [2048, 2048], P('tp', 'fsdp'), may hold values from -0.5 to 0.5
- dense_bias: float32 [2048], replicated, may hold values from -4 to 4
- second_gain: float32 [2048], replicated, may hold values from 0.1 to 1.9
- second_shift: float32 [2048], replicated, may hold values from -4 to 4
- up_weight: bfloat16 [2048, 8192], P('fsdp', 'tp'), may hold values from -0.125 to 0.125
- up_bias: float32 [8192], P('tp'), may hold values from -6 to 6
- down_weight: bfloat16 [8192, 2048], P('tp', 'fsdp'), may hold values from -0.125 to 0.125
- down_bias: float32 [2048], replicated, may hold values from -4 to 4
- joined_adapt_in: bfloat16 [8, 2048, 16], replicated, may hold values from -0.125 to 0.125
- joined_adapt_out: bfloat16 [8, 16, 6144], P(None, None, 'tp'), may hold values from -2 to 2
- dense_adapt_in: bfloat16 [8, 2048, 16], P(None, 'tp'), may hold values from -0.5 to 0.5
- dense_adapt_out: bfloat16 [8, 16, 2048], replicated, may hold values from -2 to 2
- up_adapt_in: bfloat16 [8, 2048, 16], replicated, may hold values from -0.125 to 0.125
- up_adapt_out: bfloat16 [8, 16, 8192], P(None, None, 'tp'), may hold values from -2 to 2
- down_adapt_in: bfloat16 [8, 8192, 16], P(None, 'tp'), may hold values from -0.125 to 0.125
- down_adapt_out: bfloat16 [8, 16, 2048], replicated, may hold values from -2 to 2
Outputs:
- layer_out: bfloat16 [16384, 2048], P(('fsdp', 'tp'))
- grad_tokens: float32 [16384, 2048], P(('fsdp', 'tp'))
- grad_joined_in: float32 [8, 2048, 16], replicated
- grad_joined_out: float32 [8, 16, 6144], P(None, None, 'tp')
- grad_dense_in: float32 [8, 2048, 16], P(None, 'tp')
- grad_dense_out: float32 [8, 16, 2048], replicated
- grad_up_in: float32 [8, 2048, 16], replicated
- grad_up_out: float32 [8, 16, 8192], P(None, None, 'tp')
- grad_down_in: float32 [8, 8192, 16], P(None, 'tp')
- grad_down_out: float32 [8, 16, 2048], replicated
The draws below stay inside these ranges and needn't reach their ends.
All inputs are finite; a program needn't handle non-finite values.
Results may differ from the reference program's by a relative error of at most 0.02.
Values may be sent and summed in bfloat16 or wider, within the bound.
A program may use at most 128 MiB of HBM per device.

```python
import jax
import jax.numpy as jnp
from jax import lax

D = 2048
HEADS = 32
HEAD_DIM = 64
FF = 8192
RANK = 16
ADAPTERS = 8
LEN = 1024
SEQS = 16
TOKENS = 16384
N_TP = 8


def set_ends(entries, own_key, least, largest):
    spot = [jax.random.randint(jax.random.fold_in(own_key, axis), (), 0, length) for axis, length in enumerate(entries.shape)]
    longest = entries.shape.index(max(entries.shape))
    beside = spot[:longest] + [(spot[longest] + 1) % entries.shape[longest]] + spot[longest + 1:]
    return entries.at[tuple(spot)].set(least).at[tuple(beside)].set(largest)


def shard_levels(stream_key, shape, split, smallest, high):
    loudness, own = 1.0, jax.random.fold_in(stream_key, 6)
    for axis_at, shards_of in split:
        draws = jnp.exp(jax.random.uniform(jax.random.fold_in(own, axis_at), (shards_of,), jnp.float32, smallest / len(split), high / len(split)))
        loudness = loudness * jnp.repeat(draws, shape[axis_at] // shards_of).reshape([-1 if axis == axis_at else 1 for axis in range(len(shape))])
    return loudness


def normal_values(stream_key, shape, deviation, reach, cuts=(), kind=jnp.bfloat16):
    array = deviation * jax.random.normal(stream_key, shape, jnp.float32)
    if cuts:
        array = array * shard_levels(stream_key, shape, cuts, -0.22, 0.18)
    return jnp.clip(array, -reach, reach).astype(kind)


def setup_inputs(seed: int = 0) -> dict:
    key_of = jax.random.split(jax.random.key(seed), 24)
    return {
        "tokens": normal_values(key_of[0], (TOKENS, D), 1.0, 6.0, ((0, 128),)),
        "grad_out": normal_values(key_of[1], (TOKENS, D), 1.0, 6.0, ((0, 128),)),
        "adapter_ids": set_ends(jax.random.randint(key_of[2], (SEQS,), 0, ADAPTERS), jax.random.fold_in(key_of[2], 1), 0, ADAPTERS - 1).astype(jnp.int32),
        "first_gain": jnp.clip(1.0 + 0.18 * jax.random.normal(key_of[3], (D,), jnp.float32), 0.1, 1.9),
        "first_shift": normal_values(key_of[4], (D,), 0.3, 4.0, (), jnp.float32),
        "joined_weight": normal_values(key_of[5], (D, 3 * D), D ** -0.5, 0.125, ((0, 16), (1, 8))),
        "joined_bias": normal_values(key_of[6], (3 * D,), 0.3, 4.0, ((0, 8),), jnp.float32),
        "dense_weight": normal_values(key_of[7], (D, D), (D // 16) ** -0.5, 0.5, ((0, 8), (1, 16))),
        "dense_bias": normal_values(key_of[8], (D,), 0.3, 4.0, (), jnp.float32),
        "second_gain": jnp.clip(1.0 + 0.18 * jax.random.normal(key_of[9], (D,), jnp.float32), 0.1, 1.9),
        "second_shift": normal_values(key_of[10], (D,), 0.3, 4.0, (), jnp.float32),
        "up_weight": normal_values(key_of[11], (D, FF), D ** -0.5, 0.125, ((0, 16), (1, 8))),
        "up_bias": normal_values(key_of[12], (FF,), 0.5, 6.0, ((0, 8),), jnp.float32),
        "down_weight": normal_values(key_of[13], (FF, D), (FF // 4) ** -0.5, 0.125, ((0, 8), (1, 16))),
        "down_bias": normal_values(key_of[14], (D,), 0.3, 4.0, (), jnp.float32),
        "joined_adapt_in": normal_values(key_of[15], (ADAPTERS, D, RANK), D ** -0.5, 0.125),
        "joined_adapt_out": normal_values(key_of[16], (ADAPTERS, RANK, 3 * D), 0.15, 2.0, ((2, 8),)),
        "dense_adapt_in": normal_values(key_of[17], (ADAPTERS, D, RANK), (D // 16) ** -0.5, 0.5, ((1, 8),)),
        "dense_adapt_out": normal_values(key_of[18], (ADAPTERS, RANK, D), 0.15, 2.0),
        "up_adapt_in": normal_values(key_of[19], (ADAPTERS, D, RANK), D ** -0.5, 0.125),
        "up_adapt_out": normal_values(key_of[20], (ADAPTERS, RANK, FF), 0.15, 2.0, ((2, 8),)),
        "down_adapt_in": normal_values(key_of[21], (ADAPTERS, FF, RANK), (FF // 4) ** -0.5, 0.125, ((1, 8),)),
        "down_adapt_out": normal_values(key_of[22], (ADAPTERS, RANK, D), 0.15, 2.0),
    }


EPSILON = 1e-05
MASKED = -1e+30
HIGHEST = lax.Precision.HIGHEST

@jax.custom_vjp
def low(v):
    return lax.optimization_barrier(v.astype(jnp.bfloat16)).astype(jnp.float32)

@jax.custom_vjp
def low_back(v):
    return v

def low_keep(v):
    return (low(v), None)

def low_pass(kept, grad):
    return (grad,)

def back_keep(v):
    return (v, None)

def back_low(kept, grad):
    return (low(grad),)
low.defvjp(low_keep, low_pass)
low_back.defvjp(back_keep, back_low)

def layer_norm(rows_in, gain, shift):
    row_mean = lax.optimization_barrier(jnp.mean(rows_in, axis=-1, keepdims=True))
    centered = rows_in - row_mean
    variance = lax.optimization_barrier(jnp.mean(centered * centered, axis=-1, keepdims=True))
    return centered * lax.rsqrt(variance + EPSILON) * gain + shift

def matmul(first_arg, second_arg):
    return jnp.dot(first_arg, second_arg, precision=HIGHEST)

def select_set(onehot, tensor_in):
    return jnp.einsum('a,a...->...', onehot, tensor_in, precision=HIGHEST)

def sequence_forward(seq_rows, chosen, frozen):
    first_gain, first_shift, joined_weight, joined_bias, dense_weight, dense_bias, second_gain, second_shift, up_weight, up_bias, down_weight, down_bias = frozen
    joined_in, joined_out, dense_in, dense_out, up_in, up_out, down_in, down_out = chosen
    length = seq_rows.shape[0]
    columns = 3 * D // N_TP
    head_group = HEADS // N_TP
    model_part = D // N_TP
    hidden_part = FF // N_TP
    slopes = jnp.exp2(-8.0 * (jnp.arange(HEADS) + 1).astype(jnp.float32) / HEADS).reshape(N_TP, head_group)
    positions = jnp.arange(length)
    distance = (positions[:, None] - positions[None, :]).astype(jnp.float32)
    causal = distance >= 0
    normed_one = low(layer_norm(seq_rows, first_gain, first_shift))

    def attention_group(running, pieces):
        w_joined, b_joined, joined_up, w_dense, dense_down, slope_group = pieces
        copy_one = low_back(normed_one)
        low_joined = low(low_back(matmul(copy_one, joined_in)))
        joined_cols = low(low_back(matmul(copy_one, w_joined) + b_joined + matmul(low_joined, joined_up)))
        joined_heads = joined_cols.reshape(length, head_group, 3, HEAD_DIM)
        raw_scores = jnp.einsum('qhe,khe->hqk', joined_heads[:, :, 0, :], joined_heads[:, :, 1, :], precision=HIGHEST)
        scores = low_back((raw_scores - slope_group[:, None, None] * distance[None]) / 8.0)
        scores = jnp.where(causal[None], scores, MASKED)
        row_max = lax.optimization_barrier(jnp.max(scores, axis=-1, keepdims=True))
        exp_scores = jnp.exp(scores - row_max)
        attn_probs = low(exp_scores / lax.optimization_barrier(jnp.sum(exp_scores, axis=-1, keepdims=True)))
        context = low(low_back(jnp.einsum('hqk,khe->qhe', attn_probs, joined_heads[:, :, 2, :], precision=HIGHEST)))
        context = context.reshape(length, model_part)
        low_dense = low(low_back(matmul(context, dense_down)))
        partial_value = low(matmul(context, w_dense) + matmul(low_dense, dense_out))
        return (running + partial_value, None)
    attn_pieces = (joined_weight.reshape(D, N_TP, columns).transpose(1, 0, 2), joined_bias.reshape(N_TP, columns), joined_out.reshape(RANK, N_TP, columns).transpose(1, 0, 2), dense_weight.reshape(N_TP, model_part, D), dense_in.reshape(N_TP, model_part, RANK), slopes)
    attn_total, _ = lax.scan(jax.checkpoint(attention_group), jnp.zeros((length, D), jnp.float32), attn_pieces)
    middle = seq_rows + low_back(attn_total) + dense_bias
    normed_two = low(layer_norm(middle, second_gain, second_shift))

    def mlp_group(running, pieces):
        w_up, b_up, up_proj, w_down, down_proj = pieces
        copy_two = low_back(normed_two)
        low_up = low(low_back(matmul(copy_two, up_in)))
        pre_act = low_back(matmul(copy_two, w_up) + b_up + matmul(low_up, up_proj))
        activated = low(jax.nn.gelu(pre_act, approximate=False))
        low_down = low(low_back(matmul(activated, down_proj)))
        partial_value = low(matmul(activated, w_down) + matmul(low_down, down_out))
        return (running + partial_value, None)
    mlp_pieces = (up_weight.reshape(D, N_TP, hidden_part).transpose(1, 0, 2), up_bias.reshape(N_TP, hidden_part), up_out.reshape(RANK, N_TP, hidden_part).transpose(1, 0, 2), down_weight.reshape(N_TP, hidden_part, D), down_in.reshape(N_TP, hidden_part, RANK))
    mlp_total, _ = lax.scan(jax.checkpoint(mlp_group), jnp.zeros((length, D), jnp.float32), mlp_pieces)
    return middle + low_back(mlp_total) + down_bias

def reference(tokens, grad_out, adapter_ids, first_gain, first_shift, joined_weight, joined_bias, dense_weight, dense_bias, second_gain, second_shift, up_weight, up_bias, down_weight, down_bias, joined_adapt_in, joined_adapt_out, dense_adapt_in, dense_adapt_out, up_adapt_in, up_adapt_out, down_adapt_in, down_adapt_out):
    frozen = tuple((array_in.astype(jnp.float32) for array_in in (first_gain, first_shift, joined_weight, joined_bias, dense_weight, dense_bias, second_gain, second_shift, up_weight, up_bias, down_weight, down_bias)))
    adapters = tuple((array_in.astype(jnp.float32) for array_in in (joined_adapt_in, joined_adapt_out, dense_adapt_in, dense_adapt_out, up_adapt_in, up_adapt_out, down_adapt_in, down_adapt_out)))
    inputs = tokens.astype(jnp.float32).reshape(SEQS, LEN, D)

    def forward(inputs, adapters):

        def one_sequence(sequence_item):
            seq_rows, set_id = sequence_item
            onehot = (jnp.arange(ADAPTERS) == set_id).astype(jnp.float32)
            chosen = tuple((select_set(onehot, tensor_in) for tensor_in in adapters))
            return sequence_forward(seq_rows, chosen, frozen)
        return lax.map(jax.checkpoint(one_sequence), (inputs, adapter_ids))
    output, pullback = jax.vjp(forward, inputs, adapters)
    grad_inputs, grad_sets = pullback(grad_out.astype(jnp.float32).reshape(SEQS, LEN, D))
    return (output.reshape(SEQS * LEN, D).astype(jnp.bfloat16), grad_inputs.reshape(SEQS * LEN, D), grad_sets[0], grad_sets[1], grad_sets[2], grad_sets[3], grad_sets[4], grad_sets[5], grad_sets[6], grad_sets[7])
```

```python
import functools

import jax
import jax.numpy as jnp
import numpy as np
from jax import lax
from jax.experimental import pallas as pl
from jax.experimental.pallas import tpu as pltpu
from jax.sharding import Mesh
from jax.sharding import PartitionSpec as P

HEADS = 32
HEAD_DIM = 64
EPSILON = 1e-05
MASKED = -1e30
AXES = ("xl", "y", "c", "xh", "z")
FSDP = ("xl", "y", "c")
TP = ("xh", "z")
PLANE = ("xl", "y", "xh")
MESH_ID = pl.DeviceIdType.MESH
ANY = pl.ANY
VMEM = pltpu.VMEM
F32 = jnp.float32
BF16 = jnp.bfloat16


def remote(src, dst, sems, index, device):
    send, recv = sems
    return pltpu.make_async_remote_copy(
        src_ref=src, dst_ref=dst, send_sem=send.at[index], recv_sem=recv.at[index],
        device_id=device, device_id_type=MESH_ID)


def places():
    return tuple(lax.axis_index(a) for a in AXES)


def meet(peers):
    barrier = pltpu.get_barrier_semaphore()
    for p in peers:
        pl.semaphore_signal(barrier, inc=1, device_id=p, device_id_type=MESH_ID)
    pl.semaphore_wait(barrier, len(peers))


def ring_peers():
    _, _, c, _, z = places()
    return [{"z": lax.rem(z + 1, 4)}, {"z": lax.rem(z + 3, 4)}, {"c": 1 - c}]


def plane_peers():
    xl, y, c, xh, _ = places()
    peers = []
    for d in range(1, 4):
        for core in (0, 1):
            peers.append({"y": lax.rem(y + d, 4), "c": core})
            x = lax.rem(xh * 2 + xl + d, 4)
            peers.append({"xh": x // 2, "xl": lax.rem(x, 2), "c": core})
    return peers


class GroupGather:
    sub = 4

    def __init__(self, src, dst, local_sem, sems):
        self.src, self.dst, self.local_sem, self.sems = src, dst, local_sem, sems
        _, _, self.c, _, self.z = places()
        self.up, self.down, self.other = ring_peers()
        self.rows = src.shape[0]

    @staticmethod
    def semaphores():
        return [pltpu.SemaphoreType.DMA((1,)), pltpu.SemaphoreType.DMA((8, GroupGather.sub)),
                pltpu.SemaphoreType.DMA((8, GroupGather.sub))]

    def at(self, core, z, j=None):
        first = (core * 4 + z) * self.rows
        if j is None:
            return self.dst.at[pl.ds(pl.multiple_of(first, 128), self.rows)]
        step = self.rows // self.sub
        return self.dst.at[pl.ds(pl.multiple_of(first + j * step, step), step)]

    def start(self):
        c, z = self.c, self.z
        step = self.rows // self.sub
        self.own = pltpu.make_async_copy(self.src, self.at(c, z), self.local_sem.at[0])
        self.own.start()
        self.ups, self.downs = {}, {}
        for j in range(self.sub):
            k = self.sub - 1 - j
            self.ups[j] = remote(self.src.at[pl.ds(j * step, step)], self.at(c, z, j), self.sems, (0, j), self.up)
            self.ups[j].start()
            self.downs[k] = remote(self.src.at[pl.ds(k * step, step)], self.at(c, z, k), self.sems, (1, k), self.down)
            self.downs[k].start()
        self.shared = [remote(self.src, self.at(c, z), self.sems, (2, 0), self.other)]
        self.shared[0].start()
        self.forward = []

    def share(self, z, j, kind):
        block = self.at(self.c, z, j)
        copy = remote(block, block, self.sems, (kind, j), self.other)
        copy.start()
        self.shared.append(copy)

    def near(self, j):
        c, z = self.c, self.z
        above, below = lax.rem(z + 1, 4), lax.rem(z + 3, 4)
        half = self.sub // 2
        self.ups[j].wait_recv()
        if j < half:
            block = self.at(c, below, j)
            copy = remote(block, block, self.sems, (3, j), self.up)
            copy.start()
            self.forward.append((j, copy))
        k = self.sub - 1 - j
        self.downs[k].wait_recv()
        if k >= half:
            block = self.at(c, above, k)
            copy = remote(block, block, self.sems, (4, k), self.down)
            copy.start()
            self.forward.append((k, copy))
        self.share(below, j, 5)
        self.share(above, k, 6)

    def far(self):
        opposite = lax.rem(self.z + 2, 4)
        for j, copy in self.forward:
            copy.wait_recv()
            self.share(opposite, j, 7)

    def finish(self):
        self.own.wait()
        for copy in (*self.ups.values(), *self.downs.values()):
            copy.wait_send()
        for _, copy in self.forward:
            copy.wait_send()
        for copy in self.shared:
            copy.wait()


class PlaneGather:
    def __init__(self, src, dst, by_rows, local_sem, sems):
        self.src, self.dst, self.by_rows, self.local_sem, self.sems = src, dst, by_rows, local_sem, sems
        self.xl, self.y, self.c, self.xh, _ = places()
        self.x = self.xh * 2 + self.xl
        self.home = 1 - (self.xh - self.c) * (self.xh - self.c)

    @staticmethod
    def semaphores():
        return [pltpu.SemaphoreType.DMA((1,)), pltpu.SemaphoreType.DMA((22,)), pltpu.SemaphoreType.DMA((16,))]

    def slot(self, xl, y, core):
        k = (xl * 4 + y) * 2 + core
        if self.by_rows:
            return k, self.dst.at[pl.ds(pl.multiple_of(k * 128, 128), 128)]
        return k, self.dst.at[:, pl.ds(pl.multiple_of(k * 128, 128), 128)]

    def send(self, src, where, n, device):
        k, dst = where
        send, recv = self.sems
        return pltpu.make_async_remote_copy(
            src_ref=src, dst_ref=dst, send_sem=send.at[n], recv_sem=recv.at[k],
            device_id=device, device_id_type=MESH_ID)

    def arrived(self, where):
        self.send(where[1], where, 0, {"c": 1 - self.c}).wait_recv()

    def chip_x(self, d, core):
        x = lax.rem(self.x + d, 4)
        return {"xh": x // 2, "xl": lax.rem(x, 2), "c": core}

    def chip_y(self, d, core):
        return {"y": lax.rem(self.y + d, 4), "c": core}

    def first(self, act):
        own = self.slot(self.xl, self.y, self.c)

        @pl.when(self.c == 0)
        def _():
            for d in (1, 3, 2):
                act(self.send(self.src, own, d, self.chip_x(d, self.xh)))

        @pl.when(self.c == 1)
        def _():
            for d in (1, 3, 2):
                act(self.send(self.src, own, d, self.chip_y(d, self.xh)))

        @pl.when(self.home == 0)
        def _():
            act(self.send(self.src, own, 0, {"c": 1 - self.c}))

    def start(self):
        @pl.when(self.home == 1)
        def _():
            pltpu.make_async_copy(self.src, self.slot(self.xl, self.y, self.c)[1], self.local_sem.at[0]).start()

        self.first(lambda copy: copy.start())

        @pl.when(self.home == 1)
        def _():
            pltpu.make_async_copy(self.src, self.slot(self.xl, self.y, self.c)[1], self.local_sem.at[0]).wait()

    def columns(self):
        one = self.home * self.xl
        return one, 1 - one

    def rows_step(self, n, act):
        where = self.slot(self.columns()[n], self.y, 0)
        for d in (1, 3, 2):
            act(self.send(where[1], where, 4 + n * 3 + d - 1, self.chip_y(d, self.c)))

    def columns_step(self, n, act):
        where = self.slot(self.xl, lax.rem(self.y + n, 4), 1)

        @pl.when(self.home == 1)
        def _():
            for d in (1, 3, 2):
                act(self.send(where[1], where, 10 + n * 3 + d - 1, self.chip_x(d, self.c)))

    def step(self, n):
        if n < 2:
            where = self.slot(self.columns()[n], self.y, 0)
            if n == 0:
                @pl.when(self.home * (1 - self.c) == 0)
                def _():
                    self.arrived(where)
            else:
                self.arrived(where)
            self.rows_step(n, lambda copy: copy.start())
        else:
            where = self.slot(self.xl, lax.rem(self.y + n - 2, 4), 1)
            here = self.home * (1 - self.c) if n == 2 else self.home

            @pl.when(here == 1)
            def _():
                self.arrived(where)

            self.columns_step(n - 2, lambda copy: copy.start())

    def finish(self):
        for xl in (0, 1):
            for d in (1, 2, 3):
                self.arrived(self.slot(xl, lax.rem(self.y + d, 4), 0))
        one, two = self.columns()
        for y in range(4):
            self.arrived(self.slot(two, y, 1))

        @pl.when(self.home == 0)
        def _():
            for y in range(4):
                self.arrived(self.slot(one, y, 1))

        self.first(lambda copy: copy.wait_send())
        for n in (0, 1):
            self.rows_step(n, lambda copy: copy.wait_send())
        for n in range(4):
            self.columns_step(n, lambda copy: copy.wait_send())


class GroupSum:
    def __init__(self, parts, near, sent, half, full, sems):
        self.parts, self.near, self.sent, self.half, self.full, self.sems = parts, near, sent, half, full, sems
        _, _, self.c, _, self.z = places()
        self.up, self.down, self.other = ring_peers()
        self.order = [lax.rem(self.z + d, 4) for d in (2, 1, 3, 0)]

    @staticmethod
    def scratch(rows, width):
        return [VMEM((4, rows, width), BF16), VMEM((3, rows, width), BF16), VMEM((2, rows // 2, width), BF16),
                VMEM((2, rows, width), BF16), pltpu.SemaphoreType.DMA((10,)), pltpu.SemaphoreType.DMA((10,))]

    def part(self, core, i):
        return self.parts.at[core * 4 + self.order[i]]

    def give(self, i):
        remote(self.part(1 - self.c, i), self.near.at[i], self.sems, (i,), self.other).start()

    def pair(self, i, rows=slice(None)):
        return self.part(self.c, i)[rows].astype(F32) + self.near[i, rows].astype(F32)

    def got(self, i):
        remote(self.near.at[i], self.near.at[i], self.sems, (i,), self.other).wait_recv()

    def piece(self, name):
        h = self.half.shape[1]
        low, high = pl.ds(0, h), pl.ds(h, h)
        n = ("far_up", "far_down", "up_high", "down_low", "up_low", "down_high").index(name)
        src = (self.sent.at[0, low], self.sent.at[0, high], self.sent.at[1, high], self.sent.at[2, low],
               self.sent.at[1, low], self.sent.at[2, high])[n]
        dst = (self.half.at[0], self.half.at[1], self.full.at[0, high], self.full.at[1, low],
               self.full.at[0, low], self.full.at[1, high])[n]
        return remote(src, dst, self.sems, (4 + n,), (self.up, self.down)[n % 2])

    def far(self):
        self.got(0)
        self.sent[0] = self.pair(0).astype(BF16)
        self.piece("far_up").start()
        self.piece("far_down").start()

    def near_first(self):
        h = self.half.shape[1]
        self.got(1)
        self.sent[1, pl.ds(h, h)] = self.pair(1, pl.ds(h, h)).astype(BF16)
        self.piece("up_high").start()
        self.got(2)
        self.sent[2, pl.ds(0, h)] = self.pair(2, pl.ds(0, h)).astype(BF16)
        self.piece("down_low").start()

    def near_second(self):
        h = self.half.shape[1]
        self.piece("far_up").wait_recv()
        self.sent[1, pl.ds(0, h)] = (self.pair(1, pl.ds(0, h)) + self.half[0].astype(F32)).astype(BF16)
        self.piece("up_low").start()
        self.piece("far_down").wait_recv()
        self.sent[2, pl.ds(h, h)] = (self.pair(2, pl.ds(h, h)) + self.half[1].astype(F32)).astype(BF16)
        self.piece("down_high").start()

    def total(self):
        self.got(3)
        for name in ("up_high", "down_low", "up_low", "down_high"):
            self.piece(name).wait_recv()
        return self.pair(3) + self.full[0].astype(F32) + self.full[1].astype(F32)

    def finish(self):
        for name in ("far_up", "far_down", "up_high", "down_low", "up_low", "down_high"):
            self.piece(name).wait_send()
        for i in range(4):
            remote(self.part(1 - self.c, i), self.near.at[i], self.sems, (i,), self.other).wait_send()


def params(cid, mib):
    return pltpu.CompilerParams(collective_id=cid, has_side_effects=True, vmem_limit_bytes=mib << 20)


def gather_kernel(count, by_rows, with_group, *refs):
    refs = list(refs)
    take = lambda n: [refs.pop(0) for _ in range(n)]
    x_ref = take(1)[0] if with_group else None
    shards = take(count)
    o_ref = take(1)[0] if with_group else None
    wholes = take(count)
    peers = plane_peers() + ring_peers()
    meet(peers)
    if with_group:
        local, send, recv = take(3)
        group = GroupGather(x_ref, o_ref, local, (send, recv))
        group.start()
    planes = []
    for i in range(count):
        local, send, recv = take(3)
        planes.append(PlaneGather(shards[i], wholes[i], by_rows[i], local, (send, recv)))
        planes[-1].start()
    if with_group:
        for j in range(2):
            group.near(j)
    for w in planes:
        for n in range(6):
            w.step(n)
    if with_group:
        for j in range(2, group.sub):
            group.near(j)
        group.far()
        group.finish()
    for w in planes:
        w.finish()


def gathers(cid, shards, by_rows, x=None):
    group = x is not None
    count = len(shards)
    outs = []
    if group:
        outs.append(jax.ShapeDtypeStruct((x.shape[0] * 8, x.shape[1]), x.dtype))
    for w, rows in zip(shards, by_rows):
        shape = (2048, w.shape[1]) if rows else (w.shape[0], 2048)
        outs.append(jax.ShapeDtypeStruct(shape, w.dtype))
    g = [pl.BlockSpec(memory_space=VMEM)] if group else []
    anys = [pl.BlockSpec(memory_space=ANY)] * count
    return pl.pallas_call(
        functools.partial(gather_kernel, count, tuple(by_rows), group), out_shape=outs,
        in_specs=g + anys, out_specs=g + anys,
        scratch_shapes=(GroupGather.semaphores() if group else []) + PlaneGather.semaphores() * count,
        compiler_params=params(cid, 16), name=f"gathers_{cid}")(*([x] if group else []), *shards)


def sum_kernel(p_ref, o_ref, near, sent, half, full, send, recv):
    meet(ring_peers())
    s = GroupSum(p_ref, near, sent, half, full, (send, recv))
    for i in range(4):
        s.give(i)
    s.far()
    s.near_first()
    s.near_second()
    o_ref[...] = s.total()
    s.finish()


def group_sum(parts, cid):
    rows, width = parts.shape[0] // 8, parts.shape[1]
    return pl.pallas_call(
        sum_kernel, out_shape=jax.ShapeDtypeStruct((rows, width), F32),
        in_specs=[pl.BlockSpec(memory_space=VMEM)], out_specs=pl.BlockSpec(memory_space=VMEM),
        scratch_shapes=GroupSum.scratch(rows, width), compiler_params=params(cid, 24),
        name=f"group_sum_{cid}")(parts.reshape(8, rows, width))


def ag_kernel(x_ref, o_ref, local_sem, send, recv):
    meet(ring_peers())
    g = GroupGather(x_ref, o_ref, local_sem, (send, recv))
    g.start()
    for j in range(g.sub):
        g.near(j)
    g.far()
    g.finish()


def group_gather(x, cid):
    return pl.pallas_call(
        ag_kernel, out_shape=jax.ShapeDtypeStruct((x.shape[0] * 8, x.shape[1]), x.dtype),
        in_specs=[pl.BlockSpec(memory_space=VMEM)], out_specs=pl.BlockSpec(memory_space=VMEM),
        scratch_shapes=GroupGather.semaphores(), compiler_params=params(cid, 16), name=f"group_gather_{cid}")(x)


SWAP = ((0, 0), (1, 2), (2, 1), (3, 3))


def swap(a):
    return lax.ppermute(a, ("c", "xh"), SWAP)


def layer_norm(rows_in, gain, shift):
    row_mean = jnp.mean(rows_in, axis=-1, keepdims=True)
    centered = rows_in - row_mean
    variance = jnp.mean(centered * centered, axis=-1, keepdims=True)
    return centered * lax.rsqrt(variance + EPSILON) * gain + shift


def norm_back(rows_in, gain, grad):
    row_mean = jnp.mean(rows_in, axis=-1, keepdims=True)
    centered = rows_in - row_mean
    inverse = lax.rsqrt(jnp.mean(centered * centered, axis=-1, keepdims=True) + EPSILON)
    n = centered * inverse
    e = gain * grad
    return (e - jnp.mean(e, axis=-1, keepdims=True) - n * jnp.mean(e * n, axis=-1, keepdims=True)) * inverse


def dot(a, b, dims=((1,), (0,))):
    return lax.dot_general(a, b, (dims, ((), ())), preferred_element_type=F32)


def dot_t(a, b):
    return dot(a, b, ((1,), (1,)))


def dot_o(a, b):
    return dot(a, b, ((0,), (0,)))


def exact_gelu(v):
    return jax.nn.gelu(v, approximate=False)


def scores_of(q, k, slope):
    n = q.shape[0]
    distance = (jnp.arange(n)[:, None] - jnp.arange(n)[None, :]).astype(F32)
    s = (dot_t(q, k) - slope * distance) * 0.125
    return jnp.where(distance >= 0, s, MASKED)


def attend(heads, slopes):
    outs, logs = [], []
    for h in range(4):
        q, k, v = (heads[:, h, i] for i in range(3))
        s = scores_of(q, k, slopes[h])
        top = jnp.max(s, axis=-1, keepdims=True)
        e = jnp.exp(s - top)
        total = jnp.sum(e, axis=-1, keepdims=True)
        outs.append(dot((e / total).astype(BF16), v).astype(BF16))
        logs.append(top + jnp.log(total))
    return jnp.concatenate(outs, axis=1), logs


def attend_back(heads, logs, grad, slopes):
    outs = []
    for h in range(4):
        q, k, v = (heads[:, h, i] for i in range(3))
        g = grad[:, h * 64:(h + 1) * 64]
        p = jnp.exp(scores_of(q, k, slopes[h]) - logs[h])
        dp = dot_t(g, v)
        ds = (p * (dp - jnp.sum(p * dp, axis=-1, keepdims=True))).astype(BF16)
        outs.append(jnp.stack((dot(ds, k) * 0.125, dot_o(ds, q) * 0.125, dot_o(p.astype(BF16), g)), axis=1))
    return jnp.stack(outs, axis=1).astype(BF16).reshape(grad.shape[0], 768)


def local(tokens, grad_out, adapter_ids, first_gain, first_shift, joined_weight, joined_bias, dense_weight,
          dense_bias, second_gain, second_shift, up_weight, up_bias, down_weight, down_bias, joined_adapt_in,
          joined_adapt_out, dense_adapt_in, dense_adapt_out, up_adapt_in, up_adapt_out, down_adapt_in,
          down_adapt_out):
    c, xh, z = lax.axis_index("c"), lax.axis_index("xh"), lax.axis_index("z")
    group = c * 4 + z
    own_id = adapter_ids[0]
    picked = [lax.dynamic_index_in_dim(a, own_id, 0, keepdims=False) for a in
              (joined_adapt_out, dense_adapt_in, up_adapt_out, down_adapt_in)]
    flat = swap(jnp.concatenate([a.ravel() for a in picked]))
    biases = swap(jnp.concatenate([joined_bias, up_bias]))
    set_id = swap(adapter_ids)
    pick_joined_out = flat[:12288].reshape(16, 768)
    pick_dense_in = flat[12288:16384].reshape(256, 16)
    pick_up_out = flat[16384:32768].reshape(16, 1024)
    pick_down_in = flat[32768:].reshape(1024, 16)
    b_joined, b_up = biases[:768], biases[768:]
    pick_joined_in, pick_dense_out, pick_up_in, pick_down_out = [
        lax.dynamic_index_in_dim(a, set_id[0], 0, keepdims=False) for a in
        (joined_adapt_in, dense_adapt_out, up_adapt_in, down_adapt_out)]
    slopes = jnp.exp2(-8.0 * (group * 4 + jnp.arange(4) + 1).astype(F32) / HEADS)
    tokens = swap(tokens)
    grad_out = swap(grad_out)
    residual_in = tokens.astype(F32)
    x1 = layer_norm(residual_in, first_gain, first_shift).astype(BF16)
    x1_all, w_joined = gathers(1, [joined_weight], [True], x1)
    low_joined = dot(x1_all, pick_joined_in).astype(BF16)
    joined = (dot(x1_all, w_joined) + dot(low_joined, pick_joined_out) + b_joined).astype(BF16)
    go_all, w_dense, w_up = gathers(2, [dense_weight, up_weight], [False, True], grad_out)
    heads = joined.reshape(1024, 4, 3, 64)
    context, logs = attend(heads, slopes)
    low_dense = dot(context, pick_dense_in).astype(BF16)
    attn = (dot(context, w_dense) + dot(low_dense, pick_dense_out)).astype(BF16)
    mid = residual_in + group_sum(attn, 3) + dense_bias
    x2 = layer_norm(mid, second_gain, second_shift).astype(BF16)
    x2_all, w_down = gathers(4, [down_weight], [False], x2)
    low_up = dot(x2_all, pick_up_in).astype(BF16)
    pre = dot(x2_all, w_up) + dot(low_up, pick_up_out) + b_up
    act = exact_gelu(pre).astype(BF16)
    low_down = dot(act, pick_down_in).astype(BF16)
    mlp = (dot(act, w_down) + dot(low_down, pick_down_out)).astype(BF16)
    layer_out = swap((mid + group_sum(mlp, 5) + down_bias).astype(BF16))
    grad_low_down = dot_t(go_all, pick_down_out).astype(BF16)
    grad_act = dot_t(go_all, w_down) + dot_t(grad_low_down, pick_down_in)
    grad_pre = jax.vjp(exact_gelu, pre)[1](grad_act)[0].astype(BF16)
    grad_low_up = dot_t(grad_pre, pick_up_out).astype(BF16)
    part_two = (dot_t(grad_pre, w_up) + dot_t(grad_low_up, pick_up_in)).astype(BF16)
    grad_mid = grad_out.astype(F32) + norm_back(mid, second_gain, group_sum(part_two, 6))
    ga_all = group_gather(grad_mid.astype(BF16), 7)
    grad_low_dense = dot_t(ga_all, pick_dense_out).astype(BF16)
    grad_context = (dot_t(ga_all, w_dense) + dot_t(grad_low_dense, pick_dense_in)).astype(BF16)
    grad_joined = attend_back(heads, logs, grad_context, slopes)
    grad_low_joined = dot_t(grad_joined, pick_joined_out).astype(BF16)
    part_one = (dot_t(grad_joined, w_joined) + dot_t(grad_low_joined, pick_joined_in)).astype(BF16)
    grad_tokens = swap(grad_mid + norm_back(residual_in, first_gain, group_sum(part_one, 8)))

    lows = jnp.concatenate([grad_low_joined, low_dense, grad_low_up, low_down], axis=1)
    lows = lax.psum(lows.astype(F32), ("c", "z")).astype(BF16)
    cols = [lax.dynamic_slice_in_dim(a, group * 256, 256, 1) for a in (x1_all, ga_all, x2_all, go_all)]
    halves = jnp.concatenate([dot_o(lows[:, i * 16:(i + 1) * 16], cols[i]) for i in range(4)], axis=1)
    wide = jnp.concatenate([dot_o(low_joined, grad_joined), dot_o(grad_low_dense, context), dot_o(low_up, grad_pre),
                            dot_o(grad_low_down, act)], axis=1)
    mine = jnp.concatenate([wide, halves], axis=1).astype(BF16)
    every = lax.all_gather(mine, PLANE, axis=0, tiled=False)
    ids = lax.all_gather(set_id, PLANE, axis=0, tiled=True)
    onehot = (jnp.arange(8)[:, None] == ids[None, :]).astype(BF16)
    sums = lax.dot_general(onehot, every, (((1,), (0,)), ((), ())), preferred_element_type=F32)
    split = swap(sums[:, :, :3072].astype(BF16)).astype(F32)
    whole = lax.all_gather(sums[:, :, 3072:].astype(BF16), ("c", "z"), axis=0, tiled=False).astype(F32)
    whole = whole.reshape(8, 8, 16, 4, 256)
    per = [whole[:, :, :, i].transpose(1, 2, 0, 3).reshape(8, 16, 2048) for i in range(4)]
    turn = lambda a: jnp.swapaxes(a, 1, 2)
    return (layer_out, grad_tokens, turn(per[0]), split[:, :, :768], turn(split[:, :, 768:1024]), per[1],
            turn(per[2]), split[:, :, 1024:2048], turn(split[:, :, 2048:3072]), per[3])


def solution(mesh):
    fine = Mesh(mesh.devices.reshape(2, 4, 2, 2, 4), AXES)
    rows, cols = P(FSDP, TP), P(TP, FSDP)
    tok = P((*FSDP, *TP), None)
    last, middle, one = P(None, None, TP), P(None, TP, None), P(TP)
    return jax.shard_map(
        local, mesh=fine,
        in_specs=(tok, tok, P(FSDP), P(), P(), rows, one, cols, P(), P(), P(), rows, one, cols, P(), P(), last,
                  middle, P(), P(), last, middle, P()),
        out_specs=(tok, tok, P(), last, middle, P(), P(), last, middle, P()), check_vma=False)
```

```python
import functools

import jax
import jax.numpy as jnp
from jax import lax
from jax.experimental import pallas as pl
from jax.experimental.pallas import tpu as pltpu
from jax.sharding import Mesh
from jax.sharding import PartitionSpec as P

HEADS = 32
EPSILON = 1e-05
MASKED = -1e30
AXES = ("xl", "y", "c", "xh", "z")
FSDP = ("xl", "y", "c")
TP = ("xh", "z")
PLANE = ("xl", "y", "xh")
MESH_ID = pl.DeviceIdType.MESH
ANY = pl.ANY
VMEM = pltpu.VMEM
DMA = pltpu.SemaphoreType.DMA
F32 = jnp.float32
BF16 = jnp.bfloat16
ORDER = (0, 3, 1, 2)
PICKS = dict(joined_in=(0, 2048), joined_out=(2048, 768), hot=(2816, 128), up_in=(2944, 2048), up_out=(4992, 1024),
             dense_in=(6016, 256), dense_out=(6272, 2048), down_in=(8320, 1024), down_out=(9344, 2048))
PICKED = 11392


def remote(src, dst, sems, index, device):
    send, recv = sems
    return pltpu.make_async_remote_copy(
        src_ref=src, dst_ref=dst, send_sem=send.at[index], recv_sem=recv.at[index],
        device_id=device, device_id_type=MESH_ID)


def places():
    return tuple(lax.axis_index(a) for a in AXES)


def at_home():
    _, _, c, xh, _ = places()
    return 1 - (xh - c) * (xh - c)


def meet(peers):
    barrier = pltpu.get_barrier_semaphore()
    for p in peers:
        pl.semaphore_signal(barrier, inc=1, device_id=p, device_id_type=MESH_ID)
    pl.semaphore_wait(barrier, len(peers))


def group_peer(n):
    _, _, c, _, z = places()
    return {"c": lax.rem(c + n // 4, 2), "z": lax.rem(z + n % 4, 4)}


def group_peers():
    return [group_peer(n) for n in range(1, 8)]


def diagonal():
    _, _, c, xh, _ = places()
    return {"c": 1 - c, "xh": 1 - xh}


def plane_peers():
    xl, y, c, xh, _ = places()
    peers = []
    for d in range(1, 4):
        for core in (0, 1):
            peers.append({"y": lax.rem(y + d, 4), "c": core})
            x = lax.rem(xh * 2 + xl + d, 4)
            peers.append({"xh": x // 2, "xl": lax.rem(x, 2), "c": core})
    return peers


def block(ref, n, size=128):
    return ref.at[pl.ds(pl.multiple_of(n * size, size), size)]


class GroupGather:
    SEMS = [DMA((8, 4)), DMA((8, 4))]

    def __init__(self, dst, send, recv):
        self.dst, self.sems = dst, (send, recv)
        _, _, self.c, _, self.z = places()
        self.up, self.down, self.other = group_peer(1), group_peer(3), group_peer(4)

    def at(self, core, z, j):
        return self.dst.at[pl.ds(pl.multiple_of((core * 4 + z) * 128 + j * 32, 32), 32)]

    def copy(self, z, j, kind, device):
        ref = self.at(self.c, z, j)
        return remote(ref, ref, self.sems, (kind, j), device)

    def put(self, j):
        self.copy(self.z, j, 0, self.up).start()
        self.copy(self.z, j, 1, self.down).start()
        self.copy(self.z, j, 2, self.other).start()

    def near(self, j):
        below, above = lax.rem(self.z + 3, 4), lax.rem(self.z + 1, 4)
        self.copy(below, j, 0, self.up).wait_recv()
        if j < 2:
            self.copy(below, j, 3, self.up).start()
        self.copy(below, j, 5, self.other).start()
        self.copy(above, j, 1, self.down).wait_recv()
        if j >= 2:
            self.copy(above, j, 4, self.down).start()
        self.copy(above, j, 6, self.other).start()

    def far(self, j):
        opposite = lax.rem(self.z + 2, 4)
        self.copy(opposite, j, 3 if j < 2 else 4, self.up).wait_recv()
        self.copy(opposite, j, 7, self.other).start()

    def shared(self, kind):
        for j in ORDER:
            self.copy(self.z, j, kind, self.other).wait_recv()

    def finish(self):
        for j in ORDER:
            for kind in (0, 1, 2, 3 if j < 2 else 4, 5, 6, 7):
                self.copy(self.z, j, kind, self.other).wait_send()


class LowGather:
    SEMS = [DMA((8,)), DMA((8,))]

    def __init__(self, dst, send, recv):
        self.dst, self.sems = dst, (send, recv)
        _, _, c, _, z = places()
        self.own = pl.ds(pl.multiple_of((c * 4 + z) * 128, 128), 128)

    def copies(self):
        ref = self.dst.at[:, self.own]
        return [remote(ref, ref, self.sems, (n,), group_peer(n)) for n in range(1, 8)]

    def start(self, value):
        self.dst[:, self.own] = value
        for copy in self.copies():
            copy.start()

    def wait(self):
        for copy in self.copies():
            copy.wait()


class LowSum:
    SEMS = [DMA((8,)), DMA((8,))]

    def __init__(self, src, got, send, recv):
        self.src, self.got, self.sems = src, got, (send, recv)
        _, _, self.c, _, self.z = places()

    def copies(self):
        out = []
        for n in range(1, 8):
            p = group_peer(n)
            cols = pl.ds(pl.multiple_of((p["c"] * 4 + p["z"]) * 128, 128), 128)
            out.append(remote(self.src.at[:, cols], self.got.at[n], self.sems, (n,), p))
        return out

    def start(self):
        for copy in self.copies():
            copy.start()

    def total(self):
        for copy in self.copies():
            copy.wait()
        own = pl.ds(pl.multiple_of((self.c * 4 + self.z) * 128, 128), 128)
        out = self.src[:, own].astype(F32)
        for n in range(1, 8):
            out = out + self.got[n].astype(F32)
        return out.astype(BF16)


class PlaneGather:
    SEMS = [DMA((1,)), DMA((22,)), DMA((16,))]

    def __init__(self, src, dst, by_rows, local_sem, send, recv):
        self.src, self.dst, self.by_rows, self.local_sem, self.sems = src, dst, by_rows, local_sem, (send, recv)
        self.xl, self.y, self.c, self.xh, _ = places()
        self.x = self.xh * 2 + self.xl
        self.home = at_home()

    def slot(self, xl, y, core):
        k = (xl * 4 + y) * 2 + core
        if self.by_rows:
            return k, block(self.dst, k)
        return k, self.dst.at[:, pl.ds(pl.multiple_of(k * 128, 128), 128)]

    def send(self, src, where, n, device):
        k, dst = where
        send, recv = self.sems
        return pltpu.make_async_remote_copy(
            src_ref=src, dst_ref=dst, send_sem=send.at[n], recv_sem=recv.at[k],
            device_id=device, device_id_type=MESH_ID)

    def arrived(self, where):
        self.send(where[1], where, 0, {"c": 1 - self.c}).wait_recv()

    def chip_x(self, d, core):
        x = lax.rem(self.x + d, 4)
        return {"xh": x // 2, "xl": lax.rem(x, 2), "c": core}

    def chip_y(self, d, core):
        return {"y": lax.rem(self.y + d, 4), "c": core}

    def first(self, act):
        own = self.slot(self.xl, self.y, self.c)

        @pl.when(self.c == 0)
        def _():
            for d in (1, 3, 2):
                act(self.send(self.src, own, d, self.chip_x(d, self.xh)))

        @pl.when(self.c == 1)
        def _():
            for d in (1, 3, 2):
                act(self.send(self.src, own, d, self.chip_y(d, self.xh)))

        @pl.when(self.home == 0)
        def _():
            act(self.send(self.src, own, 0, {"c": 1 - self.c}))

    def start(self):
        @pl.when(self.home == 1)
        def _():
            pltpu.make_async_copy(self.src, self.slot(self.xl, self.y, self.c)[1], self.local_sem.at[0]).start()

        self.first(lambda copy: copy.start())

    def columns(self):
        one = self.home * self.xl
        return one, 1 - one

    def rows_step(self, n, act):
        where = self.slot(self.columns()[n], self.y, 0)
        for d in (1, 3, 2):
            act(self.send(where[1], where, 4 + n * 3 + d - 1, self.chip_y(d, self.c)))

    def columns_step(self, n, act):
        where = self.slot(self.xl, lax.rem(self.y + n, 4), 1)

        @pl.when(self.home == 1)
        def _():
            for d in (1, 3, 2):
                act(self.send(where[1], where, 10 + n * 3 + d - 1, self.chip_x(d, self.c)))

    def step(self, n):
        if n == 0:
            @pl.when(self.home == 1)
            def _():
                pltpu.make_async_copy(self.src, self.slot(self.xl, self.y, self.c)[1], self.local_sem.at[0]).wait()
        if n < 2:
            where = self.slot(self.columns()[n], self.y, 0)
            if n == 0:
                @pl.when(self.home * (1 - self.c) == 0)
                def _():
                    self.arrived(where)
            else:
                self.arrived(where)
            self.rows_step(n, lambda copy: copy.start())
        else:
            where = self.slot(self.xl, lax.rem(self.y + n - 2, 4), 1)
            here = self.home * (1 - self.c) if n == 2 else self.home

            @pl.when(here == 1)
            def _():
                self.arrived(where)

            self.columns_step(n - 2, lambda copy: copy.start())

    def wait(self):
        for xl in (0, 1):
            for d in (1, 2, 3):
                self.arrived(self.slot(xl, lax.rem(self.y + d, 4), 0))
        one, two = self.columns()
        for y in range(4):
            self.arrived(self.slot(two, y, 1))

        @pl.when(self.home == 0)
        def _():
            for y in range(4):
                self.arrived(self.slot(one, y, 1))

    def finish(self):
        self.first(lambda copy: copy.wait_send())
        for n in (0, 1):
            self.rows_step(n, lambda copy: copy.wait_send())
        for n in range(4):
            self.columns_step(n, lambda copy: copy.wait_send())


class GroupSum:
    NAMES = ("far_up", "far_down", "up_high", "down_low", "up_low", "down_high")
    SCRATCH = [VMEM((1024, 2048), BF16), VMEM((4, 128, 2048), BF16), VMEM((3, 128, 2048), BF16),
               VMEM((2, 64, 2048), BF16), VMEM((2, 128, 2048), BF16), DMA((10,)), DMA((10,))]

    def __init__(self, parts, near, sent, half, full, send, recv):
        self.parts, self.near, self.sent, self.half, self.full, self.sems = parts, near, sent, half, full, (send, recv)
        _, _, self.c, _, self.z = places()
        self.up, self.down, self.other = group_peer(1), group_peer(3), group_peer(4)
        self.order = [lax.rem(self.z + d, 4) for d in (2, 1, 3, 0)]

    def part(self, core, i):
        return block(self.parts, core * 4 + self.order[i])

    def given(self, i):
        return remote(self.part(1 - self.c, i), self.near.at[i], self.sems, (i,), self.other)

    def give(self, i):
        self.given(i).start()

    def pair(self, i, rows=slice(None)):
        return self.part(self.c, i)[rows].astype(F32) + self.near[i, rows].astype(F32)

    def piece(self, name):
        low, high = pl.ds(0, 64), pl.ds(64, 64)
        n = self.NAMES.index(name)
        src = (self.sent.at[0, low], self.sent.at[0, high], self.sent.at[1, high], self.sent.at[2, low],
               self.sent.at[1, low], self.sent.at[2, high])[n]
        dst = (self.half.at[0], self.half.at[1], self.full.at[0, high], self.full.at[1, low],
               self.full.at[0, low], self.full.at[1, high])[n]
        return remote(src, dst, self.sems, (4 + n,), (self.up, self.down)[n % 2])

    def far(self):
        self.given(0).wait_recv()
        self.sent[0] = self.pair(0).astype(BF16)
        self.piece("far_up").start()
        self.piece("far_down").start()

    def near_up(self):
        self.given(1).wait_recv()
        self.sent[1, pl.ds(64, 64)] = self.pair(1, pl.ds(64, 64)).astype(BF16)
        self.piece("up_high").start()

    def near_down(self):
        self.given(2).wait_recv()
        self.sent[2, pl.ds(0, 64)] = self.pair(2, pl.ds(0, 64)).astype(BF16)
        self.piece("down_low").start()

    def pass_on(self):
        low, high = pl.ds(0, 64), pl.ds(64, 64)
        self.piece("far_up").wait_recv()
        self.sent[1, low] = (self.pair(1, low) + self.half[0].astype(F32)).astype(BF16)
        self.piece("up_low").start()
        self.piece("far_down").wait_recv()
        self.sent[2, high] = (self.pair(2, high) + self.half[1].astype(F32)).astype(BF16)
        self.piece("down_high").start()

    def arrive(self):
        self.given(3).wait_recv()
        for name in ("up_high", "down_low", "up_low", "down_high"):
            self.piece(name).wait_recv()

    def total(self, rows=slice(None)):
        return self.pair(3, rows) + self.full[0, rows].astype(F32) + self.full[1, rows].astype(F32)

    def finish(self):
        for name in self.NAMES:
            self.piece(name).wait_send()
        for i in range(4):
            self.given(i).wait_send()


def params(cid, mib):
    return pltpu.CompilerParams(collective_id=cid, has_side_effects=True, vmem_limit_bytes=mib << 20)


def plain(mib):
    return pltpu.CompilerParams(vmem_limit_bytes=mib << 20)


def shape(*dims, dtype=BF16):
    return jax.ShapeDtypeStruct(dims, dtype)


def specs(*spaces):
    return [pl.BlockSpec(memory_space=s) for s in spaces]


def layer_norm(rows_in, gain, shift):
    row_mean = jnp.mean(rows_in, axis=-1, keepdims=True)
    centered = rows_in - row_mean
    variance = jnp.mean(centered * centered, axis=-1, keepdims=True)
    return centered * lax.rsqrt(variance + EPSILON) * gain + shift


def norm_back(rows_in, gain, grad):
    row_mean = jnp.mean(rows_in, axis=-1, keepdims=True)
    centered = rows_in - row_mean
    inverse = lax.rsqrt(jnp.mean(centered * centered, axis=-1, keepdims=True) + EPSILON)
    n = centered * inverse
    e = gain * grad
    return (e - jnp.mean(e, axis=-1, keepdims=True) - n * jnp.mean(e * n, axis=-1, keepdims=True)) * inverse


def dot(a, b, dims=((1,), (0,))):
    return lax.dot_general(a, b, (dims, ((), ())), preferred_element_type=F32)


def dot_t(a, b):
    return dot(a, b, ((1,), (1,)))


def dot_o(a, b):
    return dot(a, b, ((0,), (0,)))


def tiles(count, size, body):
    def run(i, carry):
        body(pl.ds(pl.multiple_of(i * size, size), size))
        return carry

    lax.fori_loop(0, count, run, 0)


def split_refs(refs, *counts):
    refs, out = list(refs), []
    for n in counts:
        out.append(refs[:n])
        refs = refs[n:]
    return (*out, refs)


def pick(ref, name):
    first, n = PICKS[name]
    return ref[:, pl.ds(first, n)]


def row_pair(z):
    return (pl.ds(pl.multiple_of(z * 128, 128), 128), pl.ds(pl.multiple_of(512 + z * 128, 128), 128))


def take_pair(ref, z, cols=slice(None)):
    a, b = row_pair(z)
    return jnp.concatenate([ref[a, cols], ref[b, cols]], axis=0)


def put_pair(ref, z, value, cols=slice(None)):
    a, b = row_pair(z)
    ref[a, cols] = value[:128]
    ref[b, cols] = value[128:]


class Swap:
    def __init__(self, pairs, local, send, recv):
        self.pairs, self.local, self.sems, self.home = pairs, local, (send, recv), at_home()

    def near_copy(self, n):
        src, _, dst = self.pairs[n]
        return pltpu.make_async_copy(src, dst, self.local.at[n])

    def far_copy(self, n):
        src, dst, _ = self.pairs[n]
        return remote(src, dst, self.sems, (n,), diagonal())

    def start(self, n):
        @pl.when(self.home == 1)
        def _():
            self.near_copy(n).start()

        @pl.when(self.home == 0)
        def _():
            self.far_copy(n).start()

    def wait(self, n):
        @pl.when(self.home == 1)
        def _():
            self.near_copy(n).wait()

        @pl.when(self.home == 0)
        def _():
            self.far_copy(n).wait_recv()

    def finish(self):
        @pl.when(self.home == 0)
        def _():
            for n in range(len(self.pairs)):
                self.far_copy(n).wait_send()

    @staticmethod
    def sems(n):
        return [DMA((n,)), DMA((n,)), DMA((n,))]


ADAPTERS = ("joined_in", "joined_out", "dense_in", "dense_out", "up_in", "up_out", "down_in", "down_out")


def joined_kernel(*refs):
    (ids, tokens, gain, shift), adapters, (bj, bu, wj), outs, scratch = split_refs(refs, 4, 8, 3, 9)
    xs, x_all, pk, bias, qa, ka, va, wj_all, low = outs
    (mine, xbuf, wbuf, out_sem), sw_sems, g_sems, low_sems, p_sems = split_refs(scratch, 4, 3, 2, 2)
    _, _, c, _, z = places()
    own = c * 4 + z
    meet(plane_peers() + group_peers())
    sub = lambda ref, j: ref.at[pl.ds(j * 32, 32)]
    cut = 2944
    pairs = [(sub(tokens, j), sub(xs, j)) for j in range(4)]
    pairs += [(mine.at[:, :cut], pk.at[:, :cut]), (mine.at[:, cut:], pk.at[:, cut:]),
              (bj, bias.at[:, :768]), (bu, bias.at[:, 768:])]
    sw = Swap([(a, b, b) for a, b in pairs], *sw_sems)
    for j in ORDER:
        sw.start(j)
    plane = PlaneGather(wj, wbuf, True, *p_sems)
    plane.start()
    set_id = ids[0]
    for name, ref in zip(ADAPTERS, adapters):
        first, n = PICKS[name]
        mine[:, first:first + n] = ref[set_id]
    first, n = PICKS["hot"]
    mine[:, first:first + n] = jnp.where(lax.broadcasted_iota(jnp.int32, (16, 128), 0) == set_id, 1.0, 0.0).astype(BF16)
    for n in range(4, 8):
        sw.start(n)
    g = GroupGather(xbuf, *g_sems)
    lows = LowGather(low, *low_sems)
    for j in ORDER:
        sw.wait(j)
        x1 = layer_norm(xs[j * 32:(j + 1) * 32].astype(F32), gain[...], shift[...])
        xbuf[pl.ds(pl.multiple_of(own * 128 + j * 32, 32), 32)] = x1.astype(BF16)
        g.put(j)
    sw.wait(4)
    lows.start(dot_t(pick(pk, "joined_in"), block(xbuf, own)[...]).astype(BF16))
    g.near(0)
    plane.step(0)
    plane.step(1)
    g.near(3)
    for n in (2, 3):
        plane.step(n)
    g.near(1)
    for n in (4, 5):
        plane.step(n)
    g.near(2)
    for j in ORDER:
        g.far(j)
    for n in range(5, 8):
        sw.wait(n)
    for kind in (2, 5, 6, 7):
        g.shared(kind)
    x_out = pltpu.make_async_copy(xbuf, x_all, out_sem.at[0])
    x_out.start()
    plane.wait()
    w_out = pltpu.make_async_copy(wbuf, wj_all, out_sem.at[1])
    w_out.start()
    lows.wait()
    lane = lax.broadcasted_iota(jnp.int32, (256, 128), 1)
    row = lax.broadcasted_iota(jnp.int32, (256, 128), 0)

    def project(i, carry):
        rows = pl.ds(pl.multiple_of(i * 256, 256), 256)
        acc = dot(xbuf[rows], wbuf[...]) + dot_o(low[:, rows], pick(pk, "joined_out")) + bias[:, :768]
        b = acc.astype(BF16).astype(F32)
        position = (i * 256 + row).astype(F32) * 0.125
        ones = jnp.where(lane < 67, 1.0, 0.0)
        for h in range(4):
            slope = jnp.exp2((own * 4 + h + 1).astype(F32) * (-8.0 / HEADS) + jnp.zeros((1, 128), F32))
            line = position * slope
            high = line.astype(BF16).astype(F32)
            middle = (line - high).astype(BF16).astype(F32)
            lowest = line - high - middle
            tail = jnp.where(lane == 64, high, jnp.where(lane == 65, middle, jnp.where(lane == 66, lowest, jnp.where(
                lane < 70, 1.0, 0.0))))
            at = h * 192
            qa[h, rows] = jnp.where(lane < 64, b[:, at:at + 128] * 0.125, ones).astype(BF16)
            ka[h, rows] = jnp.where(lane < 64, b[:, at + 64:at + 192], tail).astype(BF16)
            v = jnp.concatenate([b[:, at + 128:at + 192], b[:, at:at + 64]], axis=1)
            va[h, rows] = jnp.where(lane < 64, v, ones).astype(BF16)
        return carry

    lax.fori_loop(0, 4, project, 0)
    x_out.wait()
    w_out.wait()
    g.finish()
    plane.finish()
    sw.finish()


def joined_call(ids, tokens, gain, shift, adapters, bj, bu, wj):
    outs = [shape(128, 2048), shape(1024, 2048), shape(16, PICKED), shape(1, 1792, dtype=F32)] + [
        shape(4, 1024, 128)] * 3 + [shape(2048, 768), shape(16, 1024)]
    return pl.pallas_call(
        joined_kernel, out_shape=outs,
        in_specs=specs(pltpu.SMEM, *[VMEM] * 13, ANY),
        out_specs=specs(VMEM, ANY, VMEM, VMEM, VMEM, VMEM, VMEM, ANY, VMEM),
        scratch_shapes=[VMEM((16, PICKED), BF16), VMEM((1024, 2048), BF16), VMEM((2048, 768), BF16), DMA((2,)),
                        *Swap.sems(8), *GroupGather.SEMS, *LowGather.SEMS, *PlaneGather.SEMS],
        compiler_params=params(1, 40), name="joined")(ids, tokens, gain, shift, *adapters, bj, bu, wj)


def attend_kernel(*refs):
    (qa, ka, va, pk, go, wd, wn), outs, scratch = split_refs(refs, 7, 7)
    qb, ctx, go_all, gos, wd_all, wn_all, low = outs
    (gbuf, c4, out_sem), sw_sems, g_sems, low_sems, d_sems, n_sems = split_refs(scratch, 3, 3, 2, 2, 3)
    _, _, c, _, z = places()
    own = c * 4 + z
    meet(plane_peers() + group_peers())
    there = (1 - c) * 4 + z
    piece = lambda who, j: gbuf.at[pl.ds(pl.multiple_of(who * 128 + j * 32, 32), 32)]
    sw = Swap([(go.at[pl.ds(j * 32, 32)], piece(there, j), piece(own, j)) for j in range(4)], *sw_sems)
    for j in ORDER:
        sw.start(j)
    dense = PlaneGather(wd, wd_all, False, *d_sems)
    down = PlaneGather(wn, wn_all, False, *n_sems)
    dense.start()
    down.start()
    g = GroupGather(gbuf, *g_sems)
    lows = LowGather(low, *low_sems)

    def begin():
        for j in ORDER:
            sw.wait(j)
            g.put(j)

    def low_start():
        gos[...] = block(gbuf, own)[...]
        lows.start(dot_t(pick(pk, "down_out"), block(gbuf, own)[...]).astype(BF16))

    hooks = [lambda: dense.step(0), begin, lambda: dense.step(1), low_start, lambda: down.step(0), lambda: down.step(1),
             lambda: dense.step(2), lambda: (dense.step(3), dense.step(4), dense.step(5)), lambda: g.near(0),
             lambda: down.step(2), lambda: g.near(3), lambda: down.step(3), lambda: g.near(1),
             lambda: down.step(4), lambda: g.near(2), lambda: down.step(5)]
    diagonal_mask = lax.broadcasted_iota(jnp.int32, (256, 256), 0) <= lax.broadcasted_iota(jnp.int32, (256, 256), 1)
    line = lax.broadcasted_iota(jnp.int32, (128, 256), 0)
    lane = lax.broadcasted_iota(jnp.int32, (256, 128), 1)

    def head(h, carry):
        for i in range(4):
            rows = pl.ds(i * 256, 256)
            q = qa[h, rows]
            last = jnp.where(diagonal_mask, dot_t(ka[h, rows], q), MASKED)
            top = jnp.max(last, axis=0, keepdims=True)
            if i:
                before = dot_t(ka[h, pl.ds(0, i * 256)], q)
                top = jnp.maximum(top, jnp.max(before, axis=0, keepdims=True))
            out = dot_o(va[h, rows], jnp.exp(last - top).astype(BF16))
            if i:
                out = out + dot_o(va[h, pl.ds(0, i * 256)], jnp.exp(before - top).astype(BF16))
            total = out[64:65]
            log = -(top + jnp.log(total))
            high = log.astype(BF16).astype(F32)
            middle = (log - high).astype(BF16).astype(F32)
            out = jnp.where(line == 67, high, jnp.where(line == 68, middle, jnp.where(
                line == 69, log - high - middle, out / total)))
            turned = out.T
            c4[h, rows] = turned.astype(BF16)
            qb[h, rows] = jnp.where(lane < 67, q.astype(F32), jnp.where(lane < 70, turned, 0.0)).astype(BF16)
            for k in range(4):
                @pl.when(h == k)
                def _(k=k, i=i):
                    hooks[k * 4 + i]()
        return carry

    lax.fori_loop(0, 4, head, 0)
    for h in (0, 2):
        ctx[:, h * 64:h * 64 + 128] = jnp.concatenate([c4[h, :, :64], c4[h + 1, :, :64]], axis=1)
    for j in ORDER:
        g.far(j)
    for kind in (2, 5, 6, 7):
        g.shared(kind)
    g_out = pltpu.make_async_copy(gbuf, go_all, out_sem.at[0])
    g_out.start()
    lows.wait()
    dense.wait()
    down.wait()
    g_out.wait()
    g.finish()
    dense.finish()
    down.finish()
    sw.finish()


def attend_call(qa, ka, va, pk, go, wd, wn):
    outs = [shape(4, 1024, 128), shape(1024, 256), shape(1024, 2048), shape(128, 2048), shape(256, 2048),
            shape(1024, 2048), shape(16, 1024)]
    return pl.pallas_call(
        attend_kernel, out_shape=outs, in_specs=specs(*[VMEM] * 4, ANY, ANY, ANY),
        out_specs=specs(VMEM, VMEM, ANY, VMEM, ANY, ANY, VMEM),
        scratch_shapes=[VMEM((1024, 2048), BF16), VMEM((4, 1024, 128), BF16), DMA((1,)), *Swap.sems(4),
                        *GroupGather.SEMS, *LowGather.SEMS, *PlaneGather.SEMS, *PlaneGather.SEMS],
        compiler_params=params(2, 40), name="attend")(qa, ka, va, pk, go, wd, wn)


ROOT_HALF = 0.7071067811865476
ROOT_TAU = 0.3989422804014327


def middle_kernel(*refs):
    (ctx, xs, pk, bias, lowg, gain, shift, dense_bias, wd, go, wn, wu), outs, scratch = split_refs(refs, 12, 7)
    mid, x_all, act, dpre, wu_all, low_u, low_d = outs
    (xbuf, ubuf, gbuf, nbuf, dbuf, dact, src, got, part_sem), s_refs, sems = split_refs(scratch, 9, 7)
    g_sems, l_sems, u_sems, t_sems, p_sems = split_refs(sems, 2, 2, 2, 2)
    _, _, c, _, z = places()
    own = c * 4 + z
    meet(plane_peers() + group_peers())
    loads = [pltpu.make_async_copy(a, b, part_sem.at[n]) for n, (a, b) in enumerate(((wd, dbuf), (go, gbuf), (wn, nbuf)))]
    for load in loads:
        load.start()
    plane = PlaneGather(wu, ubuf, True, *p_sems)
    plane.start()
    src[...] = dot_t(pick(pk, "dense_in"), ctx[...]).astype(BF16)
    total = LowSum(src, got, *l_sems)
    total.start()
    s = GroupSum(*s_refs)
    loads[0].wait()

    def part(i):
        put_pair(s.parts, s.order[i], dot(take_pair(ctx, s.order[i]), dbuf[...]).astype(BF16))
        s.give(i)

    part(0)
    part(1)
    s.far()
    plane.step(0)
    plane.step(1)
    part(2)
    s.near_up()
    part(3)
    s.near_down()
    plane.step(2)
    s.pass_on()
    plane.step(3)
    low_total = total.total()
    mid[...] = dot_o(low_total, pick(pk, "dense_out")) + dense_bias[...] + xs[...].astype(F32)
    loads[1].wait()
    loads[2].wait()

    def grad_act(rows):
        dact[rows] = dot_t(gbuf[rows], nbuf[...]) + dot_o(lowg[:, rows], pick(pk, "down_in"))

    tiles(2, 256, grad_act)
    plane.step(4)
    plane.step(5)
    tiles(2, 256, lambda rows: grad_act(pl.ds(pl.multiple_of(rows.start + 512, 256), 256)))
    s.arrive()
    g = GroupGather(xbuf, *g_sems)
    for j in ORDER:
        rows = slice(j * 32, (j + 1) * 32)
        mid[rows] = mid[rows] + s.total(rows)
        xbuf[pl.ds(pl.multiple_of(own * 128 + j * 32, 32), 32)] = layer_norm(mid[rows], gain[...], shift[...]).astype(BF16)
        g.put(j)
    lows = LowGather(low_u, *u_sems)
    lows.start(dot_t(pick(pk, "up_in"), block(xbuf, own)[...]).astype(BF16))
    sums = LowGather(low_d, *t_sems)
    sums.start(low_total)
    plane.wait()
    w_out = pltpu.make_async_copy(ubuf, wu_all, part_sem.at[0])
    w_out.start()
    lows.wait()

    def forward(at):
        x = take_pair(xbuf, at)
        lu = jnp.concatenate([low_u[:, rows] for rows in row_pair(at)], axis=1)

        def run(n, carry):
            cols = pl.ds(pl.multiple_of(n * 256, 256), 256)
            up = pk[:, pl.ds(pl.multiple_of(PICKS["up_out"][0] + n * 256, 128), 256)]
            b = bias[:, pl.ds(pl.multiple_of(768 + n * 256, 256), 256)]
            pre = dot(x, ubuf[:, cols]) + dot_o(lu, up) + b
            cdf = 0.5 * (1.0 + lax.erf(pre * ROOT_HALF))
            put_pair(act, at, (pre * cdf).astype(BF16), cols)
            slope = cdf + pre * (jnp.exp(-0.5 * pre * pre) * ROOT_TAU)
            put_pair(dpre, at, (take_pair(dact, at, cols) * slope).astype(BF16), cols)
            return carry

        lax.fori_loop(0, 4, run, 0)

    g.shared(2)
    forward(z)
    for j in ORDER:
        g.near(j)
    g.shared(5)
    forward(lax.rem(z + 3, 4))
    g.shared(6)
    forward(lax.rem(z + 1, 4))
    for j in ORDER:
        g.far(j)
    g.shared(7)
    x_out = pltpu.make_async_copy(xbuf, x_all, part_sem.at[1])
    x_out.start()
    forward(lax.rem(z + 2, 4))
    sums.wait()
    w_out.wait()
    x_out.wait()
    s.finish()
    g.finish()
    plane.finish()


def middle_call(*args):
    outs = [shape(128, 2048, dtype=F32), shape(1024, 2048), shape(1024, 1024), shape(1024, 1024), shape(2048, 1024),
            shape(16, 1024), shape(16, 1024)]
    return pl.pallas_call(
        middle_kernel, out_shape=outs, in_specs=specs(*[VMEM] * 8, *[ANY] * 4),
        out_specs=specs(VMEM, ANY, VMEM, VMEM, ANY, VMEM, VMEM),
        scratch_shapes=[VMEM((1024, 2048), BF16), VMEM((2048, 1024), BF16), VMEM((1024, 2048), BF16),
                        VMEM((1024, 2048), BF16), VMEM((256, 2048), BF16), VMEM((1024, 1024), F32),
                        VMEM((16, 1024), BF16), VMEM((8, 16, 128), BF16), DMA((3,)), *GroupSum.SCRATCH,
                        *GroupGather.SEMS, *LowSum.SEMS, *LowGather.SEMS, *LowGather.SEMS, *PlaneGather.SEMS],
        compiler_params=params(3, 56), name="middle")(*args)


def back_kernel(*refs):
    (dpre, act, mid, gos, pk, gain, wu, wn, wd), outs, scratch = split_refs(refs, 9, 7)
    dmid, ga_all, dctx, mlp, low_n, low_d, low_u = outs
    (xbuf, ubuf, nbuf, dbuf, src, got, part_sem), s_refs, sems = split_refs(scratch, 7, 7)
    g_sems, l_sems, d_sems, t_sems, _ = split_refs(sems, 2, 2, 2, 2)
    _, _, c, _, z = places()
    own = c * 4 + z
    meet(group_peers())
    loads = [pltpu.make_async_copy(a, b, part_sem.at[n]) for n, (a, b) in enumerate(((wu, ubuf), (wn, nbuf), (wd, dbuf)))]
    for load in loads:
        load.start()
    src[...] = dot_t(pick(pk, "up_out"), dpre[...]).astype(BF16)
    total = LowSum(src, got, *l_sems)
    total.start()
    s = GroupSum(*s_refs)
    loads[0].wait()

    def part(i):
        x = take_pair(dpre, s.order[i])

        def run(n, carry):
            cols = pl.ds(pl.multiple_of(n * 512, 512), 512)
            put_pair(s.parts, s.order[i], dot_t(x, ubuf[cols]).astype(BF16), cols)
            return carry

        lax.fori_loop(0, 4, run, 0)
        s.give(i)

    part(0)
    part(1)
    s.far()
    part(2)
    s.near_up()
    part(3)
    s.near_down()
    s.pass_on()
    low_total = total.total()
    dmid[...] = dot_o(low_total, pick(pk, "up_in"))
    loads[1].wait()

    def forward(rows):
        mlp[rows] = dot(act[rows], nbuf[...]).astype(BF16)

    tiles(4, 256, forward)
    low_n[...] = dot_t(pick(pk, "down_in"), act[...]).astype(BF16)
    s.arrive()
    g = GroupGather(xbuf, *g_sems)
    for j in ORDER:
        rows = slice(j * 32, (j + 1) * 32)
        dmid[rows] = gos[rows].astype(F32) + norm_back(mid[rows], gain[...], dmid[rows] + s.total(rows))
        xbuf[pl.ds(pl.multiple_of(own * 128 + j * 32, 32), 32)] = dmid[rows].astype(BF16)
        g.put(j)
    lows = LowGather(low_d, *d_sems)
    lows.start(dot_t(pick(pk, "dense_out"), block(xbuf, own)[...]).astype(BF16))
    sums = LowGather(low_u, *t_sems)
    sums.start(low_total)
    loads[2].wait()
    lows.wait()

    def context(at):
        ld = jnp.concatenate([low_d[:, rows] for rows in row_pair(at)], axis=1)
        value = dot_t(take_pair(xbuf, at), dbuf[...]) + dot_o(ld, pick(pk, "dense_in"))
        put_pair(dctx, at, value.astype(BF16))

    g.shared(2)
    context(z)
    for j in ORDER:
        g.near(j)
    g.shared(5)
    context(lax.rem(z + 3, 4))
    g.shared(6)
    context(lax.rem(z + 1, 4))
    for j in ORDER:
        g.far(j)
    g.shared(7)
    x_out = pltpu.make_async_copy(xbuf, ga_all, part_sem.at[1])
    x_out.start()
    context(lax.rem(z + 2, 4))
    sums.wait()
    x_out.wait()
    s.finish()
    g.finish()


def back_call(*args):
    outs = [shape(128, 2048, dtype=F32), shape(1024, 2048), shape(1024, 256), shape(1024, 2048), shape(16, 1024),
            shape(16, 1024), shape(16, 1024)]
    return pl.pallas_call(
        back_kernel, out_shape=outs, in_specs=specs(*[VMEM] * 6, *[ANY] * 3),
        out_specs=specs(VMEM, ANY, VMEM, VMEM, VMEM, VMEM, VMEM),
        scratch_shapes=[VMEM((1024, 2048), BF16), VMEM((2048, 1024), BF16), VMEM((1024, 2048), BF16),
                        VMEM((256, 2048), BF16), VMEM((16, 1024), BF16), VMEM((8, 16, 128), BF16), DMA((3,)),
                        *GroupSum.SCRATCH, *GroupGather.SEMS, *LowSum.SEMS, *LowGather.SEMS, *LowGather.SEMS],
        compiler_params=params(4, 56), name="back")(*args)


def attend_back_kernel(*refs):
    (qb, ka, va, ctx, dctx, mlp, low_n, mid, down_bias, pk), outs, scratch = split_refs(refs, 10, 3)
    dfused, layer, low_s = outs
    (g4, dq4, dk4, dv4, dk, dv, got), s_refs, (l_send, l_recv, t_send, t_recv) = split_refs(scratch, 7, 6)
    meet(group_peers())
    s = GroupSum(mlp, *s_refs)
    for i in range(4):
        s.give(i)
    total = LowSum(low_n, got, l_send, l_recv)
    total.start()
    lane = lax.broadcasted_iota(jnp.int32, (1024, 128), 1)
    for h in range(4):
        first = h // 2 * 128
        g = dctx[:, first:first + 128].astype(F32)
        f = ctx[:, first:first + 128].astype(F32)
        here = (lane // 64) == h % 2
        d = -jnp.sum(jnp.where(here, g * f, 0.0), axis=-1, keepdims=True)
        if h % 2:
            g = jnp.concatenate([g[:, 64:], g[:, :64]], axis=1)
        high = d.astype(BF16).astype(F32)
        middle = (d - high).astype(BF16).astype(F32)
        g4[h] = jnp.where(lane < 64, g, jnp.where(lane == 64, high, jnp.where(lane == 65, middle, jnp.where(
            lane == 66, d - high - middle, 0.0)))).astype(BF16)
    sums = LowGather(low_s, t_send, t_recv)

    def low_step():
        value = total.total()
        sums.start(value)
        layer[...] = (mid[...] + down_bias[...] + dot_o(value, pick(pk, "down_out"))).astype(BF16)

    hooks = {0: s.far, 1: s.near_up, 2: s.near_down, 5: low_step, 6: s.pass_on}
    diagonal_mask = lax.broadcasted_iota(jnp.int32, (256, 256), 0) <= lax.broadcasted_iota(jnp.int32, (256, 256), 1)

    def head(h, carry):
        dk[...] = jnp.zeros_like(dk)
        dv[...] = jnp.zeros_like(dv)
        for i in range(4):
            rows = pl.ds(i * 256, 256)
            q, g = qb[h, rows], g4[h, rows]

            def span(keys, mask):
                k = ka[h, keys]
                score = dot_t(k, q)
                if mask:
                    score = jnp.where(diagonal_mask, score, MASKED)
                p = jnp.exp(score)
                ds = (p * dot_t(va[h, keys], g)).astype(BF16)
                dk[keys] += dot(ds, q)
                dv[keys] += dot(p.astype(BF16), g)
                return dot_o(k, ds)

            dq = span(rows, True)
            if i:
                dq = dq + span(pl.ds(0, i * 256), False)
            dq4[h, rows] = (dq * 0.125).T.astype(BF16)
            for n, hook in hooks.items():
                if n % 4 == i:
                    @pl.when(h == n // 4)
                    def _(hook=hook):
                        hook()
        dk4[h] = dk[...].astype(BF16)
        dv4[h] = dv[...].astype(BF16)
        return carry

    lax.fori_loop(0, 4, head, 0)
    for h in (0, 2):
        dfused[:, h * 192:h * 192 + 384] = jnp.concatenate(
            [a[k, :, :64] for k in (h, h + 1) for a in (dq4, dk4, dv4)], axis=1)
    s.arrive()
    value = total_again(low_s, pk)
    layer[...] = (mid[...] + down_bias[...] + value + s.total()).astype(BF16)
    sums.wait()
    s.finish()


def total_again(low_s, pk):
    _, _, c, _, z = places()
    own = pl.ds(pl.multiple_of((c * 4 + z) * 128, 128), 128)
    return dot_o(low_s[:, own], pick(pk, "down_out"))


def attend_back_call(*args):
    outs = [shape(1024, 768), shape(128, 2048), shape(16, 1024)]
    return pl.pallas_call(
        attend_back_kernel, out_shape=outs, in_specs=specs(*[VMEM] * 10), out_specs=specs(*[VMEM] * 3),
        scratch_shapes=[VMEM((4, 1024, 128), BF16)] * 4 + [VMEM((1024, 128), F32)] * 2 + [
            VMEM((8, 16, 128), BF16)] + GroupSum.SCRATCH[1:] + LowSum.SEMS + LowGather.SEMS,
        compiler_params=params(5, 48), name="attend_back")(*args)


def last_kernel(*refs):
    (dfused, dmid, xs, layer, gain, pk, wj), outs, scratch = split_refs(refs, 7, 3)
    grad, out, low_s = outs
    (wbuf, mine, back, src, got, part_sem), s_refs, sems = split_refs(scratch, 6, 7)
    sw_sems, l_sems, t_sems, _ = split_refs(sems, 3, 2, 2)
    meet(group_peers() + [diagonal()])
    load = pltpu.make_async_copy(wj, wbuf, part_sem.at[0])
    load.start()
    sub = lambda ref, j: ref.at[pl.ds(j * 32, 32)]
    pairs = [(sub(mine, j), sub(back, j), sub(back, j)) for j in range(4)] + [(layer, out, out)]
    sw = Swap(pairs, *sw_sems)
    sw.start(4)
    src[...] = dot_t(pick(pk, "joined_out"), dfused[...]).astype(BF16)
    total = LowSum(src, got, *l_sems)
    total.start()
    s = GroupSum(*s_refs)
    load.wait()

    def part(i):
        x = take_pair(dfused, s.order[i])

        def run(n, carry):
            cols = pl.ds(pl.multiple_of(n * 512, 512), 512)
            put_pair(s.parts, s.order[i], dot_t(x, wbuf[cols]).astype(BF16), cols)
            return carry

        lax.fori_loop(0, 4, run, 0)
        s.give(i)

    part(0)
    part(1)
    s.far()
    part(2)
    s.near_up()
    part(3)
    s.near_down()
    s.pass_on()
    low_total = total.total()
    sums = LowGather(low_s, *t_sems)
    sums.start(low_total)
    grad[...] = dot_o(low_total, pick(pk, "joined_in"))
    s.arrive()
    for j in ORDER:
        rows = slice(j * 32, (j + 1) * 32)
        value = dmid[rows] + norm_back(xs[rows].astype(F32), gain[...], grad[rows] + s.total(rows))
        mine[rows] = value.astype(BF16)
        sw.start(j)
    for n in range(5):
        sw.wait(n)
    grad[...] = back[...].astype(F32)
    sums.wait()
    s.finish()
    sw.finish()


def last_call(*args):
    outs = [shape(128, 2048, dtype=F32), shape(128, 2048), shape(16, 1024)]
    return pl.pallas_call(
        last_kernel, out_shape=outs, in_specs=specs(*[VMEM] * 6, ANY), out_specs=specs(*[VMEM] * 3),
        scratch_shapes=[VMEM((2048, 768), BF16), VMEM((128, 2048), BF16), VMEM((128, 2048), BF16),
                        VMEM((16, 1024), BF16), VMEM((8, 16, 128), BF16), DMA((1,)), *GroupSum.SCRATCH,
                        *Swap.sems(5), *LowSum.SEMS, *LowGather.SEMS],
        compiler_params=params(6, 40), name="last")(*args)


SWAP = ((0, 0), (1, 2), (2, 1), (3, 3))


def finish(mine, hot):
    turn = lambda a: jnp.swapaxes(a, 1, 2)
    every = lax.all_gather(mine, PLANE, axis=0, tiled=False)
    onehot = lax.all_gather(hot[:, 0], PLANE, axis=1, tiled=False)
    sums = lax.dot_general(onehot, every, (((1,), (0,)), ((), ())), preferred_element_type=F32)
    split = lax.ppermute(sums[:, :, :3072].astype(BF16), ("c", "xh"), SWAP).astype(F32)
    whole = lax.all_gather(sums[:, :, 3072:].astype(BF16), ("c", "z"), axis=0, tiled=False).astype(F32)
    whole = whole.reshape(8, 8, 16, 4, 256)
    per = [whole[:, :, :, i].transpose(1, 2, 0, 3).reshape(8, 16, 2048) for i in range(4)]
    return (turn(per[0]), split[:, :, :768], turn(split[:, :, 768:1024]), per[1],
            turn(per[2]), split[:, :, 1024:2048], turn(split[:, :, 2048:3072]), per[3])


def local(tokens, grad_out, adapter_ids, first_gain, first_shift, joined_weight, joined_bias, dense_weight,
          dense_bias, second_gain, second_shift, up_weight, up_bias, down_weight, down_bias, joined_adapt_in,
          joined_adapt_out, dense_adapt_in, dense_adapt_out, up_adapt_in, up_adapt_out, down_adapt_in,
          down_adapt_out):
    c, xh, z = lax.axis_index("c"), lax.axis_index("xh"), lax.axis_index("z")
    group = c * 4 + z
    turn = lambda a: jnp.swapaxes(a, 1, 2)
    line = lambda a: a.reshape(1, -1)
    adapters = [turn(joined_adapt_in), joined_adapt_out, turn(dense_adapt_in), dense_adapt_out, turn(up_adapt_in),
                up_adapt_out, turn(down_adapt_in), down_adapt_out]
    xs, x1_all, pk, bias, qa, ka, va, w_joined, low_q = joined_call(
        adapter_ids, tokens, line(first_gain), line(first_shift), adapters, line(joined_bias), line(up_bias),
        joined_weight)
    qb, context, go_all, gos, w_dense, w_down, low_g = attend_call(qa, ka, va, pk, grad_out, dense_weight, down_weight)
    mid, x2_all, act, grad_pre, w_up, low_u, sum_d = middle_call(
        context, xs, pk, bias, low_g, line(second_gain), line(second_shift), line(dense_bias), w_dense, go_all, w_down,
        up_weight)
    grad_mid, ga_all, grad_context, mlp, low_n, low_d, sum_u = back_call(
        grad_pre, act, mid, gos, pk, line(second_gain), w_up, w_down, w_dense)
    grad_joined, layer, sum_n = attend_back_call(qb, ka, va, context, grad_context, mlp, low_n, mid, line(down_bias), pk)
    grad_tokens, layer_out, sum_q = last_call(grad_joined, grad_mid, xs, layer, line(first_gain), pk, w_joined)

    cols = [lax.dynamic_slice_in_dim(a, group * 256, 256, 1) for a in (x1_all, ga_all, x2_all, go_all)]
    halves = [dot(low, col) for low, col in zip((sum_q, sum_d, sum_u, sum_n), cols)]
    wide = [dot(low_q, grad_joined), dot(low_d, context), dot(low_u, grad_pre), dot(low_g, act)]
    mine = jnp.concatenate(wide + halves, axis=1).astype(BF16)
    first, n = PICKS["hot"]
    return (layer_out, grad_tokens, *finish(mine, pk[:8, first:first + n]))


def solution(mesh):
    fine = Mesh(mesh.devices.reshape(2, 4, 2, 2, 4), AXES)
    rows, cols = P(FSDP, TP), P(TP, FSDP)
    tok = P((*FSDP, *TP), None)
    last, middle, one = P(None, None, TP), P(None, TP, None), P(TP)
    return jax.shard_map(
        local, mesh=fine,
        in_specs=(tok, tok, P(FSDP), P(), P(), rows, one, cols, P(), P(), P(), rows, one, cols, P(), P(), last,
                  middle, P(), P(), last, middle, P()),
        out_specs=(tok, tok, P(), last, middle, P(), P(), last, middle, P()), check_vma=False)
```

```python
import functools

import jax
import jax.numpy as jnp
from jax import lax
from jax.experimental import pallas as pl
from jax.experimental.pallas import tpu as pltpu
from jax.sharding import Mesh
from jax.sharding import PartitionSpec as P

HEADS = 32
EPSILON = 1e-05
MASKED = -1e30
AXES = ("xl", "y", "c", "xh", "z")
FSDP = ("xl", "y", "c")
TP = ("xh", "z")
PLANE = ("xl", "y", "xh")
MESH_ID = pl.DeviceIdType.MESH
ANY = pl.ANY
VMEM = pltpu.VMEM
DMA = pltpu.SemaphoreType.DMA
F32 = jnp.float32
BF16 = jnp.bfloat16
ORDER = (0, 3, 1, 2)
PICKS = dict(joined_in=(0, 2048), joined_out=(2048, 768), hot=(2816, 128), up_in=(2944, 2048), up_out=(4992, 1024),
             dense_in=(6016, 256), dense_out=(6272, 2048), down_in=(8320, 1024), down_out=(9344, 2048))
PICKED = 11392


def remote(src, dst, sems, index, device):
    send, recv = sems
    return pltpu.make_async_remote_copy(
        src_ref=src, dst_ref=dst, send_sem=send.at[index], recv_sem=recv.at[index],
        device_id=device, device_id_type=MESH_ID)


def places():
    return tuple(lax.axis_index(a) for a in AXES)


def at_home():
    _, _, c, xh, _ = places()
    return 1 - (xh - c) * (xh - c)


def meet(peers):
    barrier = pltpu.get_barrier_semaphore()
    for p in peers:
        pl.semaphore_signal(barrier, inc=1, device_id=p, device_id_type=MESH_ID)
    pl.semaphore_wait(barrier, len(peers))


def group_peer(n):
    _, _, c, _, z = places()
    return {"c": lax.rem(c + n // 4, 2), "z": lax.rem(z + n % 4, 4)}


def group_peers():
    return [group_peer(n) for n in range(1, 8)]


def diagonal():
    _, _, c, xh, _ = places()
    return {"c": 1 - c, "xh": 1 - xh}


def plane_peers():
    xl, y, c, xh, _ = places()
    peers = []
    for d in range(1, 4):
        for core in (0, 1):
            peers.append({"y": lax.rem(y + d, 4), "c": core})
            x = lax.rem(xh * 2 + xl + d, 4)
            peers.append({"xh": x // 2, "xl": lax.rem(x, 2), "c": core})
    return peers


def block(ref, n, size=128):
    return ref.at[pl.ds(pl.multiple_of(n * size, size), size)]


class GroupGather:
    SEMS = [DMA((8, 4)), DMA((8, 4))]

    def __init__(self, dst, send, recv):
        self.dst, self.sems = dst, (send, recv)
        _, _, self.c, _, self.z = places()
        self.up, self.down, self.other = group_peer(1), group_peer(3), group_peer(4)

    def at(self, core, z, j):
        return self.dst.at[pl.ds(pl.multiple_of((core * 4 + z) * 128 + j * 32, 32), 32)]

    def copy(self, z, j, kind, device):
        ref = self.at(self.c, z, j)
        return remote(ref, ref, self.sems, (kind, j), device)

    def put(self, j):
        self.copy(self.z, j, 0, self.up).start()
        self.copy(self.z, j, 1, self.down).start()
        self.copy(self.z, j, 2, self.other).start()

    def near(self, j):
        below, above = lax.rem(self.z + 3, 4), lax.rem(self.z + 1, 4)
        self.copy(below, j, 0, self.up).wait_recv()
        if j < 2:
            self.copy(below, j, 3, self.up).start()
        self.copy(below, j, 5, self.other).start()
        self.copy(above, j, 1, self.down).wait_recv()
        if j >= 2:
            self.copy(above, j, 4, self.down).start()
        self.copy(above, j, 6, self.other).start()

    def far(self, j):
        opposite = lax.rem(self.z + 2, 4)
        self.copy(opposite, j, 3 if j < 2 else 4, self.up).wait_recv()
        self.copy(opposite, j, 7, self.other).start()

    def shared(self, kind):
        for j in ORDER:
            self.copy(self.z, j, kind, self.other).wait_recv()

    def finish(self):
        for j in ORDER:
            for kind in (0, 1, 2, 3 if j < 2 else 4, 5, 6, 7):
                self.copy(self.z, j, kind, self.other).wait_send()


class LowGather:
    SEMS = [DMA((8,)), DMA((8,))]

    def __init__(self, dst, send, recv):
        self.dst, self.sems = dst, (send, recv)
        _, _, c, _, z = places()
        self.own = pl.ds(pl.multiple_of((c * 4 + z) * 128, 128), 128)

    def copies(self):
        ref = self.dst.at[:, self.own]
        return [remote(ref, ref, self.sems, (n,), group_peer(n)) for n in range(1, 8)]

    def start(self, value):
        self.dst[:, self.own] = value
        for copy in self.copies():
            copy.start()

    def wait(self):
        for copy in self.copies():
            copy.wait()


class LowSum:
    SEMS = [DMA((8,)), DMA((8,))]

    def __init__(self, src, got, send, recv):
        self.src, self.got, self.sems = src, got, (send, recv)
        _, _, self.c, _, self.z = places()

    def copies(self):
        out = []
        for n in range(1, 8):
            p = group_peer(n)
            cols = pl.ds(pl.multiple_of((p["c"] * 4 + p["z"]) * 128, 128), 128)
            out.append(remote(self.src.at[:, cols], self.got.at[n], self.sems, (n,), p))
        return out

    def start(self):
        for copy in self.copies():
            copy.start()

    def total(self):
        for copy in self.copies():
            copy.wait()
        own = pl.ds(pl.multiple_of((self.c * 4 + self.z) * 128, 128), 128)
        out = self.src[:, own].astype(F32)
        for n in range(1, 8):
            out = out + self.got[n].astype(F32)
        return out.astype(BF16)


class PlaneGather:
    SEMS = [DMA((1,)), DMA((22,)), DMA((16,))]

    def __init__(self, src, dst, by_rows, local_sem, send, recv):
        self.src, self.dst, self.by_rows, self.local_sem, self.sems = src, dst, by_rows, local_sem, (send, recv)
        self.xl, self.y, self.c, self.xh, _ = places()
        self.x = self.xh * 2 + self.xl
        self.home = at_home()

    def slot(self, xl, y, core):
        k = (xl * 4 + y) * 2 + core
        if self.by_rows:
            return k, block(self.dst, k)
        return k, self.dst.at[:, pl.ds(pl.multiple_of(k * 128, 128), 128)]

    def send(self, src, where, n, device):
        k, dst = where
        send, recv = self.sems
        return pltpu.make_async_remote_copy(
            src_ref=src, dst_ref=dst, send_sem=send.at[n], recv_sem=recv.at[k],
            device_id=device, device_id_type=MESH_ID)

    def arrived(self, where):
        self.send(where[1], where, 0, {"c": 1 - self.c}).wait_recv()

    def chip_x(self, d, core):
        x = lax.rem(self.x + d, 4)
        return {"xh": x // 2, "xl": lax.rem(x, 2), "c": core}

    def chip_y(self, d, core):
        return {"y": lax.rem(self.y + d, 4), "c": core}

    def first(self, act):
        own = self.slot(self.xl, self.y, self.c)

        @pl.when(self.c == 0)
        def _():
            for d in (1, 3, 2):
                act(self.send(self.src, own, d, self.chip_x(d, self.xh)))

        @pl.when(self.c == 1)
        def _():
            for d in (1, 3, 2):
                act(self.send(self.src, own, d, self.chip_y(d, self.xh)))

        @pl.when(self.home == 0)
        def _():
            act(self.send(self.src, own, 0, {"c": 1 - self.c}))

    def start(self):
        @pl.when(self.home == 1)
        def _():
            pltpu.make_async_copy(self.src, self.slot(self.xl, self.y, self.c)[1], self.local_sem.at[0]).start()

        self.first(lambda copy: copy.start())

    def columns(self):
        one = self.home * self.xl
        return one, 1 - one

    def rows_step(self, n, act):
        where = self.slot(self.columns()[n], self.y, 0)
        for d in (1, 3, 2):
            act(self.send(where[1], where, 4 + n * 3 + d - 1, self.chip_y(d, self.c)))

    def columns_step(self, n, act):
        where = self.slot(self.xl, lax.rem(self.y + n, 4), 1)

        @pl.when(self.home == 1)
        def _():
            for d in (1, 3, 2):
                act(self.send(where[1], where, 10 + n * 3 + d - 1, self.chip_x(d, self.c)))

    def step(self, n):
        if n == 0:
            @pl.when(self.home == 1)
            def _():
                pltpu.make_async_copy(self.src, self.slot(self.xl, self.y, self.c)[1], self.local_sem.at[0]).wait()
        if n < 2:
            where = self.slot(self.columns()[n], self.y, 0)
            if n == 0:
                @pl.when(self.home * (1 - self.c) == 0)
                def _():
                    self.arrived(where)
            else:
                self.arrived(where)
            self.rows_step(n, lambda copy: copy.start())
        else:
            where = self.slot(self.xl, lax.rem(self.y + n - 2, 4), 1)
            here = self.home * (1 - self.c) if n == 2 else self.home

            @pl.when(here == 1)
            def _():
                self.arrived(where)

            self.columns_step(n - 2, lambda copy: copy.start())

    def wait(self):
        for xl in (0, 1):
            for d in (1, 2, 3):
                self.arrived(self.slot(xl, lax.rem(self.y + d, 4), 0))
        one, two = self.columns()
        for y in range(4):
            self.arrived(self.slot(two, y, 1))

        @pl.when(self.home == 0)
        def _():
            for y in range(4):
                self.arrived(self.slot(one, y, 1))

    def finish(self):
        self.first(lambda copy: copy.wait_send())
        for n in (0, 1):
            self.rows_step(n, lambda copy: copy.wait_send())
        for n in range(4):
            self.columns_step(n, lambda copy: copy.wait_send())


class GroupSum:
    NAMES = ("far_up", "far_down", "up_high", "down_low", "up_low", "down_high")
    SCRATCH = [VMEM((1024, 2048), BF16), VMEM((4, 128, 2048), BF16), VMEM((3, 128, 2048), BF16),
               VMEM((2, 64, 2048), BF16), VMEM((2, 128, 2048), BF16), DMA((10,)), DMA((10,))]

    def __init__(self, parts, near, sent, half, full, send, recv):
        self.parts, self.near, self.sent, self.half, self.full, self.sems = parts, near, sent, half, full, (send, recv)
        _, _, self.c, _, self.z = places()
        self.up, self.down, self.other = group_peer(1), group_peer(3), group_peer(4)
        self.order = [lax.rem(self.z + d, 4) for d in (2, 1, 3, 0)]

    def part(self, core, i):
        return block(self.parts, core * 4 + self.order[i])

    def given(self, i):
        return remote(self.part(1 - self.c, i), self.near.at[i], self.sems, (i,), self.other)

    def give(self, i):
        self.given(i).start()

    def pair(self, i, rows=slice(None)):
        return self.part(self.c, i)[rows].astype(F32) + self.near[i, rows].astype(F32)

    def piece(self, name):
        low, high = pl.ds(0, 64), pl.ds(64, 64)
        n = self.NAMES.index(name)
        src = (self.sent.at[0, low], self.sent.at[0, high], self.sent.at[1, high], self.sent.at[2, low],
               self.sent.at[1, low], self.sent.at[2, high])[n]
        dst = (self.half.at[0], self.half.at[1], self.full.at[0, high], self.full.at[1, low],
               self.full.at[0, low], self.full.at[1, high])[n]
        return remote(src, dst, self.sems, (4 + n,), (self.up, self.down)[n % 2])

    def far(self):
        self.given(0).wait_recv()
        self.sent[0] = self.pair(0).astype(BF16)
        self.piece("far_up").start()
        self.piece("far_down").start()

    def near_up(self):
        self.given(1).wait_recv()
        self.sent[1, pl.ds(64, 64)] = self.pair(1, pl.ds(64, 64)).astype(BF16)
        self.piece("up_high").start()

    def near_down(self):
        self.given(2).wait_recv()
        self.sent[2, pl.ds(0, 64)] = self.pair(2, pl.ds(0, 64)).astype(BF16)
        self.piece("down_low").start()

    def pass_on(self):
        low, high = pl.ds(0, 64), pl.ds(64, 64)
        self.piece("far_up").wait_recv()
        self.sent[1, low] = (self.pair(1, low) + self.half[0].astype(F32)).astype(BF16)
        self.piece("up_low").start()
        self.piece("far_down").wait_recv()
        self.sent[2, high] = (self.pair(2, high) + self.half[1].astype(F32)).astype(BF16)
        self.piece("down_high").start()

    def arrive(self):
        self.given(3).wait_recv()
        for name in ("up_high", "down_low", "up_low", "down_high"):
            self.piece(name).wait_recv()

    def total(self, rows=slice(None)):
        return self.pair(3, rows) + self.full[0, rows].astype(F32) + self.full[1, rows].astype(F32)

    def finish(self):
        for name in self.NAMES:
            self.piece(name).wait_send()
        for i in range(4):
            self.given(i).wait_send()


def params(cid, mib):
    return pltpu.CompilerParams(collective_id=cid, has_side_effects=True, vmem_limit_bytes=mib << 20)


def plain(mib):
    return pltpu.CompilerParams(vmem_limit_bytes=mib << 20)


def shape(*dims, dtype=BF16):
    return jax.ShapeDtypeStruct(dims, dtype)


def specs(*spaces):
    return [pl.BlockSpec(memory_space=s) for s in spaces]


def layer_norm(rows_in, gain, shift):
    row_mean = jnp.mean(rows_in, axis=-1, keepdims=True)
    centered = rows_in - row_mean
    variance = jnp.mean(centered * centered, axis=-1, keepdims=True)
    return centered * lax.rsqrt(variance + EPSILON) * gain + shift


def norm_back(rows_in, gain, grad):
    row_mean = jnp.mean(rows_in, axis=-1, keepdims=True)
    centered = rows_in - row_mean
    inverse = lax.rsqrt(jnp.mean(centered * centered, axis=-1, keepdims=True) + EPSILON)
    n = centered * inverse
    e = gain * grad
    return (e - jnp.mean(e, axis=-1, keepdims=True) - n * jnp.mean(e * n, axis=-1, keepdims=True)) * inverse


def dot(a, b, dims=((1,), (0,))):
    return lax.dot_general(a, b, (dims, ((), ())), preferred_element_type=F32)


def dot_t(a, b):
    return dot(a, b, ((1,), (1,)))


def dot_o(a, b):
    return dot(a, b, ((0,), (0,)))


def tiles(count, size, body):
    def run(i, carry):
        body(pl.ds(pl.multiple_of(i * size, size), size))
        return carry

    lax.fori_loop(0, count, run, 0)


def split_refs(refs, *counts):
    refs, out = list(refs), []
    for n in counts:
        out.append(refs[:n])
        refs = refs[n:]
    return (*out, refs)


def pick(ref, name):
    first, n = PICKS[name]
    return ref[:, pl.ds(first, n)]


def row_pair(z):
    return (pl.ds(pl.multiple_of(z * 128, 128), 128), pl.ds(pl.multiple_of(512 + z * 128, 128), 128))


def take_pair(ref, z, cols=slice(None)):
    a, b = row_pair(z)
    return jnp.concatenate([ref[a, cols], ref[b, cols]], axis=0)


def put_pair(ref, z, value, cols=slice(None)):
    a, b = row_pair(z)
    ref[a, cols] = value[:128]
    ref[b, cols] = value[128:]


class Swap:
    def __init__(self, pairs, local, send, recv):
        self.pairs, self.local, self.sems, self.home = pairs, local, (send, recv), at_home()

    def near_copy(self, n):
        src, _, dst = self.pairs[n]
        return pltpu.make_async_copy(src, dst, self.local.at[n])

    def far_copy(self, n):
        src, dst, _ = self.pairs[n]
        return remote(src, dst, self.sems, (n,), diagonal())

    def start(self, n):
        @pl.when(self.home == 1)
        def _():
            self.near_copy(n).start()

        @pl.when(self.home == 0)
        def _():
            self.far_copy(n).start()

    def wait(self, n):
        @pl.when(self.home == 1)
        def _():
            self.near_copy(n).wait()

        @pl.when(self.home == 0)
        def _():
            self.far_copy(n).wait_recv()

    def finish(self):
        @pl.when(self.home == 0)
        def _():
            for n in range(len(self.pairs)):
                self.far_copy(n).wait_send()

    @staticmethod
    def sems(n):
        return [DMA((n,)), DMA((n,)), DMA((n,))]


class Spread:
    SCRATCH = [VMEM((16, 5, 8, 128), BF16), VMEM((16, 5, 8, 128), BF16), VMEM((8, 3, 8, 128), BF16),
               VMEM((8, 8, 128), BF16), DMA((16,)), DMA((16,)), DMA((9,)), DMA((16,)), DMA((20,)), DMA((20,)), DMA((2,))]

    def __init__(self, split, whole, send, got, part, full, one_send, one_recv, two_send, two_recv, send3, recv3, local):
        self.split, self.whole, self.send, self.got, self.part, self.full = split, whole, send, got, part, full
        self.one, self.two, self.three, self.local = (one_send, one_recv), (two_send, two_recv), (send3, recv3), local
        self.xl, self.y, self.c, self.xh, self.z = places()
        self.q = (self.xh * 2 + self.xl) * 4 + self.y
        self.home = at_home()

    def put(self, n, value):
        for m in range(4):
            k = 2 * n + m
            where = (k // 3, k % 3) if k < 48 else (k - 48, 3)
            row, col = m % 2 * 8, m // 2 * 128
            self.send[where] = value[row:row + 8, col:col + 128].astype(BF16)

    def mark(self, hot):
        for j in range(16):
            self.send[j, 4] = hot

    def chip(self, n):
        q = lax.rem(self.q + n, 16)
        x = q // 4
        return q, {"xh": x // 2, "xl": lax.rem(x, 2), "y": lax.rem(q, 4)}

    def to_owners(self):
        out = []
        for n in range(1, 16):
            q, device = self.chip(n)
            out.append(remote(self.send.at[q], self.got.at[n], self.one, (n,), device))
        return out

    def start(self):
        for copy in self.to_owners():
            copy.start()

    def add(self):
        self.got[0] = self.send[self.q]
        for copy in self.to_owners():
            copy.wait_recv()
        for b in range(8):
            total = jnp.zeros((4, 8, 128), F32)
            for n in range(16):
                hot = self.got[n, 4].astype(F32)[b:b + 1]
                total = total + self.got[n, 0:4].astype(F32) * hot
            total = total.astype(BF16)
            self.part[b] = total[:3]
            self.full[b] = total[3]

    def split_copies(self):
        out = []
        for e in (0, 1):
            for d in range(4):
                device = {"xh": self.c, "xl": lax.rem(self.xl + e, 2), "y": lax.rem(self.y + d, 4)}
                send, recv = self.two
                out.append(pltpu.make_async_remote_copy(
                    src_ref=self.part, dst_ref=self.split.at[self.q], send_sem=send.at[e * 4 + d],
                    recv_sem=recv.at[self.q], device_id=device, device_id_type=MESH_ID))
        return out

    def split_own(self):
        return pltpu.make_async_copy(self.part, self.split.at[self.q], self.local.at[0])

    def whole_own(self):
        return pltpu.make_async_copy(self.full, self.whole.at[self.c * 4 + self.z, self.q], self.local.at[1])

    def line_copies(self):
        where = self.whole.at[self.c * 4 + self.z, self.q]
        return [remote(self.full, where, self.three, (d,), {"z": lax.rem(self.z + d, 4)}) for d in (1, 2, 3)]

    def plane_copies(self):
        where = self.whole.at[pl.ds(self.c * 4, 4), self.q]
        return [remote(where, where, self.three, (4 + n,), self.chip(n)[1]) for n in range(1, 16)]

    def shared_whole(self):
        where = self.whole.at[pl.ds(self.c * 4, 4)]
        return remote(where, where, self.three, (0,), {"c": 1 - self.c})

    def shared_split(self):
        send, recv = self.two
        return pltpu.make_async_remote_copy(
            src_ref=self.split, dst_ref=self.split, send_sem=send.at[8], recv_sem=recv.at[0],
            device_id={"c": 1 - self.c}, device_id_type=MESH_ID)

    def deal(self):
        self.whole_own().start()
        for copy in self.line_copies():
            copy.start()
        copies = self.split_copies()

        @pl.when(self.home == 1)
        def _():
            self.split_own().start()

        @pl.when(self.home == 0)
        def _():
            copies[0].start()

        for copy in copies[1:]:
            copy.start()

    def deal_plane(self):
        self.whole_own().wait()
        for copy in self.line_copies():
            copy.wait_recv()
        for copy in self.plane_copies():
            copy.start()

    def share(self):
        @pl.when(self.home == 1)
        def _():
            self.split_own().wait()
            send, recv = self.two
            for q in range(16):
                @pl.when(self.q != q)
                def _(q=q):
                    pltpu.make_async_remote_copy(
                        src_ref=self.part, dst_ref=self.split.at[q], send_sem=send.at[0], recv_sem=recv.at[q],
                        device_id={"c": 1 - self.c}, device_id_type=MESH_ID).wait_recv()

            self.shared_split().start()

        for copy in self.plane_copies():
            copy.wait_recv()
        self.shared_whole().start()

    def finish(self):
        self.shared_whole().wait()

        @pl.when(self.home == 1)
        def _():
            self.shared_split().wait_send()

        @pl.when(self.home == 0)
        def _():
            self.shared_split().wait_recv()
            self.split_copies()[0].wait_send()

        for copy in self.split_copies()[1:] + self.line_copies() + self.plane_copies() + self.to_owners():
            copy.wait_send()


def far_peers():
    xl, y, _, xh, _ = places()
    peers = []
    for d in range(1, 4):
        x = lax.rem(xh * 2 + xl + d, 4)
        for e in range(1, 4):
            peers.append({"xh": x // 2, "xl": lax.rem(x, 2), "y": lax.rem(y + e, 4)})
    return peers


ROOT_HALF = 0.7071067811865476
ROOT_TAU = 0.3989422804014327
SETS = dict(joined_in=(0, 0), up_in=(128, 0), dense_out=(256, 0), down_out=(384, 0), up_out=(512, 0),
            down_in=(512, 1024), joined_out=(640, 0), dense_in=(640, 768))


def cast_parts(value):
    high = value.astype(BF16).astype(F32)
    middle = (value - high).astype(BF16).astype(F32)
    return high, middle, value - high - middle


def block_kernel(*refs):
    (ids, tokens, go, *vectors), adapters, shards, outs, scratch = split_refs(refs, 11, 8, 4, 4)
    back, out, split, whole = outs
    names = list(SCRATCH)
    v = dict(zip(names, scratch))
    rest = list(scratch[len(names):])

    def sems(n):
        taken = rest[:n]
        del rest[:n]
        return taken

    load_sem, vector_sem, copy_sem = sems(3)
    xl, y, c, xh, z = places()
    own = c * 4 + z
    mine_rows = pl.ds(pl.multiple_of(own * 128, 128), 128)
    there_rows = (1 - c) * 4 + z
    gain1, shift1, gain2, shift2, bias_d, bias_n = (v["lines"].at[n:n + 1] for n in range(6))
    pk, xs, xbuf, gbuf = v["pk"], v["xs"], v["xbuf"], v["gbuf"]
    sets = v["parts"]
    loads = {}
    for n, (name, ref) in enumerate(zip(SETS, adapters)):
        row, col = SETS[name]
        loads[name] = pltpu.make_async_copy(ref, sets.at[pl.ds(row, 128), pl.ds(col, ref.shape[1])], load_sem.at[n])
        loads[name].start()
    lines = [pltpu.make_async_copy(ref, v["lines"].at[n:n + 1], vector_sem.at[n]) for n, ref in enumerate(vectors[:6])]
    for line in lines:
        line.start()
    meet(plane_peers() + group_peers() + far_peers())

    bias = v["bias"]
    mine = v["mine"]
    piece = lambda who, j: gbuf.at[pl.ds(pl.multiple_of(who * 128 + j * 32, 32), 32)]
    sub = lambda ref, j: ref.at[pl.ds(j * 32, 32)]
    cut = 2944
    pairs = [(sub(tokens, j), sub(xs, j), sub(xs, j)) for j in range(4)]
    pairs += [(m, p, p) for m, p in ((mine.at[:, :cut], pk.at[:, :cut]), (mine.at[:, cut:], pk.at[:, cut:]),
                                     (vectors[6], bias.at[:, :1024]), (vectors[7], bias.at[:, 1024:]))]
    pairs += [(sub(go, j), piece(there_rows, j), piece(own, j)) for j in range(4)]
    sw = Swap(pairs, *sems(3))
    for j in ORDER:
        sw.start(j)
    joined = PlaneGather(shards[0], v["wj"], True, *sems(3))
    dense = PlaneGather(shards[1], v["wd"], False, *sems(3))
    down = PlaneGather(shards[2], v["wn"], False, *sems(3))
    up = PlaneGather(shards[3], v["wu"], True, *sems(3))
    joined.start()
    set_id = ids[0]
    for name, (row, col) in SETS.items():
        first, n = PICKS[name]
        loads[name].wait()
        chosen = sets[row:row + 16, col:col + n]
        for k in range(1, 8):
            chosen = jnp.where(set_id == k, sets[row + k * 16:row + k * 16 + 16, col:col + n], chosen)
        mine[:, first:first + n] = chosen
    first, n = PICKS["hot"]
    mine[:, first:first + n] = jnp.where(lax.broadcasted_iota(jnp.int32, (16, 128), 0) == set_id, 1.0, 0.0).astype(BF16)
    for n in range(4, 8):
        sw.start(n)
    for line in lines:
        line.wait()
    g1 = GroupGather(xbuf, *sems(2))
    low_q = LowGather(v["low_q"], *sems(2))
    for j in ORDER:
        sw.wait(j)
        x1 = layer_norm(xs[j * 32:(j + 1) * 32].astype(F32), gain1[...], shift1[...])
        xbuf[pl.ds(pl.multiple_of(own * 128 + j * 32, 32), 32)] = x1.astype(BF16)
        g1.put(j)
    sw.wait(4)
    low_q.start(dot_t(pick(pk, "joined_in"), xbuf[mine_rows]).astype(BF16))
    for j in ORDER:
        sw.start(8 + j)
    g1.near(0)
    joined.step(0)
    joined.step(1)
    g1.near(3)
    joined.step(2)
    joined.step(3)
    g1.near(1)
    joined.step(4)
    joined.step(5)
    g1.near(2)
    for n in range(5, 8):
        sw.wait(n)
    for j in ORDER:
        g1.far(j)
    g2 = GroupGather(gbuf, *sems(2))
    for j in ORDER:
        sw.wait(8 + j)
        g2.put(j)
    low_g = LowGather(v["low_g"], *sems(2))
    low_g.start(dot_t(pick(pk, "down_out"), gbuf[mine_rows]).astype(BF16))
    v["gos"][...] = gbuf[mine_rows]
    dense.start()
    for kind in (2, 5, 6, 7):
        g1.shared(kind)
    joined.wait()
    down.start()
    low_q.wait()

    lane = lax.broadcasted_iota(jnp.int32, (256, 128), 1)
    row = lax.broadcasted_iota(jnp.int32, (256, 128), 0)
    qa, ka, va = v["qa"], v["ka"], v["va"]

    def project(i, carry):
        rows = pl.ds(pl.multiple_of(i * 256, 256), 256)
        acc = dot(xbuf[rows], v["wj"][...]) + dot_o(v["low_q"][:, rows], pick(pk, "joined_out")) + bias[:, :768]
        b = acc.astype(BF16).astype(F32)
        position = (i * 256 + row).astype(F32) * 0.125
        ones = jnp.where(lane < 67, 1.0, 0.0)
        for h in range(4):
            slope = jnp.exp2((own * 4 + h + 1).astype(F32) * (-8.0 / HEADS) + jnp.zeros((1, 128), F32))
            high, middle, lowest = cast_parts(position * slope)
            tail = jnp.where(lane == 64, high, jnp.where(lane == 65, middle, jnp.where(lane == 66, lowest, jnp.where(
                lane < 70, 1.0, 0.0))))
            at = h * 192
            qa[h, rows] = jnp.where(lane < 64, b[:, at:at + 128] * 0.125, ones).astype(BF16)
            ka[h, rows] = jnp.where(lane < 64, b[:, at + 64:at + 192], tail).astype(BF16)
            value = jnp.concatenate([b[:, at + 128:at + 192], b[:, at:at + 64]], axis=1)
            va[h, rows] = jnp.where(lane < 64, value, ones).astype(BF16)
        return carry

    lax.fori_loop(0, 4, project, 0)
    own_cols = pl.ds(pl.multiple_of(own * 256, 256), 256)
    keep = lambda n, ref: pltpu.make_async_copy(ref.at[:, own_cols], v["cols"].at[n], copy_sem.at[n])
    keep(0, xbuf).start()
    dense.step(0)
    dense.step(1)

    hooks = [lambda: g2.near(0), lambda: down.step(0), lambda: g2.near(3), lambda: down.step(1), lambda: g2.near(1),
             lambda: (dense.step(2), dense.step(3)), lambda: g2.near(2), lambda: (dense.step(4), dense.step(5)),
             lambda: down.step(2), lambda: (g2.far(0), g2.far(3)), lambda: down.step(3), lambda: (g2.far(1), g2.far(2)),
             lambda: down.step(4), lambda: None, lambda: down.step(5), lambda: up.start()]
    mask = lax.broadcasted_iota(jnp.int32, (256, 256), 0) <= lax.broadcasted_iota(jnp.int32, (256, 256), 1)
    line = lax.broadcasted_iota(jnp.int32, (128, 256), 0)
    c4 = v["c4"]

    def head(h, carry):
        for i in range(4):
            rows = pl.ds(i * 256, 256)
            q = qa[h, rows]
            last = jnp.where(mask, dot_t(ka[h, rows], q), MASKED)
            top = jnp.max(last, axis=0, keepdims=True)
            if i:
                before = dot_t(ka[h, pl.ds(0, i * 256)], q)
                top = jnp.maximum(top, jnp.max(before, axis=0, keepdims=True))
            mix = dot_o(va[h, rows], jnp.exp(last - top).astype(BF16))
            if i:
                mix = mix + dot_o(va[h, pl.ds(0, i * 256)], jnp.exp(before - top).astype(BF16))
            total = mix[64:65]
            high, middle, lowest = cast_parts(-(top + jnp.log(total)))
            mix = jnp.where(line == 67, high, jnp.where(line == 68, middle, jnp.where(
                line == 69, lowest, mix / total)))
            turned = mix.T
            c4[h, rows] = turned.astype(BF16)
            qa[h, rows] = jnp.where(lane < 67, q.astype(F32), jnp.where(lane < 70, turned, 0.0)).astype(BF16)
            for k in range(4):
                @pl.when(h == k)
                def _(k=k, i=i):
                    hooks[k * 4 + i]()
        return carry

    lax.fori_loop(0, 4, head, 0)
    ctx = v["ctx"]
    for h in (0, 2):
        ctx[:, h * 64:h * 64 + 128] = jnp.concatenate([c4[h, :, :64], c4[h + 1, :, :64]], axis=1)

    src, got = v["low_src"], v["low_got"]
    src[0] = dot_t(pick(pk, "dense_in"), ctx[...]).astype(BF16)
    sum_d = LowSum(src.at[0], got.at[0], *sems(2))
    sum_d.start()
    s1 = GroupSum(*[v[n] for n in ("parts", "near", "sent", "half", "full")], *sems(2))
    dense.wait()
    keep(0, xbuf).wait()
    g1.finish()

    def dense_part(i):
        put_pair(s1.parts, s1.order[i], dot(take_pair(ctx, s1.order[i]), v["wd"][...]).astype(BF16))
        s1.give(i)

    dense_part(0)
    dense_part(1)
    s1.far()
    up.step(0)
    up.step(1)
    dense_part(2)
    s1.near_up()
    dense_part(3)
    s1.near_down()
    up.step(2)
    up.step(3)
    for kind in (2, 5, 6, 7):
        g2.shared(kind)
    keep(3, gbuf).start()
    s1.pass_on()
    mid, dmid, dact = v["mid"], v["dmid"], v["dact"]
    total_d = sum_d.total()
    mid[...] = dot_o(total_d, pick(pk, "dense_out")) + bias_d[...] + xs[...].astype(F32)
    low_g.wait()
    down.wait()

    def grad_act(rows):
        dact[rows] = dot_t(gbuf[rows], v["wn"][...]) + dot_o(v["low_g"][:, rows], pick(pk, "down_in"))

    tiles(2, 256, grad_act)
    up.step(4)
    up.step(5)
    tiles(2, 256, lambda rows: grad_act(pl.ds(pl.multiple_of(rows.start + 512, 256), 256)))
    s1.arrive()
    g3 = GroupGather(xbuf, *sems(2))
    for j in ORDER:
        rows = slice(j * 32, (j + 1) * 32)
        mid[rows] = mid[rows] + s1.total(rows)
        xbuf[pl.ds(pl.multiple_of(own * 128 + j * 32, 32), 32)] = layer_norm(mid[rows], gain2[...], shift2[...]).astype(BF16)
        g3.put(j)
    low_u = LowGather(v["low_u"], *sems(2))
    low_u.start(dot_t(pick(pk, "up_in"), xbuf[mine_rows]).astype(BF16))
    all_d = LowGather(v["sum_d"], *sems(2))
    all_d.start(total_d)
    up.wait()
    low_u.wait()
    act, dpre = v["act"], v["dpre"]

    def forward(at):
        x = take_pair(xbuf, at)
        lu = jnp.concatenate([v["low_u"][:, rows] for rows in row_pair(at)], axis=1)

        def run(n, carry):
            cols = pl.ds(pl.multiple_of(n * 256, 256), 256)
            w = pk[:, pl.ds(pl.multiple_of(PICKS["up_out"][0] + n * 256, 128), 256)]
            b = bias[:, pl.ds(pl.multiple_of(1024 + n * 256, 256), 256)]
            pre = dot(x, v["wu"][:, cols]) + dot_o(lu, w) + b
            cdf = 0.5 * (1.0 + lax.erf(pre * ROOT_HALF))
            put_pair(act, at, (pre * cdf).astype(BF16), cols)
            slope = cdf + pre * (jnp.exp(-0.5 * pre * pre) * ROOT_TAU)
            put_pair(dpre, at, (take_pair(dact, at, cols) * slope).astype(BF16), cols)
            return carry

        lax.fori_loop(0, 4, run, 0)

    def by_pairs(g, work):
        g.shared(2)
        work(z)
        for j in ORDER:
            g.near(j)
        g.shared(5)
        work(lax.rem(z + 3, 4))
        g.shared(6)
        work(lax.rem(z + 1, 4))
        for j in ORDER:
            g.far(j)
        g.shared(7)
        work(lax.rem(z + 2, 4))

    by_pairs(g3, forward)
    keep(2, xbuf).start()

    src[1] = dot_t(pick(pk, "up_out"), dpre[...]).astype(BF16)
    sum_u = LowSum(src.at[1], got.at[1], *sems(2))
    sum_u.start()
    s2 = GroupSum(*[v[n] for n in ("parts", "near", "sent", "half", "full")], *sems(2))
    s1.finish()

    def wide_part(s, ref, weight):
        def part(i):
            x = take_pair(ref, s.order[i])

            def run(n, carry):
                cols = pl.ds(pl.multiple_of(n * 512, 512), 512)
                put_pair(s.parts, s.order[i], dot_t(x, weight[cols]).astype(BF16), cols)
                return carry

            lax.fori_loop(0, 4, run, 0)
            s.give(i)

        part(0)
        part(1)
        s.far()
        part(2)
        s.near_up()
        part(3)
        s.near_down()
        s.pass_on()

    keep(2, xbuf).wait()
    g3.finish()
    wide_part(s2, dpre, v["wu"])
    total_u = sum_u.total()
    keep(3, gbuf).wait()
    g2.finish()
    mlp = gbuf

    def forward_down(rows):
        mlp[rows] = dot(act[rows], v["wn"][...]).astype(BF16)

    tiles(4, 256, forward_down)
    src[2] = dot_t(pick(pk, "down_in"), act[...]).astype(BF16)
    dmid[...] = dot_o(total_u, pick(pk, "up_in"))
    s2.arrive()
    g4 = GroupGather(xbuf, *sems(2))
    for j in ORDER:
        rows = slice(j * 32, (j + 1) * 32)
        dmid[rows] = v["gos"][rows].astype(F32) + norm_back(mid[rows], gain2[...], dmid[rows] + s2.total(rows))
        xbuf[pl.ds(pl.multiple_of(own * 128 + j * 32, 32), 32)] = dmid[rows].astype(BF16)
        g4.put(j)
    low_d = LowGather(v["low_d"], *sems(2))
    low_d.start(dot_t(pick(pk, "dense_out"), xbuf[mine_rows]).astype(BF16))
    all_u = LowGather(v["sum_u"], *sems(2))
    all_u.start(total_u)
    sum_n = LowSum(src.at[2], got.at[2], *sems(2))
    sum_n.start()
    low_d.wait()
    dctx = v["dctx"]

    def context(at):
        ld = jnp.concatenate([v["low_d"][:, rows] for rows in row_pair(at)], axis=1)
        value = dot_t(take_pair(xbuf, at), v["wd"][...]) + dot_o(ld, pick(pk, "dense_in"))
        put_pair(dctx, at, value.astype(BF16))

    by_pairs(g4, context)
    keep(1, xbuf).start()

    s3 = GroupSum(mlp, *[v[n] for n in ("near2", "sent2", "half2", "full2")], *sems(2))
    for i in range(4):
        s3.give(i)
    wide_lane = lax.broadcasted_iota(jnp.int32, (1024, 128), 1)
    grads = c4
    for h in range(4):
        first = h // 2 * 128
        g = dctx[:, first:first + 128].astype(F32)
        f = ctx[:, first:first + 128].astype(F32)
        here = (wide_lane // 64) == h % 2
        high, middle, lowest = cast_parts(-jnp.sum(jnp.where(here, g * f, 0.0), axis=-1, keepdims=True))
        if h % 2:
            g = jnp.concatenate([g[:, 64:], g[:, :64]], axis=1)
        grads[h] = jnp.where(wide_lane < 64, g, jnp.where(wide_lane == 64, high, jnp.where(
            wide_lane == 65, middle, jnp.where(wide_lane == 66, lowest, 0.0)))).astype(BF16)
    all_n = LowGather(v["sum_n"], *sems(2))

    def low_step():
        all_n.start(sum_n.total())

    hooks_back = {0: s3.far, 1: s3.near_up, 2: s3.near_down, 5: low_step, 6: s3.pass_on}
    dk, dv = v["dk"], v["dv"]

    def head_back(h, carry):
        dk[...] = jnp.zeros_like(dk)
        dv[...] = jnp.zeros_like(dv)
        for i in range(4):
            rows = pl.ds(i * 256, 256)
            q, g = qa[h, rows], grads[h, rows]

            def span(keys, masked):
                k = ka[h, keys]
                score = dot_t(k, q)
                if masked:
                    score = jnp.where(mask, score, MASKED)
                p = jnp.exp(score)
                ds = (p * dot_t(va[h, keys], g)).astype(BF16)
                dk[keys] += dot(ds, q)
                dv[keys] += dot(p.astype(BF16), g)
                return dot_o(k, ds)

            dq = span(rows, True)
            if i:
                dq = dq + span(pl.ds(0, i * 256), False)
            grads[h, rows] = (dq * 0.125).T.astype(BF16)
            for n, hook in hooks_back.items():
                if n % 4 == i:
                    @pl.when(h == n // 4)
                    def _(hook=hook):
                        hook()
        ka[h] = dk[...].astype(BF16)
        va[h] = dv[...].astype(BF16)
        return carry

    lax.fori_loop(0, 4, head_back, 0)
    dfused = v["dfused"]
    for h in (0, 2):
        dfused[:, h * 192:h * 192 + 384] = jnp.concatenate(
            [ref[k, :, :64] for k in (h, h + 1) for ref in (grads, ka, va)], axis=1)

    src[3] = dot_t(pick(pk, "joined_out"), dfused[...]).astype(BF16)
    sum_q = LowSum(src.at[3], got.at[3], *sems(2))
    sum_q.start()
    s4 = GroupSum(*[v[n] for n in ("parts", "near", "sent", "half", "full")], *sems(2))
    s2.finish()
    wide_part(s4, dfused, v["wj"])
    total_q = sum_q.total()
    all_q = LowGather(v["sum_q"], *sems(2))
    all_q.start(total_q)
    sw2_sems = sems(3)
    layer, mine_grad = v["layer"], v["gos"]
    pairs = [(sub(mine_grad, j), sub(back, j), sub(back, j)) for j in range(4)] + [(layer, out, out)]
    sw2 = Swap(pairs, *sw2_sems)
    s3.arrive()
    all_n.wait()
    layer[...] = (mid[...] + bias_n[...] + dot_o(v["sum_n"][:, mine_rows], pick(pk, "down_out")) + s3.total()).astype(BF16)
    sw2.start(4)

    spread = Spread(split, whole, *rest)

    def product(first, count, low, ref):
        for n in range(0, count, 2):
            spread.put(first + n, dot(low[...], ref[:, n * 128:n * 128 + 256]))

    all_d.wait()
    all_u.wait()
    keep(1, xbuf).wait()
    spread.mark(pk[:8, PICKS["hot"][0]:PICKS["hot"][0] + 128])
    product(0, 6, v["low_q"], dfused)
    product(6, 2, v["low_d"], ctx)
    product(8, 8, v["low_u"], dpre)
    product(16, 8, v["low_g"], act)
    product(26, 2, v["sum_d"], v["cols"].at[1])
    product(28, 2, v["sum_u"], v["cols"].at[2])
    product(30, 2, v["sum_n"], v["cols"].at[3])
    all_q.wait()
    product(24, 2, v["sum_q"], v["cols"].at[0])
    spread.start()
    correction = dot_o(total_q, pick(pk, "joined_in"))
    spread.add()
    spread.deal()
    s4.arrive()
    for j in ORDER:
        rows = slice(j * 32, (j + 1) * 32)
        value = dmid[rows] + norm_back(xs[rows].astype(F32), gain1[...], correction[rows] + s4.total(rows))
        mine_grad[rows] = value.astype(BF16)
        sw2.start(j)
    spread.deal_plane()
    for n in range(5):
        sw2.wait(n)
    spread.share()
    spread.finish()
    for thing in (g4, joined, dense, down, up, s3, s4, sw, sw2):
        thing.finish()


SCRATCH = dict(
    lines=((8, 2048), F32), bias=((1, 2048), F32), mine=((16, PICKED), BF16), pk=((16, PICKED), BF16),
    xs=((128, 2048), BF16), xbuf=((1024, 2048), BF16), gbuf=((1024, 2048), BF16), gos=((128, 2048), BF16),
    wj=((2048, 768), BF16), wd=((256, 2048), BF16), wn=((1024, 2048), BF16), wu=((2048, 1024), BF16),
    qa=((4, 1024, 128), BF16), ka=((4, 1024, 128), BF16), va=((4, 1024, 128), BF16), c4=((4, 1024, 128), BF16),
    ctx=((1024, 256), BF16), dctx=((1024, 256), BF16), dfused=((1024, 768), BF16), act=((1024, 1024), BF16),
    dpre=((1024, 1024), BF16), dact=((1024, 1024), F32), mid=((128, 2048), F32), dmid=((128, 2048), F32),
    layer=((128, 2048), BF16), cols=((4, 1024, 256), BF16),
    dk=((1024, 128), F32), dv=((1024, 128), F32), low_src=((4, 16, 1024), BF16), low_got=((4, 8, 16, 128), BF16),
    low_q=((16, 1024), BF16), low_g=((16, 1024), BF16), low_u=((16, 1024), BF16), low_d=((16, 1024), BF16),
    sum_d=((16, 1024), BF16), sum_u=((16, 1024), BF16), sum_n=((16, 1024), BF16), sum_q=((16, 1024), BF16),
    parts=((1024, 2048), BF16), near=((4, 128, 2048), BF16), sent=((3, 128, 2048), BF16), half=((2, 64, 2048), BF16),
    full=((2, 128, 2048), BF16), near2=((4, 128, 2048), BF16), sent2=((3, 128, 2048), BF16),
    half2=((2, 64, 2048), BF16), full2=((2, 128, 2048), BF16))


def block_call(*args):
    outs = [shape(128, 2048), shape(128, 2048), shape(16, 8, 3, 8, 128), shape(8, 16, 8, 8, 128)]
    low = [DMA((8,)), DMA((8,))]
    sums = [DMA((10,)), DMA((10,))]
    gather = GroupGather.SEMS
    kinds = [DMA((8,)), DMA((8,)), DMA((4,)), *Swap.sems(12), *PlaneGather.SEMS * 4, *gather, *low, *gather, *low, *low, *sums,
             *gather, *low, *low, *low, *sums, *gather, *low, *low, *low, *sums, *low, *low, *sums, *low, *Swap.sems(5),
             *Spread.SCRATCH]
    return pl.pallas_call(
        block_kernel, out_shape=outs, in_specs=specs(pltpu.SMEM, *[ANY] * 22), out_specs=specs(*[ANY] * 4),
        scratch_shapes=[VMEM(*s) for s in SCRATCH.values()] + kinds,
        compiler_params=params(1, 60), name="block")(*args)


WIDE = ((6, 0), (2, 6), (8, 8), (8, 16))


def write_kernel(split, whole, back, layer, *outs):
    for ref, (count, first) in zip(outs[:4], WIDE):
        for n in range(count):
            for half in (0, 1):
                k = 2 * (first + n) + half
                ref[0, half * 8:half * 8 + 8, n * 128:n * 128 + 128] = split[k // 3, 0, k % 3].astype(F32)
    for i, ref in enumerate(outs[4:8]):
        for t in range(8):
            for n in range(2):
                for half in (0, 1):
                    at = t * 256 + n * 128
                    ref[0, half * 8:half * 8 + 8, at:at + 128] = whole[t, i * 4 + n * 2 + half, 0].astype(F32)
    outs[8][...] = back[...].astype(F32)
    outs[9][...] = layer[...]


def write_call(split, whole, back, layer):
    widths = [count * 128 for count, _ in WIDE] + [2048] * 4
    rows = pl.BlockSpec((16, 2048), lambda b: (b, 0))
    return pl.pallas_call(
        write_kernel, grid=(8,),
        out_shape=[shape(8, 16, n, dtype=F32) for n in widths] + [shape(128, 2048, dtype=F32), shape(128, 2048)],
        in_specs=[pl.BlockSpec((16, 1, 3, 8, 128), lambda b: (0, b, 0, 0, 0)),
                  pl.BlockSpec((8, 16, 1, 8, 128), lambda b: (0, 0, b, 0, 0)), rows, rows],
        out_specs=[pl.BlockSpec((1, 16, n), lambda b: (b, 0, 0)) for n in widths] + [rows, rows],
        compiler_params=plain(16), name="write")(split, whole, back, layer)


def local(tokens, grad_out, adapter_ids, first_gain, first_shift, joined_weight, joined_bias, dense_weight,
          dense_bias, second_gain, second_shift, up_weight, up_bias, down_weight, down_bias, joined_adapt_in,
          joined_adapt_out, dense_adapt_in, dense_adapt_out, up_adapt_in, up_adapt_out, down_adapt_in,
          down_adapt_out):
    turn = lambda a: jnp.swapaxes(a, 1, 2)
    flat = lambda a: a.reshape(128, a.shape[2])
    vectors = [a.reshape(1, -1) for a in (first_gain, first_shift, second_gain, second_shift, dense_bias, down_bias,
                                          jnp.pad(joined_bias, (0, 256)), up_bias)]
    adapters = dict(joined_in=turn(joined_adapt_in), joined_out=joined_adapt_out, dense_in=turn(dense_adapt_in),
                    dense_out=dense_adapt_out, up_in=turn(up_adapt_in), up_out=up_adapt_out,
                    down_in=turn(down_adapt_in), down_out=down_adapt_out)
    back, layer, split, whole = block_call(
        adapter_ids, tokens, grad_out, *vectors, *[flat(adapters[n]) for n in SETS], joined_weight, dense_weight,
        down_weight, up_weight)
    joined_out, dense_in, up_out, down_in, joined_in, dense_out, up_in, down_out, grad_tokens, layer_out = write_call(
        split, whole, back, layer)
    return (layer_out, grad_tokens, turn(joined_in), joined_out, turn(dense_in), dense_out, turn(up_in), up_out,
            turn(down_in), down_out)


def solution(mesh):
    fine = Mesh(mesh.devices.reshape(2, 4, 2, 2, 4), AXES)
    rows, cols = P(FSDP, TP), P(TP, FSDP)
    tok = P((*FSDP, *TP), None)
    last, middle, one = P(None, None, TP), P(None, TP, None), P(TP)
    return jax.shard_map(
        local, mesh=fine,
        in_specs=(tok, tok, P(FSDP), P(), P(), rows, one, cols, P(), P(), P(), rows, one, cols, P(), P(), last,
                  middle, P(), P(), last, middle, P()),
        out_specs=(tok, tok, P(), last, middle, P(), P(), last, middle, P()), check_vma=False)
```

```python
import functools

import jax
import jax.numpy as jnp
from jax import lax
from jax.experimental import pallas as pl
from jax.experimental.pallas import tpu as pltpu
from jax.sharding import Mesh
from jax.sharding import PartitionSpec as P

HEADS = 32
EPSILON = 1e-05
MASKED = -1e30
AXES = ("xl", "y", "c", "xh", "z")
FSDP = ("xl", "y", "c")
TP = ("xh", "z")
PLANE = ("xl", "y", "xh")
MESH_ID = pl.DeviceIdType.MESH
ANY = pl.ANY
VMEM = pltpu.VMEM
DMA = pltpu.SemaphoreType.DMA
F32 = jnp.float32
BF16 = jnp.bfloat16
ORDER = (0, 3, 1, 2)
PICKS = dict(joined_in=(0, 2048), joined_out=(2048, 768), hot=(2816, 128), up_in=(2944, 2048), up_out=(4992, 1024),
             dense_in=(6016, 256), dense_out=(6272, 2048), down_in=(8320, 1024), down_out=(9344, 2048))
PICKED = 11392


def remote(src, dst, sems, index, device):
    send, recv = sems
    return pltpu.make_async_remote_copy(
        src_ref=src, dst_ref=dst, send_sem=send.at[index], recv_sem=recv.at[index],
        device_id=device, device_id_type=MESH_ID)


def places():
    return tuple(lax.axis_index(a) for a in AXES)


def at_home():
    _, _, c, xh, _ = places()
    return 1 - (xh - c) * (xh - c)


def meet(peers):
    barrier = pltpu.get_barrier_semaphore()
    for p in peers:
        pl.semaphore_signal(barrier, inc=1, device_id=p, device_id_type=MESH_ID)
    pl.semaphore_wait(barrier, len(peers))


def group_peer(n):
    _, _, c, _, z = places()
    return {"c": lax.rem(c + n // 4, 2), "z": lax.rem(z + n % 4, 4)}


def group_peers():
    return [group_peer(n) for n in range(1, 8)]


def diagonal():
    _, _, c, xh, _ = places()
    return {"c": 1 - c, "xh": 1 - xh}


def plane_peers():
    xl, y, c, xh, _ = places()
    peers = []
    for d in range(1, 4):
        for core in (0, 1):
            peers.append({"y": lax.rem(y + d, 4), "c": core})
            x = lax.rem(xh * 2 + xl + d, 4)
            peers.append({"xh": x // 2, "xl": lax.rem(x, 2), "c": core})
    return peers


def block(ref, n, size=128):
    return ref.at[pl.ds(pl.multiple_of(n * size, size), size)]


class GroupGather:
    SEMS = [DMA((8, 4)), DMA((8, 4))]

    def __init__(self, dst, send, recv):
        self.dst, self.sems = dst, (send, recv)
        _, _, self.c, _, self.z = places()
        self.up, self.down, self.other = group_peer(1), group_peer(3), group_peer(4)

    def at(self, core, z, j):
        return self.dst.at[pl.ds(pl.multiple_of((core * 4 + z) * 128 + j * 32, 32), 32)]

    def copy(self, z, j, kind, device):
        ref = self.at(self.c, z, j)
        return remote(ref, ref, self.sems, (kind, j), device)

    def put(self, j):
        self.copy(self.z, j, 0, self.up).start()
        self.copy(self.z, j, 1, self.down).start()
        self.copy(self.z, j, 2, self.other).start()

    def near(self, j):
        below, above = lax.rem(self.z + 3, 4), lax.rem(self.z + 1, 4)
        self.copy(below, j, 0, self.up).wait_recv()
        if j < 2:
            self.copy(below, j, 3, self.up).start()
        self.copy(below, j, 5, self.other).start()
        self.copy(above, j, 1, self.down).wait_recv()
        if j >= 2:
            self.copy(above, j, 4, self.down).start()
        self.copy(above, j, 6, self.other).start()

    def far(self, j):
        opposite = lax.rem(self.z + 2, 4)
        self.copy(opposite, j, 3 if j < 2 else 4, self.up).wait_recv()
        self.copy(opposite, j, 7, self.other).start()

    def shared(self, kind):
        for j in ORDER:
            self.copy(self.z, j, kind, self.other).wait_recv()

    def finish(self):
        for j in ORDER:
            for kind in (0, 1, 2, 3 if j < 2 else 4, 5, 6, 7):
                self.copy(self.z, j, kind, self.other).wait_send()


class LowGather:
    SEMS = [DMA((8,)), DMA((8,))]

    def __init__(self, dst, send, recv):
        self.dst, self.sems = dst, (send, recv)
        _, _, c, _, z = places()
        self.own = pl.ds(pl.multiple_of((c * 4 + z) * 128, 128), 128)

    def copies(self):
        ref = self.dst.at[:, self.own]
        return [remote(ref, ref, self.sems, (n,), group_peer(n)) for n in range(1, 8)]

    def start(self, value):
        self.dst[:, self.own] = value
        for copy in self.copies():
            copy.start()

    def wait(self):
        for copy in self.copies():
            copy.wait()


class LowSum:
    SEMS = [DMA((8,)), DMA((8,))]

    def __init__(self, src, got, send, recv):
        self.src, self.got, self.sems = src, got, (send, recv)
        _, _, self.c, _, self.z = places()

    def copies(self):
        out = []
        for n in range(1, 8):
            p = group_peer(n)
            cols = pl.ds(pl.multiple_of((p["c"] * 4 + p["z"]) * 128, 128), 128)
            out.append(remote(self.src.at[:, cols], self.got.at[n], self.sems, (n,), p))
        return out

    def start(self):
        for copy in self.copies():
            copy.start()

    def total(self):
        for copy in self.copies():
            copy.wait()
        own = pl.ds(pl.multiple_of((self.c * 4 + self.z) * 128, 128), 128)
        out = self.src[:, own].astype(F32)
        for n in range(1, 8):
            out = out + self.got[n].astype(F32)
        return out.astype(BF16)


class PlaneGather:
    SEMS = [DMA((1,)), DMA((42,)), DMA((16, 2))]

    def __init__(self, src, dst, by_rows, local_sem, send, recv):
        self.src, self.dst, self.by_rows, self.local_sem, self.sems = src, dst, by_rows, local_sem, (send, recv)
        self.xl, self.y, self.c, self.xh, _ = places()
        self.x = self.xh * 2 + self.xl
        self.home = at_home()

    def whole(self, xl, y, core):
        k = (xl * 4 + y) * 2 + core
        if self.by_rows:
            return block(self.dst, k)
        return self.dst.at[:, pl.ds(pl.multiple_of(k * 128, 128), 128)]

    def half(self, ref, h):
        n = ref.shape[0] // 2
        return ref.at[pl.ds(h * n, n)]

    def copy(self, place, h, n, device, src=None):
        xl, y, core = place
        send, recv = self.sems
        dst = self.half(self.whole(*place), h)
        return pltpu.make_async_remote_copy(
            src_ref=dst if src is None else self.half(src, h), dst_ref=dst, send_sem=send.at[n],
            recv_sem=recv.at[(xl * 4 + y) * 2 + core, h], device_id=device, device_id_type=MESH_ID)

    def arrived(self, place, *halves):
        for h in halves:
            self.copy(place, h, 0, {"c": 1 - self.c}).wait_recv()

    def chip_x(self, d, core):
        x = lax.rem(self.x + d, 4)
        return {"xh": x // 2, "xl": lax.rem(x, 2), "c": core}

    def chip_y(self, d, core):
        return {"y": lax.rem(self.y + d, 4), "c": core}

    def both_ways(self, place, n, chip, core, act, src=None):
        act(self.copy(place, 0, n, chip(1, core), src))
        act(self.copy(place, 1, n + 1, chip(3, core), src))
        act(self.copy(place, 1, n + 2, chip(1, core), src))
        act(self.copy(place, 0, n + 3, chip(3, core), src))

    def first(self, act):
        place = (self.xl, self.y, self.c)

        @pl.when(self.c == 0)
        def _():
            self.both_ways(place, 0, self.chip_x, self.xh, act, self.src)

        @pl.when(self.c == 1)
        def _():
            self.both_ways(place, 0, self.chip_y, self.xh, act, self.src)

        @pl.when(self.home == 0)
        def _():
            for h in (0, 1):
                act(self.copy(place, h, (4, 40)[h], {"c": 1 - self.c}, self.src))

    def local(self):
        return pltpu.make_async_copy(self.src, self.whole(self.xl, self.y, self.c), self.local_sem.at[0])

    def start(self):
        @pl.when(self.home == 1)
        def _():
            self.local().start()

        self.first(lambda copy: copy.start())

    def column(self, e):
        return e, lax.rem(self.x - (2 * self.c + e) + 4, 4)

    def along_y(self, e, act):
        self.both_ways((e, self.y, 0), 5 + 4 * e, self.chip_y, self.c, act)

    def along_x(self, d, act):
        self.both_ways((self.xl, lax.rem(self.y + d, 4), 1), 17 + 4 * d, self.chip_x, self.c, act)

    def pass_x(self, e, act):
        _, d = self.column(e)

        @pl.when(d == 1)
        def _():
            act(self.copy((e, self.y, 0), 0, 13 + e, self.chip_x(1, self.c)))

        @pl.when(d == 3)
        def _():
            act(self.copy((e, self.y, 0), 1, 13 + e, self.chip_x(3, self.c)))

    def pass_y(self, n, act):
        place = (self.xl, lax.rem(self.y + (3, 1)[n], 4), 1)
        act(self.copy(place, n, 15 + n, self.chip_y((1, 3)[n], self.c)))

    def pass_on_y(self, e, n, act):
        place = (e, lax.rem(self.y + (3, 1)[n], 4), 0)
        act(self.copy(place, n, 33 + 2 * e + n, self.chip_y((1, 3)[n], self.c)))

    def pass_on_x(self, e, k, act, wait=False):
        _, d = self.column(e)
        place = (e, lax.rem(self.y + k, 4), 1)
        for n, there in ((0, 1), (1, 3)):
            @pl.when(d == there)
            def _(n=n, there=there):
                if wait:
                    self.arrived(place, n)
                act(self.copy(place, n, (37, 38, 39, 41)[k], self.chip_x(there, self.c)))

    def step(self, n):
        go = lambda copy: copy.start()
        if n == 0:
            @pl.when(self.home == 1)
            def _():
                self.local().wait()
                for core in (0, 1):
                    @pl.when(self.c != core)
                    def _(core=core):
                        self.arrived((self.xl, self.y, core), 0, 1)

                for e in (0, 1):
                    @pl.when(self.xl == e)
                    def _(e=e):
                        self.along_y(e, go)

                self.along_x(0, go)
        elif n == 1:
            for e in (0, 1):
                _, d = self.column(e)
                for there in (1, 3):
                    @pl.when(d == there)
                    def _(e=e, there=there):
                        self.arrived((e, self.y, 0), there // 2)

                self.pass_x(e, go)

            @pl.when(self.home == 1)
            def _():
                for k in (0, 1):
                    self.arrived((self.xl, lax.rem(self.y + (3, 1)[k], 4), 1), k)
                    self.pass_y(k, go)
        elif n == 2:
            for e in (0, 1):
                _, d = self.column(e)
                for there in (1, 3):
                    @pl.when(d == there)
                    def _(e=e, there=there):
                        self.arrived((e, self.y, 0), 1 - there // 2)
                        self.along_y(e, go)

            @pl.when(self.home == 1)
            def _():
                for k in (0, 1):
                    self.arrived((self.xl, lax.rem(self.y + (3, 1)[k], 4), 1), 1 - k)
                    self.along_x((3, 1)[k], go)
        elif n == 3:
            for e in (0, 1):
                _, d = self.column(e)

                @pl.when(d == 2)
                def _(e=e):
                    self.arrived((e, self.y, 0), 0, 1)
                    self.along_y(e, go)

            @pl.when(self.home == 1)
            def _():
                self.arrived((self.xl, lax.rem(self.y + 2, 4), 1), 0, 1)
                self.along_x(2, go)
        elif n == 4:
            for e in (0, 1):
                for k in (0, 1):
                    self.arrived((e, lax.rem(self.y + (3, 1)[k], 4), 0), k)
                    self.pass_on_y(e, k, go)
        else:
            for k in (0, 3, 1, 2)[(n - 5) * 2:(n - 5) * 2 + 2]:
                for e in (0, 1):
                    self.pass_on_x(e, k, go, True)

    STEPS = 7

    def wait(self):
        for e in (0, 1):
            for k in (0, 1):
                self.arrived((e, lax.rem(self.y + (3, 1)[k], 4), 0), 1 - k)
            self.arrived((e, lax.rem(self.y + 2, 4), 0), 0, 1)
            _, d = self.column(e)
            for there, halves in ((1, (1,)), (3, (0,)), (2, (0, 1))):
                @pl.when(d == there)
                def _(e=e, halves=halves):
                    for k in range(4):
                        self.arrived((e, k, 1), *halves)

    def finish(self):
        end = lambda copy: copy.wait_send()
        self.first(end)
        for e in (0, 1):
            _, d = self.column(e)
            self.along_y(e, end)
            self.pass_x(e, end)
            for k in (0, 1):
                self.pass_on_y(e, k, end)
            for k in range(4):
                self.pass_on_x(e, k, end)

        @pl.when(self.home == 1)
        def _():
            for k in (0, 1):
                self.pass_y(k, end)
            for k in range(4):
                self.along_x(k, end)


class GroupSum:
    NAMES = ("far_up", "far_down", "up_high", "down_low", "up_low", "down_high")
    SCRATCH = [VMEM((1024, 2048), BF16), VMEM((4, 128, 2048), BF16), VMEM((3, 128, 2048), BF16),
               VMEM((2, 64, 2048), BF16), VMEM((2, 128, 2048), BF16), DMA((10,)), DMA((10,))]

    def __init__(self, parts, near, sent, half, full, send, recv):
        self.parts, self.near, self.sent, self.half, self.full, self.sems = parts, near, sent, half, full, (send, recv)
        _, _, self.c, _, self.z = places()
        self.up, self.down, self.other = group_peer(1), group_peer(3), group_peer(4)
        self.order = [lax.rem(self.z + d, 4) for d in (2, 1, 3, 0)]

    def part(self, core, i):
        return block(self.parts, core * 4 + self.order[i])

    def given(self, i):
        return remote(self.part(1 - self.c, i), self.near.at[i], self.sems, (i,), self.other)

    def give(self, i):
        self.given(i).start()

    def pair(self, i, rows=slice(None)):
        return self.part(self.c, i)[rows].astype(F32) + self.near[i, rows].astype(F32)

    def piece(self, name):
        low, high = pl.ds(0, 64), pl.ds(64, 64)
        n = self.NAMES.index(name)
        src = (self.sent.at[0, low], self.sent.at[0, high], self.sent.at[1, high], self.sent.at[2, low],
               self.sent.at[1, low], self.sent.at[2, high])[n]
        dst = (self.half.at[0], self.half.at[1], self.full.at[0, high], self.full.at[1, low],
               self.full.at[0, low], self.full.at[1, high])[n]
        return remote(src, dst, self.sems, (4 + n,), (self.up, self.down)[n % 2])

    def far(self):
        self.given(0).wait_recv()
        self.sent[0] = self.pair(0).astype(BF16)
        self.piece("far_up").start()
        self.piece("far_down").start()

    def near_up(self):
        self.given(1).wait_recv()
        self.sent[1, pl.ds(64, 64)] = self.pair(1, pl.ds(64, 64)).astype(BF16)
        self.piece("up_high").start()

    def near_down(self):
        self.given(2).wait_recv()
        self.sent[2, pl.ds(0, 64)] = self.pair(2, pl.ds(0, 64)).astype(BF16)
        self.piece("down_low").start()

    def pass_on(self):
        low, high = pl.ds(0, 64), pl.ds(64, 64)
        self.piece("far_up").wait_recv()
        self.sent[1, low] = (self.pair(1, low) + self.half[0].astype(F32)).astype(BF16)
        self.piece("up_low").start()
        self.piece("far_down").wait_recv()
        self.sent[2, high] = (self.pair(2, high) + self.half[1].astype(F32)).astype(BF16)
        self.piece("down_high").start()

    def arrive(self):
        self.given(3).wait_recv()
        for name in ("up_high", "down_low", "up_low", "down_high"):
            self.piece(name).wait_recv()

    def total(self, rows=slice(None)):
        return self.pair(3, rows) + self.full[0, rows].astype(F32) + self.full[1, rows].astype(F32)

    def finish(self):
        for name in self.NAMES:
            self.piece(name).wait_send()
        for i in range(4):
            self.given(i).wait_send()


def params(cid, mib):
    return pltpu.CompilerParams(collective_id=cid, has_side_effects=True, vmem_limit_bytes=mib << 20)


def plain(mib):
    return pltpu.CompilerParams(vmem_limit_bytes=mib << 20)


def shape(*dims, dtype=BF16):
    return jax.ShapeDtypeStruct(dims, dtype)


def specs(*spaces):
    return [pl.BlockSpec(memory_space=s) for s in spaces]


def layer_norm(rows_in, gain, shift):
    row_mean = jnp.mean(rows_in, axis=-1, keepdims=True)
    centered = rows_in - row_mean
    variance = jnp.mean(centered * centered, axis=-1, keepdims=True)
    return centered * lax.rsqrt(variance + EPSILON) * gain + shift


def norm_back(rows_in, gain, grad):
    row_mean = jnp.mean(rows_in, axis=-1, keepdims=True)
    centered = rows_in - row_mean
    inverse = lax.rsqrt(jnp.mean(centered * centered, axis=-1, keepdims=True) + EPSILON)
    n = centered * inverse
    e = gain * grad
    return (e - jnp.mean(e, axis=-1, keepdims=True) - n * jnp.mean(e * n, axis=-1, keepdims=True)) * inverse


def dot(a, b, dims=((1,), (0,))):
    return lax.dot_general(a, b, (dims, ((), ())), preferred_element_type=F32)


def dot_t(a, b):
    return dot(a, b, ((1,), (1,)))


def dot_o(a, b):
    return dot(a, b, ((0,), (0,)))


def tiles(count, size, body):
    def run(i, carry):
        body(pl.ds(pl.multiple_of(i * size, size), size))
        return carry

    lax.fori_loop(0, count, run, 0)


def split_refs(refs, *counts):
    refs, out = list(refs), []
    for n in counts:
        out.append(refs[:n])
        refs = refs[n:]
    return (*out, refs)


def pick(ref, name):
    first, n = PICKS[name]
    return ref[:, pl.ds(first, n)]


def row_pair(z):
    return (pl.ds(pl.multiple_of(z * 128, 128), 128), pl.ds(pl.multiple_of(512 + z * 128, 128), 128))


def take_pair(ref, z, cols=slice(None)):
    a, b = row_pair(z)
    return jnp.concatenate([ref[a, cols], ref[b, cols]], axis=0)


def put_pair(ref, z, value, cols=slice(None)):
    a, b = row_pair(z)
    ref[a, cols] = value[:128]
    ref[b, cols] = value[128:]


class Swap:
    def __init__(self, pairs, local, send, recv):
        self.pairs, self.local, self.sems, self.home = pairs, local, (send, recv), at_home()

    def near_copy(self, n):
        src, _, dst = self.pairs[n]
        return pltpu.make_async_copy(src, dst, self.local.at[n])

    def far_copy(self, n):
        src, dst, _ = self.pairs[n]
        return remote(src, dst, self.sems, (n,), diagonal())

    def start(self, n):
        @pl.when(self.home == 1)
        def _():
            self.near_copy(n).start()

        @pl.when(self.home == 0)
        def _():
            self.far_copy(n).start()

    def wait(self, n):
        @pl.when(self.home == 1)
        def _():
            self.near_copy(n).wait()

        @pl.when(self.home == 0)
        def _():
            self.far_copy(n).wait_recv()

    def finish(self):
        @pl.when(self.home == 0)
        def _():
            for n in range(len(self.pairs)):
                self.far_copy(n).wait_send()

    @staticmethod
    def sems(n):
        return [DMA((n,)), DMA((n,)), DMA((n,))]


class Spread:
    SCRATCH = [VMEM((16, 5, 8, 128), BF16), VMEM((16, 5, 8, 128), BF16), VMEM((8, 3, 8, 128), BF16),
               VMEM((8, 8, 128), BF16), DMA((16,)), DMA((16,)), DMA((9,)), DMA((16,)), DMA((20,)), DMA((20,)), DMA((2,))]

    def __init__(self, split, whole, send, got, part, full, one_send, one_recv, two_send, two_recv, send3, recv3, local):
        self.split, self.whole, self.send, self.got, self.part, self.full = split, whole, send, got, part, full
        self.one, self.two, self.three, self.local = (one_send, one_recv), (two_send, two_recv), (send3, recv3), local
        self.xl, self.y, self.c, self.xh, self.z = places()
        self.q = (self.xh * 2 + self.xl) * 4 + self.y
        self.home = at_home()

    def put(self, n, value):
        for m in range(4):
            k = 2 * n + m
            where = (k // 3, k % 3) if k < 48 else (k - 48, 3)
            row, col = m % 2 * 8, m // 2 * 128
            self.send[where] = value[row:row + 8, col:col + 128].astype(BF16)

    def mark(self, hot):
        for j in range(16):
            self.send[j, 4] = hot

    def chip(self, n):
        q = lax.rem(self.q + n, 16)
        x = q // 4
        return q, {"xh": x // 2, "xl": lax.rem(x, 2), "y": lax.rem(q, 4)}

    def to_owners(self):
        out = []
        for n in range(1, 16):
            q, device = self.chip(n)
            out.append(remote(self.send.at[q], self.got.at[n], self.one, (n,), device))
        return out

    def start(self):
        for copy in self.to_owners():
            copy.start()

    def add(self):
        self.got[0] = self.send[self.q]
        for copy in self.to_owners():
            copy.wait_recv()
        for b in range(8):
            total = jnp.zeros((4, 8, 128), F32)
            for n in range(16):
                hot = self.got[n, 4].astype(F32)[b:b + 1]
                total = total + self.got[n, 0:4].astype(F32) * hot
            total = total.astype(BF16)
            self.part[b] = total[:3]
            self.full[b] = total[3]

    def copies_to_groups(self, slot):
        out = []
        for e in (0, 1):
            for d in range(4):
                device = {"xh": self.c, "xl": lax.rem(self.xl + e, 2), "y": lax.rem(self.y + d, 4)}
                send, recv = self.two
                out.append(pltpu.make_async_remote_copy(
                    src_ref=self.part, dst_ref=self.split.at[:, slot], send_sem=send.at[e * 4 + d],
                    recv_sem=recv.at[self.q], device_id=device, device_id_type=MESH_ID))
        return out

    def split_copies(self):
        return self.copies_to_groups(self.q)

    def split_own(self):
        return pltpu.make_async_copy(self.part, self.split.at[:, self.q], self.local.at[0])

    def whole_own(self):
        return pltpu.make_async_copy(self.full, self.whole.at[:, self.c * 4 + self.z, self.q], self.local.at[1])

    def line_copies(self):
        where = self.whole.at[:, self.c * 4 + self.z, self.q]
        return [remote(self.full, where, self.three, (d,), {"z": lax.rem(self.z + d, 4)}) for d in (1, 2, 3)]

    def plane_copies(self):
        where = self.whole.at[:, pl.ds(self.c * 4, 4), self.q]
        return [remote(where, where, self.three, (4 + n,), self.chip(n)[1]) for n in range(1, 16)]

    def shared_whole(self):
        where = self.whole.at[:, pl.ds(self.c * 4, 4)]
        return remote(where, where, self.three, (0,), {"c": 1 - self.c})

    def shared_split(self):
        send, recv = self.two
        return pltpu.make_async_remote_copy(
            src_ref=self.split, dst_ref=self.split, send_sem=send.at[8], recv_sem=recv.at[0],
            device_id={"c": 1 - self.c}, device_id_type=MESH_ID)

    def deal_groups(self):
        copies = self.split_copies()

        @pl.when(self.home == 1)
        def _():
            self.split_own().start()

        @pl.when(self.home == 0)
        def _():
            copies[0].start()

        for copy in copies[1:]:
            copy.start()

    def deal(self):
        self.whole_own().start()
        for copy in self.line_copies():
            copy.start()
        self.deal_groups()

    def deal_plane(self):
        self.whole_own().wait()
        for copy in self.line_copies():
            copy.wait_recv()
        for copy in self.plane_copies():
            copy.start()

    def wait_groups(self, count):
        send, recv = self.two
        for q in range(count):
            @pl.when(self.q != q)
            def _(q=q):
                pltpu.make_async_remote_copy(
                    src_ref=self.part, dst_ref=self.split.at[:, q], send_sem=send.at[0], recv_sem=recv.at[q],
                    device_id={"c": 1 - self.c}, device_id_type=MESH_ID).wait_recv()

    def share(self):
        @pl.when(self.home == 1)
        def _():
            self.split_own().wait()
            self.wait_groups(16)
            self.shared_split().start()

        for copy in self.plane_copies():
            copy.wait_recv()
        self.shared_whole().start()

    def finish_shares(self):
        self.shared_whole().wait()

        @pl.when(self.home == 1)
        def _():
            self.shared_split().wait_send()

        @pl.when(self.home == 0)
        def _():
            self.shared_split().wait_recv()

    def finish_groups(self):
        copies = self.split_copies()

        @pl.when(self.home == 0)
        def _():
            copies[0].wait_send()

        for copy in copies[1:]:
            copy.wait_send()

    def finish(self):
        self.finish_shares()
        self.finish_groups()
        for copy in self.line_copies() + self.plane_copies() + self.to_owners():
            copy.wait_send()


class LastSpread(Spread):
    SCRATCH = [VMEM((16, 2, 8, 128), BF16), VMEM((16, 2, 8, 128), BF16), VMEM((8, 8, 128), BF16),
               DMA((16,)), DMA((16,)), DMA((9,)), DMA((16,)), DMA((20,)), DMA((20,)), DMA((2,))]

    def __init__(self, split, whole, send, got, part, *sems):
        super().__init__(split, whole, send, got, part, part, *sems)

    def put(self, n, value):
        for m in range(4):
            row, col = m % 2 * 8, m // 2 * 128
            self.send[2 * n + m, 0] = value[row:row + 8, col:col + 128].astype(BF16)

    def mark(self, hot):
        for j in range(16):
            self.send[j, 1] = hot

    def add(self):
        self.got[0] = self.send[self.q]
        for copy in self.to_owners():
            copy.wait_recv()
        for b in range(8):
            total = jnp.zeros((8, 128), F32)
            for n in range(16):
                total = total + self.got[n, 0].astype(F32) * self.got[n, 1].astype(F32)[b:b + 1]
            self.part[b] = total.astype(BF16)

    def split_copies(self):
        return self.copies_to_groups(lax.rem(self.q, 12))

    def split_own(self):
        return pltpu.make_async_copy(self.part, self.split.at[:, lax.rem(self.q, 12)], self.local.at[0])

    def late(self):
        return lax.rem(self.q, 4)

    def whole_own(self):
        return pltpu.make_async_copy(self.part, self.whole.at[:, self.c * 4 + self.z, self.late()], self.local.at[1])

    def line_copies(self):
        where = self.whole.at[:, self.c * 4 + self.z]
        return [remote(where, where, self.three, (d,), {"z": lax.rem(self.z + d, 4)}) for d in (1, 2, 3)]

    def plane_copies(self):
        where = self.whole.at[:, self.c * 4 + self.z, self.late()]
        return [remote(self.part, where, self.three, (4 + n,), self.chip(n)[1]) for n in range(1, 16)]

    def deal(self):
        @pl.when(self.q >= 12)
        def _():
            self.whole_own().start()
            for copy in self.plane_copies():
                copy.start()

        @pl.when(self.q < 12)
        def _():
            self.deal_groups()

    def share_groups(self):
        @pl.when(self.home == 1)
        def _():
            @pl.when(self.q < 12)
            def _():
                self.split_own().wait()

            self.wait_groups(12)
            self.shared_split().start()

    def line(self):
        @pl.when(self.q >= 12)
        def _():
            self.whole_own().wait()

        for k, copy in enumerate(self.plane_copies()):
            @pl.when(lax.rem(self.q - (k + 1) + 16, 16) >= 12)
            def _(copy=copy):
                copy.wait_recv()

        for copy in self.line_copies():
            copy.start()

    def share_line(self):
        for copy in self.line_copies():
            copy.wait_recv()
        self.shared_whole().start()

    def finish(self):
        self.finish_shares()

        @pl.when(self.q < 12)
        def _():
            self.finish_groups()

        @pl.when(self.q >= 12)
        def _():
            for copy in self.plane_copies():
                copy.wait_send()

        for copy in self.line_copies() + self.to_owners():
            copy.wait_send()


def far_peers():
    xl, y, _, xh, _ = places()
    peers = []
    for d in range(1, 4):
        x = lax.rem(xh * 2 + xl + d, 4)
        for e in range(1, 4):
            peers.append({"xh": x // 2, "xl": lax.rem(x, 2), "y": lax.rem(y + e, 4)})
    return peers


ROOT_HALF = 0.7071067811865476
ROOT_TAU = 0.3989422804014327
SETS = dict(joined_in=(0, 0), up_in=(128, 0), dense_out=(256, 0), down_out=(384, 0), up_out=(512, 0),
            down_in=(512, 1024), joined_out=(640, 0), dense_in=(640, 768))


def cast_parts(value):
    high = value.astype(BF16).astype(F32)
    middle = (value - high).astype(BF16).astype(F32)
    return high, middle, value - high - middle


def block_kernel(*refs):
    (ids, tokens, go, *vectors), adapters, shards, outs, scratch = split_refs(refs, 11, 8, 4, 6)
    back, out, split, whole, split2, whole2 = outs
    names = list(SCRATCH)
    v = dict(zip(names, scratch))
    rest = list(scratch[len(names):])

    def sems(n):
        taken = rest[:n]
        del rest[:n]
        return taken

    load_sem, vector_sem, copy_sem = sems(3)
    xl, y, c, xh, z = places()
    own = c * 4 + z
    mine_rows = pl.ds(pl.multiple_of(own * 128, 128), 128)
    there_rows = (1 - c) * 4 + z
    gain1, shift1, gain2, shift2, bias_d, bias_n = (v["lines"].at[n:n + 1] for n in range(6))
    pk, xs, xbuf, gbuf = v["pk"], v["xs"], v["xbuf"], v["gbuf"]
    sets = v["parts"]
    loads = {}
    for n, (name, ref) in enumerate(zip(SETS, adapters)):
        row, col = SETS[name]
        loads[name] = pltpu.make_async_copy(ref, sets.at[pl.ds(row, 128), pl.ds(col, ref.shape[1])], load_sem.at[n])
        loads[name].start()
    lines = [pltpu.make_async_copy(ref, v["lines"].at[n:n + 1], vector_sem.at[n]) for n, ref in enumerate(vectors[:6])]
    for line in lines:
        line.start()
    meet(plane_peers() + group_peers() + far_peers())

    bias = v["bias"]
    mine = v["mine"]
    piece = lambda who, j: gbuf.at[pl.ds(pl.multiple_of(who * 128 + j * 32, 32), 32)]
    sub = lambda ref, j: ref.at[pl.ds(j * 32, 32)]
    cut = 2944
    pairs = [(sub(tokens, j), sub(xs, j), sub(xs, j)) for j in range(4)]
    pairs += [(m, p, p) for m, p in ((mine.at[:, :cut], pk.at[:, :cut]), (mine.at[:, cut:], pk.at[:, cut:]),
                                     (vectors[7], v["bias_one"]), (vectors[6], bias))]
    pairs += [(sub(go, j), piece(there_rows, j), piece(own, j)) for j in range(4)]
    sw = Swap(pairs, *sems(3))
    for j in ORDER:
        sw.start(j)
    joined = PlaneGather(shards[0], v["wj"], True, *sems(3))
    dense = PlaneGather(shards[1], v["wd"], False, *sems(3))
    down = PlaneGather(shards[2], v["wn"], False, *sems(3))
    up = PlaneGather(shards[3], v["wu"], True, *sems(3))
    joined.start()
    set_id = ids[0]
    for name, (row, col) in SETS.items():
        first, n = PICKS[name]
        loads[name].wait()
        chosen = sets[row:row + 16, col:col + n]
        for k in range(1, 8):
            chosen = jnp.where(set_id == k, sets[row + k * 16:row + k * 16 + 16, col:col + n], chosen)
        mine[:, first:first + n] = chosen
    first, n = PICKS["hot"]
    mine[:, first:first + n] = jnp.where(lax.broadcasted_iota(jnp.int32, (16, 128), 0) == set_id, 1.0, 0.0).astype(BF16)
    for n in (4, 6, 7):
        sw.start(n)
    for line in lines:
        line.wait()
    g1 = GroupGather(xbuf, *sems(2))
    for j in ORDER:
        sw.wait(j)
        x1 = layer_norm(xs[j * 32:(j + 1) * 32].astype(F32), gain1[...], shift1[...])
        xbuf[pl.ds(pl.multiple_of(own * 128 + j * 32, 32), 32)] = x1.astype(BF16)
        g1.put(j)
    dense.start()
    joined.step(0)
    joined.step(1)
    g1.near(0)
    joined.step(2)
    g1.near(3)
    joined.step(3)
    g1.near(1)
    joined.step(4)
    g1.near(2)
    joined.step(5)
    joined.step(6)
    for j in ORDER:
        sw.start(8 + j)
    dense.step(0)
    dense.step(1)
    down.start()
    sw.wait(4)

    def low_pair(at):
        low = dot_t(pick(pk, "joined_in"), take_pair(xbuf, at)).astype(BF16)
        for n, rows in enumerate(row_pair(at)):
            v["low_q"][:, rows] = low[:, n * 128:n * 128 + 128]

    g1.shared(2)
    low_pair(z)
    for j in ORDER:
        g1.far(j)
    g1.shared(5)
    low_pair(lax.rem(z + 3, 4))
    g1.shared(6)
    low_pair(lax.rem(z + 1, 4))
    sw.start(5)
    g1.shared(7)
    low_pair(lax.rem(z + 2, 4))
    g2 = GroupGather(gbuf, *sems(2))
    for n in (6, 7):
        sw.wait(n)
    joined.wait()

    lane = lax.broadcasted_iota(jnp.int32, (256, 128), 1)
    row = lax.broadcasted_iota(jnp.int32, (256, 128), 0)
    qa, ka, va = v["qa"], v["ka"], v["va"]

    def project(i, carry):
        rows = pl.ds(pl.multiple_of(i * 256, 256), 256)
        acc = dot(xbuf[rows], v["wj"][...]) + dot_o(v["low_q"][:, rows], pick(pk, "joined_out")) + v["bias_one"][...].reshape(1, 768)
        b = acc.astype(BF16).astype(F32)
        position = (i * 256 + row).astype(F32) * 0.125
        ones = jnp.where(lane < 67, 1.0, 0.0)
        for h in range(4):
            slope = jnp.exp2((own * 4 + h + 1).astype(F32) * (-8.0 / HEADS) + jnp.zeros((1, 128), F32))
            high, middle, lowest = cast_parts(position * slope)
            tail = jnp.where(lane == 64, high, jnp.where(lane == 65, middle, jnp.where(lane == 66, lowest, jnp.where(
                lane < 70, 1.0, 0.0))))
            at = h * 192
            qa[h, rows] = jnp.where(lane < 64, b[:, at:at + 128] * 0.125, ones).astype(BF16)
            ka[h, rows] = jnp.where(lane < 64, b[:, at + 64:at + 192], tail).astype(BF16)
            value = jnp.concatenate([b[:, at + 128:at + 192], b[:, at:at + 64]], axis=1)
            va[h, rows] = jnp.where(lane < 64, value, ones).astype(BF16)
        return carry

    lax.fori_loop(0, 4, project, 0)
    own_cols = pl.ds(pl.multiple_of(own * 256, 256), 256)
    keep = lambda n, ref: pltpu.make_async_copy(ref.at[:, own_cols], v["cols"].at[n], copy_sem.at[n])
    keep(0, xbuf).start()
    for j in ORDER:
        sw.wait(8 + j)
        g2.put(j)

    hooks = [lambda: dense.step(2), lambda: down.step(0), lambda: (dense.step(3), down.step(1)), lambda: g2.near(0), lambda: dense.step(4),
             lambda: g2.near(3), lambda: down.step(2), lambda: g2.near(1), lambda: (dense.step(5), dense.step(6)),
             lambda: g2.near(2), lambda: up.start(), lambda: down.step(3), lambda: (g2.far(0), g2.far(3)),
             lambda: None, lambda: (g2.far(1), g2.far(2)), lambda: down.step(4)]
    mask = lax.broadcasted_iota(jnp.int32, (256, 256), 0) <= lax.broadcasted_iota(jnp.int32, (256, 256), 1)
    line = lax.broadcasted_iota(jnp.int32, (128, 256), 0)
    c4 = v["c4"]

    def head(h, carry):
        for i in range(4):
            rows = pl.ds(i * 256, 256)
            q = qa[h, rows]
            last = jnp.where(mask, dot_t(ka[h, rows], q), MASKED)
            top = jnp.max(last, axis=0, keepdims=True)
            if i:
                before = dot_t(ka[h, pl.ds(0, i * 256)], q)
                top = jnp.maximum(top, jnp.max(before, axis=0, keepdims=True))
            mix = dot_o(va[h, rows], jnp.exp(last - top).astype(BF16))
            if i:
                mix = mix + dot_o(va[h, pl.ds(0, i * 256)], jnp.exp(before - top).astype(BF16))
            total = mix[64:65]
            high, middle, lowest = cast_parts(-(top + jnp.log(total)))
            mix = jnp.where(line == 67, high, jnp.where(line == 68, middle, jnp.where(
                line == 69, lowest, mix / total)))
            turned = mix.T
            c4[h, rows] = turned.astype(BF16)
            qa[h, rows] = jnp.where(lane < 67, q.astype(F32), jnp.where(lane < 70, turned, 0.0)).astype(BF16)
            for k in range(4):
                @pl.when(h == k)
                def _(k=k, i=i):
                    hooks[k * 4 + i]()
        return carry

    lax.fori_loop(0, 4, head, 0)
    ctx = v["ctx"]
    for h in (0, 2):
        ctx[:, h * 64:h * 64 + 128] = jnp.concatenate([c4[h, :, :64], c4[h + 1, :, :64]], axis=1)

    sw.wait(5)
    v["gos"][...] = gbuf[mine_rows]

    src, got = v["low_src"], v["low_got"]
    src[0] = dot_t(pick(pk, "dense_in"), ctx[...]).astype(BF16)
    sum_d = LowSum(src.at[0], got.at[0], *sems(2))
    sum_d.start()
    s1 = GroupSum(*[v[n] for n in ("parts", "near", "sent", "half", "full")], *sems(2))
    dense.wait()
    keep(0, xbuf).wait()
    g1.finish()

    def dense_part(i):
        put_pair(s1.parts, s1.order[i], dot(take_pair(ctx, s1.order[i]), v["wd"][...]).astype(BF16))
        s1.give(i)

    dense_part(0)
    dense_part(1)
    s1.far()
    dense_part(2)
    s1.near_up()
    dense_part(3)
    s1.near_down()
    for kind in (2, 5, 6, 7):
        g2.shared(kind)
    keep(3, gbuf).start()

    def low_tile(rows):
        v["low_g"][:, rows] = dot_t(pick(pk, "down_out"), gbuf[rows]).astype(BF16)

    down.step(5)
    up.step(0)
    tiles(4, 256, low_tile)
    down.step(6)
    up.step(1)
    s1.pass_on()
    up.step(2)
    mid, dmid, dact = v["mid"], v["dmid"], v["dact"]
    total_d = sum_d.total()
    mid[...] = dot_o(total_d, pick(pk, "dense_out")) + bias_d[...] + xs[...].astype(F32)
    up.step(3)
    up.step(4)
    s1.arrive()
    g3 = GroupGather(xbuf, *sems(2))
    for j in ORDER:
        rows = slice(j * 32, (j + 1) * 32)
        mid[rows] = mid[rows] + s1.total(rows)
        xbuf[pl.ds(pl.multiple_of(own * 128 + j * 32, 32), 32)] = layer_norm(mid[rows], gain2[...], shift2[...]).astype(BF16)
        g3.put(j)
    all_d = LowGather(v["sum_d"], *sems(2))
    all_d.start(total_d)
    up.step(5)
    down.wait()

    def grad_act(rows):
        dact[rows] = dot_t(gbuf[rows], v["wn"][...]) + dot_o(v["low_g"][:, rows], pick(pk, "down_in"))

    tiles(2, 256, grad_act)
    g3.near(0)
    g3.near(3)
    up.step(6)
    tiles(2, 256, lambda rows: grad_act(pl.ds(pl.multiple_of(rows.start + 512, 256), 256)))
    g3.near(1)
    g3.near(2)
    up.wait()
    act, dpre = v["act"], v["dpre"]

    def forward(at):
        x = take_pair(xbuf, at)
        lu = dot_t(pick(pk, "up_in"), x).astype(BF16)
        for n, rows in enumerate(row_pair(at)):
            v["low_u"][:, rows] = lu[:, n * 128:n * 128 + 128]

        def run(n, carry):
            cols = pl.ds(pl.multiple_of(n * 256, 256), 256)
            w = pk[:, pl.ds(pl.multiple_of(PICKS["up_out"][0] + n * 256, 128), 256)]
            b = bias[:, pl.ds(pl.multiple_of(n * 256, 256), 256)]
            pre = dot(x, v["wu"][:, cols]) + dot_o(lu, w) + b
            cdf = 0.5 * (1.0 + lax.erf(pre * ROOT_HALF))
            put_pair(act, at, (pre * cdf).astype(BF16), cols)
            slope = cdf + pre * (jnp.exp(-0.5 * pre * pre) * ROOT_TAU)
            put_pair(dpre, at, (take_pair(dact, at, cols) * slope).astype(BF16), cols)
            return carry

        lax.fori_loop(0, 4, run, 0)

    def by_pairs(g, work, beside=None):
        g.shared(2)
        work(z)
        if beside:
            beside()
            for j in ORDER:
                g.near(j)
        g.shared(5)
        work(lax.rem(z + 3, 4))
        g.shared(6)
        work(lax.rem(z + 1, 4))
        for j in ORDER:
            g.far(j)
        g.shared(7)
        work(lax.rem(z + 2, 4))

    by_pairs(g3, forward)
    keep(2, xbuf).start()

    src[1] = dot_t(pick(pk, "up_out"), dpre[...]).astype(BF16)
    sum_u = LowSum(src.at[1], got.at[1], *sems(2))
    sum_u.start()
    s2 = GroupSum(*[v[n] for n in ("parts", "near", "sent", "half", "full")], *sems(2))
    s1.finish()

    def wide_part(s, ref, weight, before, beside):
        def part(i):
            x = take_pair(ref, s.order[i])

            def run(n, carry):
                cols = pl.ds(pl.multiple_of(n * 512, 512), 512)
                put_pair(s.parts, s.order[i], dot_t(x, weight[cols]).astype(BF16), cols)
                return carry

            lax.fori_loop(0, 4, run, 0)
            s.give(i)

        part(0)
        part(1)
        before()
        s.far()
        part(2)
        s.near_up()
        part(3)
        s.near_down()
        beside()
        s.pass_on()

    keep(2, xbuf).wait()
    g3.finish()
    wide_part(s2, dpre, v["wu"], lambda: None, lambda: None)
    total_u = sum_u.total()
    keep(3, gbuf).wait()
    g2.finish()
    mlp = gbuf

    def forward_down(rows):
        mlp[rows] = dot(act[rows], v["wn"][...]).astype(BF16)

    tiles(4, 256, forward_down)
    src[2] = dot_t(pick(pk, "down_in"), act[...]).astype(BF16)
    dmid[...] = dot_o(total_u, pick(pk, "up_in"))
    sum_n = LowSum(src.at[2], got.at[2], *sems(2))
    sum_n.start()
    all_u = LowGather(v["sum_u"], *sems(2))
    all_u.start(total_u)
    s2.arrive()
    all_n = LowGather(v["sum_n"], *sems(2))
    all_n.start(sum_n.total())
    g4 = GroupGather(xbuf, *sems(2))
    for j in ORDER:
        rows = slice(j * 32, (j + 1) * 32)
        dmid[rows] = v["gos"][rows].astype(F32) + norm_back(mid[rows], gain2[...], dmid[rows] + s2.total(rows))
        xbuf[pl.ds(pl.multiple_of(own * 128 + j * 32, 32), 32)] = dmid[rows].astype(BF16)
        g4.put(j)
    spread = Spread(split, whole, *sems(11))

    def product(first, count, low, ref):
        for n in range(0, count, 2):
            spread.put(first + n, dot(low[...], ref[:, n * 128:n * 128 + 256]))

    def early_products():
        spread.mark(pk[:8, PICKS["hot"][0]:PICKS["hot"][0] + 128])
        product(2, 8, v["low_u"], dpre)
        product(10, 8, v["low_g"], act)
        all_u.wait()
        product(28, 2, v["sum_u"], v["cols"].at[2])

    grads = c4

    def context(at):
        x = take_pair(xbuf, at)
        ld = dot_t(pick(pk, "dense_out"), x).astype(BF16)
        for n, rows in enumerate(row_pair(at)):
            v["low_d"][:, rows] = ld[:, n * 128:n * 128 + 128]
        value = dot_t(x, v["wd"][...]) + dot_o(ld, pick(pk, "dense_in"))
        value = value.astype(BF16).astype(F32)
        mix = take_pair(ctx, at).astype(F32)
        for h in range(4):
            first = h // 2 * 128
            g = value[:, first:first + 128]
            here = (lane // 64) == h % 2
            d = -jnp.sum(jnp.where(here, g * mix[:, first:first + 128], 0.0), axis=-1, keepdims=True)
            high, middle, lowest = cast_parts(d)
            if h % 2:
                g = jnp.concatenate([g[:, 64:], g[:, :64]], axis=1)
            put_pair(grads.at[h], at, jnp.where(lane < 64, g, jnp.where(lane == 64, high, jnp.where(
                lane == 65, middle, jnp.where(lane == 66, lowest, 0.0)))).astype(BF16))

    by_pairs(g4, context, early_products)
    keep(1, xbuf).start()

    s3 = GroupSum(mlp, *[v[n] for n in ("near2", "sent2", "half2", "full2")], *sems(2))
    for i in range(4):
        s3.give(i)
    product(0, 2, v["low_d"], ctx)
    all_d.wait()
    keep(1, xbuf).wait()
    product(26, 2, v["sum_d"], v["cols"].at[1])
    all_n.wait()
    product(30, 2, v["sum_n"], v["cols"].at[3])
    spread.start()
    hooks_back = {0: s3.far, 1: s3.near_up, 2: s3.near_down, 6: spread.add, 7: spread.deal, 8: s3.pass_on,
                  13: spread.deal_plane}
    dk, dv = v["dact"].at[:, 0:128], v["dact"].at[:, 128:256]

    def head_back(h, carry):
        dk[...] = jnp.zeros_like(dk)
        dv[...] = jnp.zeros_like(dv)
        for i in range(4):
            rows = pl.ds(i * 256, 256)
            q, g = qa[h, rows], grads[h, rows]

            def span(keys, masked):
                k = ka[h, keys]
                score = dot_t(k, q)
                if masked:
                    score = jnp.where(mask, score, MASKED)
                p = jnp.exp(score)
                ds = (p * dot_t(va[h, keys], g)).astype(BF16)
                dk[keys] += dot(ds, q)
                dv[keys] += dot(p.astype(BF16), g)
                return dot_o(k, ds)

            dq = span(rows, True)
            if i:
                dq = dq + span(pl.ds(0, i * 256), False)
            grads[h, rows] = (dq * 0.125).T.astype(BF16)
            for n, hook in hooks_back.items():
                if n % 4 == i:
                    @pl.when(h == n // 4)
                    def _(hook=hook):
                        hook()
        ka[h] = dk[...].astype(BF16)
        va[h] = dv[...].astype(BF16)
        return carry

    lax.fori_loop(0, 4, head_back, 0)
    dfused = v["dfused"]
    for h in (0, 2):
        dfused[:, h * 192:h * 192 + 384] = jnp.concatenate(
            [ref[k, :, :64] for k in (h, h + 1) for ref in (grads, ka, va)], axis=1)

    src[3] = dot_t(pick(pk, "joined_out"), dfused[...]).astype(BF16)
    sum_q = LowSum(src.at[3], got.at[3], *sems(2))
    sum_q.start()
    s4 = GroupSum(*[v[n] for n in ("parts", "near", "sent", "half", "full")], *sems(2))
    s2.finish()
    all_q = LowGather(v["sum_q"], *sems(2))
    total_q = []

    def early_low():
        total_q.append(sum_q.total())
        all_q.start(total_q[0])

    spread2 = LastSpread(split2, whole2, *sems(10))

    def late_products():
        spread2.mark(pk[:8, PICKS["hot"][0]:PICKS["hot"][0] + 128])
        for n in range(0, 6, 2):
            spread2.put(n, dot(v["low_q"][...], dfused[:, n * 128:n * 128 + 256]))

    wide_part(s4, dfused, v["wj"], early_low, late_products)
    all_q.wait()
    spread2.put(6, dot(v["sum_q"][...], v["cols"][0]))
    spread2.start()
    layer, mine_grad = v["layer"], v["gos"]
    pairs = [(sub(mine_grad, j), sub(back, j), sub(back, j)) for j in range(4)] + [(layer, out, out)]
    sw2 = Swap(pairs, *sems(3))
    s3.arrive()
    layer[...] = (mid[...] + bias_n[...] + dot_o(v["sum_n"][:, mine_rows], pick(pk, "down_out")) + s3.total()).astype(BF16)
    sw2.start(4)
    spread.share()
    correction = dot_o(total_q[0], pick(pk, "joined_in"))
    spread2.add()
    spread2.deal()
    s4.arrive()
    for j in ORDER:
        rows = slice(j * 32, (j + 1) * 32)
        value = dmid[rows] + norm_back(xs[rows].astype(F32), gain1[...], correction[rows] + s4.total(rows))
        mine_grad[rows] = value.astype(BF16)
        sw2.start(j)
    spread2.share_groups()
    spread2.line()
    spread.finish()
    spread2.share_line()
    for n in range(5):
        sw2.wait(n)
    spread2.finish()
    for thing in (g4, joined, dense, down, up, s3, s4, sw, sw2):
        thing.finish()


SCRATCH = dict(
    lines=((8, 2048), F32), bias=((1, 1024), F32), bias_one=((768,), F32), mine=((16, PICKED), BF16), pk=((16, PICKED), BF16),
    xs=((128, 2048), BF16), xbuf=((1024, 2048), BF16), gbuf=((1024, 2048), BF16), gos=((128, 2048), BF16),
    wj=((2048, 768), BF16), wd=((256, 2048), BF16), wn=((1024, 2048), BF16), wu=((2048, 1024), BF16),
    qa=((4, 1024, 128), BF16), ka=((4, 1024, 128), BF16), va=((4, 1024, 128), BF16), c4=((4, 1024, 128), BF16),
    ctx=((1024, 256), BF16), dfused=((1024, 768), BF16), act=((1024, 1024), BF16),
    dpre=((1024, 1024), BF16), dact=((1024, 1024), F32), mid=((128, 2048), F32), dmid=((128, 2048), F32),
    layer=((128, 2048), BF16), cols=((4, 1024, 256), BF16),
    low_src=((4, 16, 1024), BF16), low_got=((4, 8, 16, 128), BF16),
    low_q=((16, 1024), BF16), low_g=((16, 1024), BF16), low_u=((16, 1024), BF16), low_d=((16, 1024), BF16),
    sum_d=((16, 1024), BF16), sum_u=((16, 1024), BF16), sum_n=((16, 1024), BF16), sum_q=((16, 1024), BF16),
    parts=((1024, 2048), BF16), near=((4, 128, 2048), BF16), sent=((3, 128, 2048), BF16), half=((2, 64, 2048), BF16),
    full=((2, 128, 2048), BF16), near2=((4, 128, 2048), BF16), sent2=((3, 128, 2048), BF16),
    half2=((2, 64, 2048), BF16), full2=((2, 128, 2048), BF16))


def block_call(*args):
    outs = [shape(128, 2048), shape(128, 2048), shape(8, 16, 3, 8, 128), shape(8, 8, 16, 8, 128),
            shape(8, 12, 8, 128), shape(8, 8, 4, 8, 128)]
    low = [DMA((8,)), DMA((8,))]
    sums = [DMA((10,)), DMA((10,))]
    gather = GroupGather.SEMS
    kinds = [DMA((8,)), DMA((8,)), DMA((4,)), *Swap.sems(12), *PlaneGather.SEMS * 4, *gather, *gather, *low, *sums,
             *gather, *low, *low, *sums, *low, *low, *low, *gather, *Spread.SCRATCH, *sums, *low, *sums, *low,
             *LastSpread.SCRATCH, *Swap.sems(5)]
    return pl.pallas_call(
        block_kernel, out_shape=outs, in_specs=specs(pltpu.SMEM, *[ANY] * 22), out_specs=specs(*[ANY] * 6),
        scratch_shapes=[VMEM(*s) for s in SCRATCH.values()] + kinds,
        compiler_params=params(1, 60), name="block")(*args)


def write_kernel(split, whole, split2, whole2, back, layer, *outs):
    joined_out, dense_in, up_out, down_in, *wholes, grad, out = outs
    for ref, count, first in ((dense_in, 2, 0), (up_out, 8, 2), (down_in, 8, 10)):
        for n in range(count):
            for half in (0, 1):
                k = 2 * (first + n) + half
                ref[:, half * 8:half * 8 + 8, n * 128:n * 128 + 128] = split[:, k // 3, k % 3].astype(F32)
    for n in range(6):
        for half in (0, 1):
            joined_out[:, half * 8:half * 8 + 8, n * 128:n * 128 + 128] = split2[:, 2 * n + half].astype(F32)
    for i, ref in enumerate(wholes):
        for t in range(8):
            for n in range(2):
                for half in (0, 1):
                    at = t * 256 + n * 128
                    k = n * 2 + half
                    block_in = whole2[:, t, k] if i == 0 else whole[:, t, i * 4 + k]
                    ref[:, half * 8:half * 8 + 8, at:at + 128] = block_in.astype(F32)
    grad[...] = back[...].astype(F32)
    out[...] = layer[...]


def write_call(split, whole, split2, whole2, back, layer):
    widths = [768, 256, 1024, 1024] + [2048] * 4
    rows = pl.BlockSpec((32, 2048), lambda b: (b, 0))
    return pl.pallas_call(
        write_kernel, grid=(4,),
        out_shape=[shape(8, 16, n, dtype=F32) for n in widths] + [shape(128, 2048, dtype=F32), shape(128, 2048)],
        in_specs=[pl.BlockSpec((2, *n, 8, 128), lambda b, n=n: (b, *[0] * len(n), 0, 0)) for n in ((16, 3), (8, 16), (12,), (8, 4))
                  ] + [rows, rows],
        out_specs=[pl.BlockSpec((2, 16, n), lambda b: (b, 0, 0)) for n in widths] + [rows, rows],
        compiler_params=plain(58), name="write")(split, whole, split2, whole2, back, layer)


def local(tokens, grad_out, adapter_ids, first_gain, first_shift, joined_weight, joined_bias, dense_weight,
          dense_bias, second_gain, second_shift, up_weight, up_bias, down_weight, down_bias, joined_adapt_in,
          joined_adapt_out, dense_adapt_in, dense_adapt_out, up_adapt_in, up_adapt_out, down_adapt_in,
          down_adapt_out):
    turn = lambda a: jnp.swapaxes(a, 1, 2)
    flat = lambda a: a.reshape(128, a.shape[2])
    vectors = [a.reshape(1, -1) for a in (first_gain, first_shift, second_gain, second_shift, dense_bias, down_bias,
                                          up_bias)] + [joined_bias]
    adapters = dict(joined_in=turn(joined_adapt_in), joined_out=joined_adapt_out, dense_in=turn(dense_adapt_in),
                    dense_out=dense_adapt_out, up_in=turn(up_adapt_in), up_out=up_adapt_out,
                    down_in=turn(down_adapt_in), down_out=down_adapt_out)
    back, layer, split, whole, split2, whole2 = block_call(
        adapter_ids, tokens, grad_out, *vectors, *[flat(adapters[n]) for n in SETS], joined_weight, dense_weight,
        down_weight, up_weight)
    joined_out, dense_in, up_out, down_in, joined_in, dense_out, up_in, down_out, grad_tokens, layer_out = write_call(
        split, whole, split2, whole2, back, layer)
    return (layer_out, grad_tokens, turn(joined_in), joined_out, turn(dense_in), dense_out, turn(up_in), up_out,
            turn(down_in), down_out)


def solution(mesh):
    fine = Mesh(mesh.devices.reshape(2, 4, 2, 2, 4), AXES)
    rows, cols = P(FSDP, TP), P(TP, FSDP)
    tok = P((*FSDP, *TP), None)
    last, middle, one = P(None, None, TP), P(None, TP, None), P(TP)
    return jax.shard_map(
        local, mesh=fine,
        in_specs=(tok, tok, P(FSDP), P(), P(), rows, one, cols, P(), P(), P(), rows, one, cols, P(), P(), last,
                  middle, P(), P(), last, middle, P()),
        out_specs=(tok, tok, P(), last, middle, P(), P(), last, middle, P()), check_vma=False)
```

```python
import functools

import jax
import jax.numpy as jnp
from jax import lax
from jax.experimental import pallas as pl
from jax.experimental.pallas import tpu as pltpu
from jax.sharding import Mesh
from jax.sharding import PartitionSpec as P

HEADS = 32
EPSILON = 1e-05
MASKED = -1e30
AXES = ("xl", "y", "c", "xh", "z")
FSDP = ("xl", "y", "c")
TP = ("xh", "z")
PLANE = ("xl", "y", "xh")
MESH_ID = pl.DeviceIdType.MESH
ANY = pl.ANY
VMEM = pltpu.VMEM
DMA = pltpu.SemaphoreType.DMA
F32 = jnp.float32
BF16 = jnp.bfloat16
ORDER = (0, 3, 1, 2)
PICKS = dict(hot=(0, 128), joined_out=(128, 768), up_out=(896, 1024), dense_in=(1920, 256), down_in=(2176, 1024),
             joined_in=(3200, 2048), up_in=(5248, 2048), dense_out=(7296, 2048), down_out=(9344, 2048))
TRADED = 3200
PICKED = 11392


def remote(src, dst, sems, index, device):
    send, recv = sems
    return pltpu.make_async_remote_copy(
        src_ref=src, dst_ref=dst, send_sem=send.at[index], recv_sem=recv.at[index],
        device_id=device, device_id_type=MESH_ID)


def places():
    return tuple(lax.axis_index(a) for a in AXES)


def at_home():
    _, _, c, xh, _ = places()
    return 1 - (xh - c) * (xh - c)


def meet(peers):
    barrier = pltpu.get_barrier_semaphore()
    for p in peers:
        pl.semaphore_signal(barrier, inc=1, device_id=p, device_id_type=MESH_ID)
    pl.semaphore_wait(barrier, len(peers))


def group_peer(n):
    _, _, c, _, z = places()
    return {"c": lax.rem(c + n // 4, 2), "z": lax.rem(z + n % 4, 4)}


def group_peers():
    return [group_peer(n) for n in range(1, 8)]


def diagonal():
    _, _, c, xh, _ = places()
    return {"c": 1 - c, "xh": 1 - xh}


def plane_peers():
    xl, y, c, xh, _ = places()
    peers = []
    for d in range(1, 4):
        for core in (0, 1):
            peers.append({"y": lax.rem(y + d, 4), "c": core})
            x = lax.rem(xh * 2 + xl + d, 4)
            peers.append({"xh": x // 2, "xl": lax.rem(x, 2), "c": core})
    return peers


def block(ref, n, size=128):
    return ref.at[pl.ds(pl.multiple_of(n * size, size), size)]


def loop(count, body, first=0):
    def run(i, carry):
        body(i)
        return carry

    lax.fori_loop(first, count, run, 0)


class GroupGather:
    SEMS = [DMA((8, 4)), DMA((8, 4))]

    def __init__(self, dst, send, recv):
        self.dst, self.sems = dst, (send, recv)
        _, _, self.c, _, self.z = places()
        self.up, self.down, self.other = group_peer(1), group_peer(3), group_peer(4)

    def at(self, core, z, j):
        return self.dst.at[pl.ds(pl.multiple_of((core * 4 + z) * 128 + j * 32, 32), 32)]

    def copy(self, z, j, kind, device):
        ref = self.at(self.c, z, j)
        return remote(ref, ref, self.sems, (kind, j), device)

    def put(self, j):
        self.copy(self.z, j, 0, self.up).start()
        self.copy(self.z, j, 1, self.down).start()
        self.copy(self.z, j, 2, self.other).start()

    def near(self, j):
        below, above = lax.rem(self.z + 3, 4), lax.rem(self.z + 1, 4)
        self.copy(below, j, 0, self.up).wait_recv()
        if j < 2:
            self.copy(below, j, 3, self.up).start()
        self.copy(below, j, 5, self.other).start()
        self.copy(above, j, 1, self.down).wait_recv()
        if j >= 2:
            self.copy(above, j, 4, self.down).start()
        self.copy(above, j, 6, self.other).start()

    def far(self, j):
        opposite = lax.rem(self.z + 2, 4)
        self.copy(opposite, j, 3 if j < 2 else 4, self.up).wait_recv()
        self.copy(opposite, j, 7, self.other).start()

    def shared(self, kind):
        loop(4, lambda j: self.copy(self.z, j, kind, self.other).wait_recv())

    def finish(self):
        def end(j):
            for kind in (0, 1, 2, 3 + j // 2, 5, 6, 7):
                self.copy(self.z, j, kind, self.other).wait_send()

        loop(4, end)


class LowGather:
    SEMS = [DMA((8,)), DMA((8,))]

    def __init__(self, dst, send, recv):
        self.dst, self.sems = dst, (send, recv)
        _, _, c, _, z = places()
        self.own = pl.ds(pl.multiple_of((c * 4 + z) * 128, 128), 128)

    def copy(self, n):
        ref = self.dst.at[:, self.own]
        return remote(ref, ref, self.sems, (n,), group_peer(n))

    def start(self, value):
        self.dst[:, self.own] = value
        loop(8, lambda n: self.copy(n).start(), 1)

    def wait(self):
        loop(8, lambda n: self.copy(n).wait(), 1)


class LowSum:
    SEMS = [DMA((8,)), DMA((8,))]

    def __init__(self, src, got, send, recv):
        self.src, self.got, self.sems = src, got, (send, recv)
        _, _, self.c, _, self.z = places()

    def copy(self, n):
        p = group_peer(n)
        cols = pl.ds(pl.multiple_of((p["c"] * 4 + p["z"]) * 128, 128), 128)
        return remote(self.src.at[:, cols], self.got.at[n], self.sems, (n,), p)

    def start(self):
        loop(8, lambda n: self.copy(n).start(), 1)

    def total(self):
        loop(8, lambda n: self.copy(n).wait(), 1)
        own = pl.ds(pl.multiple_of((self.c * 4 + self.z) * 128, 128), 128)
        out = self.src[:, own].astype(F32)
        for n in range(1, 8):
            out = out + self.got[n].astype(F32)
        return out.astype(BF16)


class PlaneGather:
    SEMS = [DMA((1,)), DMA((41,)), DMA((16, 2))]

    def __init__(self, src, dst, by_rows, local_sem, send, recv):
        self.src, self.dst, self.by_rows, self.local_sem, self.sems = src, dst, by_rows, local_sem, (send, recv)
        self.xl, self.y, self.c, self.xh, _ = places()
        self.x = self.xh * 2 + self.xl
        self.home = at_home()
        r = lax.rem(self.x - 2 * self.c + 4, 4)
        self.odd = 1 - lax.rem(r, 2)
        self.even = lax.rem(r, 2)
        self.away = lax.rem(r - self.odd + 4, 4)

    def whole(self, xl, y, core):
        k = (xl * 4 + y) * 2 + core
        if self.by_rows:
            return block(self.dst, k)
        return self.dst.at[:, pl.ds(pl.multiple_of(k * 128, 128), 128)]

    def half(self, ref, h):
        n = ref.shape[0] // 2
        return ref.at[pl.ds(pl.multiple_of(h * n, n), n)]

    def copy(self, place, h, n, device, src=None):
        xl, y, core = place
        send, recv = self.sems
        dst = self.half(self.whole(*place), h)
        return pltpu.make_async_remote_copy(
            src_ref=dst if src is None else self.half(src, h), dst_ref=dst, send_sem=send.at[n],
            recv_sem=recv.at[(xl * 4 + y) * 2 + core, h], device_id=device, device_id_type=MESH_ID)

    def arrived(self, place, h):
        self.copy(place, h, 0, {"c": 1 - self.c}).wait_recv()

    def arrived_whole(self, place):
        loop(2, lambda h: self.arrived(place, h))

    def chip(self, dx, dy, core):
        x = lax.rem(self.x + dx, 4)
        return {"xh": x // 2, "xl": lax.rem(x, 2), "y": lax.rem(self.y + dy, 4), "c": core}

    def both_ways(self, place, n, along_x, along_y, core, src=None):
        def send(i):
            d = 1 + 2 * lax.rem(i, 2)
            h = lax.rem(i + i // 2, 2)
            self.copy(place, h, n + i, self.chip(along_x * d, along_y * d, core), src).start()

        loop(4, send)

    def local(self):
        return pltpu.make_async_copy(self.src, self.whole(self.xl, self.y, self.c), self.local_sem.at[0])

    def start(self):
        place = (self.xl, self.y, self.c)

        @pl.when(self.home == 1)
        def _():
            self.local().start()

        self.both_ways(place, 0, 1 - self.c, self.c, self.xh, self.src)

        @pl.when(self.home == 0)
        def _():
            loop(2, lambda h: self.copy(place, h, 39 + h, {"c": 1 - self.c}, self.src).start())

    def row(self, d):
        return lax.rem(self.y + d, 4)

    def along_y(self, e):
        self.both_ways((e, self.y, 0), 4 + 4 * e, 0, 1, self.c)

    def along_x(self, d):
        self.both_ways((self.xl, self.row(d), 1), 23 + 4 * d, 1, 0, self.c)

    def step(self, n):
        if n == 0:
            @pl.when(self.home == 1)
            def _():
                self.local().wait()
                self.arrived_whole((self.xl, self.y, 1 - self.c))
                self.along_y(self.xl)
                self.along_x(0)
        elif n == 1:
            place, h = (self.odd, self.y, 0), self.away // 2
            self.arrived(place, h)
            self.copy(place, h, 12, self.chip(self.away, 0, self.c)).start()

            @pl.when(self.home == 1)
            def _():
                def pass_y(k):
                    place = (self.xl, self.row(3 - 2 * k), 1)
                    self.arrived(place, k)
                    self.copy(place, k, 21 + k, self.chip(0, 1 + 2 * k, self.c)).start()

                loop(2, pass_y)
        elif n == 2:
            self.arrived((self.odd, self.y, 0), 1 - self.away // 2)
            self.along_y(self.odd)

            @pl.when(self.home == 1)
            def _():
                def spread(k):
                    self.arrived((self.xl, self.row(3 - 2 * k), 1), 1 - k)
                    self.along_x(3 - 2 * k)

                loop(2, spread)
        elif n == 3:
            @pl.when(self.home == 0)
            def _():
                self.arrived_whole((self.even, self.y, 0))
                self.along_y(self.even)

            @pl.when(self.home == 1)
            def _():
                self.arrived_whole((self.xl, self.row(2), 1))
                self.along_x(2)
        elif n == 4:
            def pass_on(i):
                e, k = i // 2, lax.rem(i, 2)
                place = (e, self.row(3 - 2 * k), 0)
                self.arrived(place, k)
                self.copy(place, k, 13 + i, self.chip(0, 1 + 2 * k, self.c)).start()

            loop(4, pass_on)
        else:
            def pass_on(i):
                k = i * (3 if n == 5 else 1) + (n - 5)
                place, h = (self.odd, self.row(k), 1), self.away // 2
                self.arrived(place, h)
                self.copy(place, h, 17 + k, self.chip(self.away, 0, self.c)).start()

            loop(2, pass_on)

    def wait(self):
        def rows(e):
            loop(2, lambda k: self.arrived((e, self.row(3 - 2 * k), 0), 1 - k))
            self.arrived_whole((e, self.row(2), 0))

        loop(2, rows)
        loop(4, lambda y: self.arrived((self.odd, y, 1), 1 - self.away // 2))

        @pl.when(self.home == 0)
        def _():
            loop(4, lambda y: self.arrived_whole((self.even, y, 1)))

    def finish(self):
        sent = lambda n: self.copy((0, 0, 0), 0, n, {"c": 1 - self.c}).wait_send()
        loop(21, sent)

        @pl.when(self.home == 1)
        def _():
            loop(39, sent, 21)

        @pl.when(self.home == 0)
        def _():
            loop(41, sent, 39)


class GroupSum:
    NAMES = ("far_up", "far_down", "up_high", "down_low", "up_low", "down_high")
    SCRATCH = [VMEM((1024, 2048), BF16), VMEM((4, 128, 2048), BF16), VMEM((3, 128, 2048), BF16),
               VMEM((2, 64, 2048), BF16), VMEM((2, 128, 2048), BF16), DMA((10,)), DMA((10,))]

    def __init__(self, parts, near, sent, half, full, send, recv):
        self.parts, self.near, self.sent, self.half, self.full, self.sems = parts, near, sent, half, full, (send, recv)
        _, _, self.c, _, self.z = places()
        self.up, self.down, self.other = group_peer(1), group_peer(3), group_peer(4)
        self.order = [lax.rem(self.z + d, 4) for d in (2, 1, 3, 0)]

    def part(self, core, i):
        return block(self.parts, core * 4 + self.order[i])

    def given(self, i):
        return remote(self.part(1 - self.c, i), self.near.at[i], self.sems, (i,), self.other)

    def give_from(self, i, at):
        remote(block(self.parts, (1 - self.c) * 4 + at), self.near.at[i], self.sems, (i,), self.other).start()

    def give(self, i):
        self.given(i).start()

    def pair(self, i, rows=slice(None)):
        return self.part(self.c, i)[rows].astype(F32) + self.near[i, rows].astype(F32)

    def piece(self, name):
        low, high = pl.ds(0, 64), pl.ds(64, 64)
        n = self.NAMES.index(name)
        src = (self.sent.at[0, low], self.sent.at[0, high], self.sent.at[1, high], self.sent.at[2, low],
               self.sent.at[1, low], self.sent.at[2, high])[n]
        dst = (self.half.at[0], self.half.at[1], self.full.at[0, high], self.full.at[1, low],
               self.full.at[0, low], self.full.at[1, high])[n]
        return remote(src, dst, self.sems, (4 + n,), (self.up, self.down)[n % 2])

    def far(self):
        self.given(0).wait_recv()
        self.sent[0] = self.pair(0).astype(BF16)
        self.piece("far_up").start()
        self.piece("far_down").start()

    def near_up(self):
        self.given(1).wait_recv()
        self.sent[1, pl.ds(64, 64)] = self.pair(1, pl.ds(64, 64)).astype(BF16)
        self.piece("up_high").start()

    def near_down(self):
        self.given(2).wait_recv()
        self.sent[2, pl.ds(0, 64)] = self.pair(2, pl.ds(0, 64)).astype(BF16)
        self.piece("down_low").start()

    def pass_on(self):
        low, high = pl.ds(0, 64), pl.ds(64, 64)
        self.piece("far_up").wait_recv()
        self.sent[1, low] = (self.pair(1, low) + self.half[0].astype(F32)).astype(BF16)
        self.piece("up_low").start()
        self.piece("far_down").wait_recv()
        self.sent[2, high] = (self.pair(2, high) + self.half[1].astype(F32)).astype(BF16)
        self.piece("down_high").start()

    def arrive(self):
        self.given(3).wait_recv()
        for name in ("up_high", "down_low", "up_low", "down_high"):
            self.piece(name).wait_recv()

    def total(self, rows=slice(None)):
        return self.pair(3, rows) + self.full[0, rows].astype(F32) + self.full[1, rows].astype(F32)

    def finish(self):
        for name in self.NAMES:
            self.piece(name).wait_send()
        for i in range(4):
            self.given(i).wait_send()


def params(cid, mib):
    return pltpu.CompilerParams(collective_id=cid, has_side_effects=True, vmem_limit_bytes=mib << 20)


def plain(mib):
    return pltpu.CompilerParams(vmem_limit_bytes=mib << 20)


def shape(*dims, dtype=BF16):
    return jax.ShapeDtypeStruct(dims, dtype)


def specs(*spaces):
    return [pl.BlockSpec(memory_space=s) for s in spaces]


def layer_norm(rows_in, gain, shift):
    row_mean = jnp.mean(rows_in, axis=-1, keepdims=True)
    centered = rows_in - row_mean
    variance = jnp.mean(centered * centered, axis=-1, keepdims=True)
    return centered * lax.rsqrt(variance + EPSILON) * gain + shift


def norm_back(rows_in, gain, grad):
    row_mean = jnp.mean(rows_in, axis=-1, keepdims=True)
    centered = rows_in - row_mean
    inverse = lax.rsqrt(jnp.mean(centered * centered, axis=-1, keepdims=True) + EPSILON)
    n = centered * inverse
    e = gain * grad
    return (e - jnp.mean(e, axis=-1, keepdims=True) - n * jnp.mean(e * n, axis=-1, keepdims=True)) * inverse


def dot(a, b, dims=((1,), (0,))):
    return lax.dot_general(a, b, (dims, ((), ())), preferred_element_type=F32)


def dot_t(a, b):
    return dot(a, b, ((1,), (1,)))


def dot_o(a, b):
    return dot(a, b, ((0,), (0,)))


def tiles(count, size, body):
    def run(i, carry):
        body(pl.ds(pl.multiple_of(i * size, size), size))
        return carry

    lax.fori_loop(0, count, run, 0)


def split_refs(refs, *counts):
    refs, out = list(refs), []
    for n in counts:
        out.append(refs[:n])
        refs = refs[n:]
    return (*out, refs)


def pick(ref, name):
    first, n = PICKS[name]
    return ref[:, pl.ds(first, n)]


def row_pair(z):
    return (pl.ds(pl.multiple_of(z * 128, 128), 128), pl.ds(pl.multiple_of(512 + z * 128, 128), 128))


def take_pair(ref, z, cols=slice(None)):
    a, b = row_pair(z)
    return jnp.concatenate([ref[a, cols], ref[b, cols]], axis=0)


def put_pair(ref, z, value, cols=slice(None)):
    a, b = row_pair(z)
    ref[a, cols] = value[:128]
    ref[b, cols] = value[128:]


class Swap:
    def __init__(self, pairs, local, send, recv):
        self.pairs, self.local, self.sems, self.home = pairs, local, (send, recv), at_home()

    def near_copy(self, n):
        src, _, dst = self.pairs[n]
        return pltpu.make_async_copy(src, dst, self.local.at[n])

    def far_copy(self, n):
        src, dst, _ = self.pairs[n]
        return remote(src, dst, self.sems, (n,), diagonal())

    def start(self, n):
        @pl.when(self.home == 1)
        def _():
            self.near_copy(n).start()

        @pl.when(self.home == 0)
        def _():
            self.far_copy(n).start()

    def wait(self, n):
        @pl.when(self.home == 1)
        def _():
            self.near_copy(n).wait()

        @pl.when(self.home == 0)
        def _():
            self.far_copy(n).wait_recv()

    def finish(self):
        @pl.when(self.home == 0)
        def _():
            for n in range(len(self.pairs)):
                self.far_copy(n).wait_send()

    @staticmethod
    def sems(n):
        return [DMA((n,)), DMA((n,)), DMA((n,))]


class Spread:
    SCRATCH = [VMEM((16, 5, 8, 128), BF16), VMEM((16, 5, 8, 128), BF16), VMEM((8, 3, 8, 128), BF16),
               VMEM((8, 8, 128), BF16), DMA((16,)), DMA((16,)), DMA((9,)), DMA((16,)), DMA((20,)), DMA((20,)), DMA((2,))]

    def __init__(self, split, whole, send, got, part, full, one_send, one_recv, two_send, two_recv, send3, recv3, local):
        self.split, self.whole, self.send, self.got, self.part, self.full = split, whole, send, got, part, full
        self.one, self.two, self.three, self.local = (one_send, one_recv), (two_send, two_recv), (send3, recv3), local
        self.xl, self.y, self.c, self.xh, self.z = places()
        self.q = (self.xh * 2 + self.xl) * 4 + self.y
        self.home = at_home()

    def put(self, n, value):
        for m in range(4):
            k = 2 * n + m
            where = (k // 3, k % 3) if k < 48 else (k - 48, 3)
            row, col = m % 2 * 8, m // 2 * 128
            self.send[where] = value[row:row + 8, col:col + 128].astype(BF16)

    def mark(self, hot):
        for j in range(16):
            self.send[j, 4] = hot

    def chip(self, n):
        q = lax.rem(self.q + n, 16)
        x = q // 4
        return q, {"xh": x // 2, "xl": lax.rem(x, 2), "y": lax.rem(q, 4)}

    def to_owner(self, n):
        q, device = self.chip(n)
        return remote(self.send.at[q], self.got.at[n], self.one, (n,), device)

    def start(self):
        loop(16, lambda n: self.to_owner(n).start(), 1)

    def add(self):
        self.got[0] = self.send[self.q]
        loop(16, lambda n: self.to_owner(n).wait_recv(), 1)
        for b in range(8):
            def more(n, total, b=b):
                return total + self.got[n, 0:4].astype(F32) * self.got[n, 4].astype(F32)[b:b + 1]

            total = lax.fori_loop(0, 16, more, jnp.zeros((4, 8, 128), F32)).astype(BF16)
            self.part[b] = total[:3]
            self.full[b] = total[3]

    def copy_to_groups(self, slot, i):
        device = {"xh": self.c, "xl": lax.rem(self.xl + i // 4, 2), "y": lax.rem(self.y + lax.rem(i, 4), 4)}
        send, recv = self.two
        return pltpu.make_async_remote_copy(
            src_ref=self.part, dst_ref=self.split.at[:, slot], send_sem=send.at[i],
            recv_sem=recv.at[self.q], device_id=device, device_id_type=MESH_ID)

    def split_copy(self, i):
        return self.copy_to_groups(self.q, i)

    def split_own(self):
        return pltpu.make_async_copy(self.part, self.split.at[:, self.q], self.local.at[0])

    def whole_own(self):
        return pltpu.make_async_copy(self.full, self.whole.at[:, self.c * 4 + self.z, self.q], self.local.at[1])

    def line_copies(self):
        where = self.whole.at[:, self.c * 4 + self.z, self.q]
        return [remote(self.full, where, self.three, (d,), {"z": lax.rem(self.z + d, 4)}) for d in (1, 2, 3)]

    def plane_copy(self, n):
        where = self.whole.at[:, pl.ds(self.c * 4, 4), self.q]
        return remote(where, where, self.three, (4 + n,), self.chip(n)[1])

    def shared_whole(self):
        where = self.whole.at[:, pl.ds(self.c * 4, 4)]
        return remote(where, where, self.three, (0,), {"c": 1 - self.c})

    def shared_split(self):
        send, recv = self.two
        return pltpu.make_async_remote_copy(
            src_ref=self.split, dst_ref=self.split, send_sem=send.at[8], recv_sem=recv.at[0],
            device_id={"c": 1 - self.c}, device_id_type=MESH_ID)

    def deal_groups(self):
        @pl.when(self.home == 1)
        def _():
            self.split_own().start()

        @pl.when(self.home == 0)
        def _():
            self.split_copy(0).start()

        loop(8, lambda i: self.split_copy(i).start(), 1)

    def deal(self):
        self.whole_own().start()
        for copy in self.line_copies():
            copy.start()
        self.deal_groups()

    def deal_plane(self):
        self.whole_own().wait()
        for copy in self.line_copies():
            copy.wait_recv()
        loop(16, lambda n: self.plane_copy(n).start(), 1)

    def wait_groups(self, count):
        send, recv = self.two
        def wait(q):
            @pl.when(self.q != q)
            def _():
                pltpu.make_async_remote_copy(
                    src_ref=self.part, dst_ref=self.split.at[:, q], send_sem=send.at[0], recv_sem=recv.at[q],
                    device_id={"c": 1 - self.c}, device_id_type=MESH_ID).wait_recv()

        loop(count, wait)

    def share(self):
        @pl.when(self.home == 1)
        def _():
            self.split_own().wait()
            self.wait_groups(16)
            self.shared_split().start()

        loop(16, lambda n: self.plane_copy(n).wait_recv(), 1)
        self.shared_whole().start()

    def finish_shares(self):
        self.shared_whole().wait()

        @pl.when(self.home == 1)
        def _():
            self.shared_split().wait_send()

        @pl.when(self.home == 0)
        def _():
            self.shared_split().wait_recv()

    def finish_groups(self):
        @pl.when(self.home == 0)
        def _():
            self.split_copy(0).wait_send()

        loop(8, lambda i: self.split_copy(i).wait_send(), 1)

    def finish(self):
        self.finish_shares()
        self.finish_groups()
        for copy in self.line_copies():
            copy.wait_send()

        def end(n):
            self.plane_copy(n).wait_send()
            self.to_owner(n).wait_send()

        loop(16, end, 1)


class LastSpread(Spread):
    SCRATCH = [VMEM((16, 2, 8, 128), BF16), VMEM((16, 2, 8, 128), BF16), VMEM((8, 8, 128), BF16),
               DMA((16,)), DMA((16,)), DMA((9,)), DMA((16,)), DMA((20,)), DMA((20,)), DMA((2,))]

    def __init__(self, split, whole, send, got, part, *sems):
        super().__init__(split, whole, send, got, part, part, *sems)

    def put(self, n, value):
        for m in range(4):
            row, col = m % 2 * 8, m // 2 * 128
            self.send[2 * n + m, 0] = value[row:row + 8, col:col + 128].astype(BF16)

    def mark(self, hot):
        for j in range(16):
            self.send[j, 1] = hot

    def add(self):
        self.got[0] = self.send[self.q]
        loop(16, lambda n: self.to_owner(n).wait_recv(), 1)
        for b in range(8):
            def more(n, total, b=b):
                return total + self.got[n, 0].astype(F32) * self.got[n, 1].astype(F32)[b:b + 1]

            self.part[b] = lax.fori_loop(0, 16, more, jnp.zeros((8, 128), F32)).astype(BF16)

    def split_copy(self, i):
        return self.copy_to_groups(lax.rem(self.q, 12), i)

    def split_own(self):
        return pltpu.make_async_copy(self.part, self.split.at[:, lax.rem(self.q, 12)], self.local.at[0])

    def late(self):
        return lax.rem(self.q, 4)

    def whole_own(self):
        return pltpu.make_async_copy(self.part, self.whole.at[:, self.c * 4 + self.z, self.late()], self.local.at[1])

    def line_copies(self):
        where = self.whole.at[:, self.c * 4 + self.z]
        return [remote(where, where, self.three, (d,), {"z": lax.rem(self.z + d, 4)}) for d in (1, 2, 3)]

    def plane_copy(self, n):
        where = self.whole.at[:, self.c * 4 + self.z, self.late()]
        return remote(self.part, where, self.three, (4 + n,), self.chip(n)[1])

    def deal(self):
        @pl.when(self.q >= 12)
        def _():
            self.whole_own().start()
            loop(16, lambda n: self.plane_copy(n).start(), 1)

        @pl.when(self.q < 12)
        def _():
            self.deal_groups()

    def share_groups(self):
        @pl.when(self.home == 1)
        def _():
            @pl.when(self.q < 12)
            def _():
                self.split_own().wait()

            self.wait_groups(12)
            self.shared_split().start()

    def line(self):
        @pl.when(self.q >= 12)
        def _():
            self.whole_own().wait()

        def late(n):
            @pl.when(lax.rem(self.q - n + 16, 16) >= 12)
            def _():
                self.plane_copy(n).wait_recv()

        loop(16, late, 1)

        for copy in self.line_copies():
            copy.start()

    def share_line(self):
        for copy in self.line_copies():
            copy.wait_recv()
        self.shared_whole().start()

    def finish(self):
        self.finish_shares()

        @pl.when(self.q < 12)
        def _():
            self.finish_groups()

        @pl.when(self.q >= 12)
        def _():
            loop(16, lambda n: self.plane_copy(n).wait_send(), 1)

        for copy in self.line_copies():
            copy.wait_send()
        loop(16, lambda n: self.to_owner(n).wait_send(), 1)


def far_peers():
    xl, y, _, xh, _ = places()
    peers = []
    for d in range(1, 4):
        x = lax.rem(xh * 2 + xl + d, 4)
        for e in range(1, 4):
            peers.append({"xh": x // 2, "xl": lax.rem(x, 2), "y": lax.rem(y + e, 4)})
    return peers


ROOT_HALF = 0.7071067811865476
ROOT_TAU = 0.3989422804014327
SETS = dict(joined_in=(0, 0), up_in=(128, 0), dense_out=(256, 0), down_out=(384, 0), up_out=(512, 0),
            down_in=(512, 1024), joined_out=(640, 0), dense_in=(640, 768))


def cast_parts(value):
    high = value.astype(BF16).astype(F32)
    middle = (value - high).astype(BF16).astype(F32)
    return high, middle, value - high - middle


def block_kernel(*refs):
    (ids, tokens, go, *vectors), adapters, shards, outs, scratch = split_refs(refs, 11, 8, 4, 6)
    back, out, split, whole, split2, whole2 = outs
    names = list(SCRATCH)
    v = dict(zip(names, scratch))
    rest = list(scratch[len(names):])

    def sems(n):
        taken = rest[:n]
        del rest[:n]
        return taken

    load_sem, vector_sem, copy_sem = sems(3)
    xl, y, c, xh, z = places()
    own = c * 4 + z
    mine_rows = pl.ds(pl.multiple_of(own * 128, 128), 128)
    there_rows = (1 - c) * 4 + z
    gain1, shift1, gain2, shift2, bias_d, bias_n = (v["lines"].at[n:n + 1] for n in range(6))
    pk, xs, xbuf, gbuf = v["pk"], v["xs"], v["xbuf"], v["gbuf"]
    sets = v["parts"]
    loads = {}
    for n, (name, ref) in enumerate(zip(SETS, adapters)):
        row, col = SETS[name]
        loads[name] = pltpu.make_async_copy(ref, sets.at[pl.ds(row, 128), pl.ds(col, ref.shape[1])], load_sem.at[n])
        loads[name].start()
    lines = [pltpu.make_async_copy(ref, v["lines"].at[n:n + 1], vector_sem.at[n]) for n, ref in enumerate(vectors[:6])]
    for line in lines:
        line.start()
    meet(plane_peers() + group_peers() + far_peers())

    bias = v["bias"]
    mine = v["mine"]
    piece = lambda who, j: gbuf.at[pl.ds(pl.multiple_of(who * 128 + j * 32, 32), 32)]
    sub = lambda ref, j: ref.at[pl.ds(j * 32, 32)]
    pairs = [(sub(tokens, j), sub(xs, j), sub(xs, j)) for j in range(4)]
    pairs += [(m, p, p) for m, p in ((mine, pk.at[:, :TRADED]), (vectors[7], v["bias_one"]), (vectors[6], bias))]
    pairs += [(sub(go, j), piece(there_rows, j), piece(own, j)) for j in range(4)]
    sw = Swap(pairs, *sems(3))
    for j in ORDER:
        sw.start(j)
    joined = PlaneGather(shards[0], v["wj"], True, *sems(3))
    dense = PlaneGather(shards[1], v["wd"], False, *sems(3))
    down = PlaneGather(shards[2], v["wn"], False, *sems(3))
    up = PlaneGather(shards[3], v["wu"], True, *sems(3))
    joined.start()
    set_id = ids[0]
    for name in ("joined_out", "up_out", "dense_in", "down_in"):
        (row, col), (first, n) = SETS[name], PICKS[name]
        loads[name].wait()
        chosen = sets[row:row + 16, col:col + n]
        for k in range(1, 8):
            chosen = jnp.where(set_id == k, sets[row + k * 16:row + k * 16 + 16, col:col + n], chosen)
        mine[:, first:first + n] = chosen
    first, n = PICKS["hot"]
    mine[:, first:first + n] = jnp.where(lax.broadcasted_iota(jnp.int32, (16, 128), 0) == set_id, 1.0, 0.0).astype(BF16)
    for n in (4, 5, 6):
        sw.start(n)
    for line in lines:
        line.wait()
    g1 = GroupGather(xbuf, *sems(2))
    for j in ORDER:
        sw.wait(j)
        x1 = layer_norm(xs[j * 32:(j + 1) * 32].astype(F32), gain1[...], shift1[...])
        xbuf[pl.ds(pl.multiple_of(own * 128 + j * 32, 32), 32)] = x1.astype(BF16)
        g1.put(j)
    dense.start()
    joined.step(0)
    joined.step(1)
    g1.near(0)
    joined.step(2)
    g1.near(3)
    joined.step(3)
    g1.near(1)
    joined.step(4)
    g1.near(2)
    joined.step(5)
    joined.step(6)
    for j in ORDER:
        sw.start(7 + j)
    dense.step(0)
    dense.step(1)
    down.start()
    sw.wait(4)
    for name in ("joined_in", "up_in", "dense_out", "down_out"):
        (row, col), (first, n) = SETS[name], PICKS[name]
        loads[name].wait()
        chosen = jnp.zeros((16, n), F32)
        for k in range(8):
            chosen = chosen + sets[row + k * 16:row + k * 16 + 16, col:col + n].astype(F32) * pk[k:k + 1, 0:1].astype(F32)
        pk[:, first:first + n] = chosen.astype(BF16)

    def low_pair(at):
        low = dot_t(pick(pk, "joined_in"), take_pair(xbuf, at)).astype(BF16)
        for n, rows in enumerate(row_pair(at)):
            v["low_q"][:, rows] = low[:, n * 128:n * 128 + 128]

    g1.shared(2)
    low_pair(z)
    for j in ORDER:
        g1.far(j)
    g1.shared(5)
    low_pair(lax.rem(z + 3, 4))
    g1.shared(6)
    low_pair(lax.rem(z + 1, 4))
    g1.shared(7)
    low_pair(lax.rem(z + 2, 4))
    g2 = GroupGather(gbuf, *sems(2))
    for n in (5, 6):
        sw.wait(n)
    joined.wait()

    lane = lax.broadcasted_iota(jnp.int32, (256, 128), 1)
    row = lax.broadcasted_iota(jnp.int32, (256, 128), 0)
    qa, ka, va = v["qa"], v["ka"], v["va"]

    def project(i, carry):
        rows = pl.ds(pl.multiple_of(i * 256, 256), 256)
        acc = dot(xbuf[rows], v["wj"][...]) + dot_o(v["low_q"][:, rows], pick(pk, "joined_out")) + v["bias_one"][...].reshape(1, 768)
        b = acc.astype(BF16).astype(F32)
        position = (i * 256 + row).astype(F32) * 0.125
        ones = jnp.where(lane < 67, 1.0, 0.0)
        for h in range(4):
            slope = jnp.exp2((own * 4 + h + 1).astype(F32) * (-8.0 / HEADS) + jnp.zeros((1, 128), F32))
            high, middle, lowest = cast_parts(position * slope)
            tail = jnp.where(lane == 64, high, jnp.where(lane == 65, middle, jnp.where(lane == 66, lowest, jnp.where(
                lane < 70, 1.0, 0.0))))
            at = h * 192
            qa[h, rows] = jnp.where(lane < 64, b[:, at:at + 128] * 0.125, ones).astype(BF16)
            ka[h, rows] = jnp.where(lane < 64, b[:, at + 64:at + 192], tail).astype(BF16)
            value = jnp.concatenate([b[:, at + 128:at + 192], b[:, at:at + 64]], axis=1)
            va[h, rows] = jnp.where(lane < 64, value, ones).astype(BF16)
        return carry

    lax.fori_loop(0, 4, project, 0)
    own_cols = pl.ds(pl.multiple_of(own * 256, 256), 256)
    keep = lambda n, ref: pltpu.make_async_copy(ref.at[:, own_cols], v["cols"].at[n], copy_sem.at[n])
    keep(0, xbuf).start()
    for j in ORDER:
        sw.wait(7 + j)
        g2.put(j)

    hooks = [lambda: dense.step(2), lambda: down.step(0), lambda: (dense.step(3), down.step(1)), lambda: g2.near(0), lambda: dense.step(4),
             lambda: g2.near(3), lambda: down.step(2), lambda: g2.near(1), lambda: (dense.step(5), dense.step(6)),
             lambda: g2.near(2), lambda: up.start(), lambda: down.step(3), lambda: (g2.far(0), g2.far(3)),
             lambda: None, lambda: (g2.far(1), g2.far(2)), lambda: down.step(4)]
    mask = lax.broadcasted_iota(jnp.int32, (256, 256), 0) <= lax.broadcasted_iota(jnp.int32, (256, 256), 1)
    line = lax.broadcasted_iota(jnp.int32, (128, 256), 0)
    c4 = v["c4"]

    def head(h, carry):
        for i in range(4):
            rows = pl.ds(i * 256, 256)
            q = qa[h, rows]
            last = jnp.where(mask, dot_t(ka[h, rows], q), MASKED)
            top = jnp.max(last, axis=0, keepdims=True)
            if i:
                before = dot_t(ka[h, pl.ds(0, i * 256)], q)
                top = jnp.maximum(top, jnp.max(before, axis=0, keepdims=True))
            mix = dot_o(va[h, rows], jnp.exp(last - top).astype(BF16))
            if i:
                mix = mix + dot_o(va[h, pl.ds(0, i * 256)], jnp.exp(before - top).astype(BF16))
            total = mix[64:65]
            high, middle, lowest = cast_parts(-(top + jnp.log(total)))
            mix = jnp.where(line == 67, high, jnp.where(line == 68, middle, jnp.where(
                line == 69, lowest, mix / total)))
            turned = mix.T
            c4[h, rows] = turned.astype(BF16)
            qa[h, rows] = jnp.where(lane < 67, q.astype(F32), jnp.where(lane < 70, turned, 0.0)).astype(BF16)
            for k in range(4):
                @pl.when(h == k)
                def _(k=k, i=i):
                    hooks[k * 4 + i]()
        return carry

    lax.fori_loop(0, 4, head, 0)
    ctx = v["ctx"]
    for h in (0, 2):
        ctx[:, h * 64:h * 64 + 128] = jnp.concatenate([c4[h, :, :64], c4[h + 1, :, :64]], axis=1)

    v["gos"][...] = gbuf[mine_rows]

    src, got = v["low_src"], v["low_got"]
    src[0] = dot_t(pick(pk, "dense_in"), ctx[...]).astype(BF16)
    sum_d = LowSum(src.at[0], got.at[0], *sems(2))
    sum_d.start()
    s1 = GroupSum(*[v[n] for n in ("parts", "near", "sent", "half", "full")], *sems(2))
    dense.wait()
    keep(0, xbuf).wait()
    g1.finish()

    def summed(s, compute, before=lambda: None, beside=lambda: None):
        def part(i, carry):
            compute(s, lax.rem(z + 2 - i + 3 * (i // 2) - 2 * (i // 3) + 4, 4))
            s.give_from(i, lax.rem(z + 2 - i + 3 * (i // 2) - 2 * (i // 3) + 4, 4))

            @pl.when(i == 1)
            def _():
                before()
                s.far()

            @pl.when(i == 2)
            def _():
                s.near_up()

            return carry

        lax.fori_loop(0, 4, part, 0)
        s.near_down()
        beside()
        s.pass_on()

    def dense_part(s, at):
        put_pair(s.parts, at, dot(take_pair(ctx, at), v["wd"][...]).astype(BF16))

    def low_tile(rows):
        v["low_g"][:, rows] = dot_t(pick(pk, "down_out"), gbuf[rows]).astype(BF16)

    def beside_dense():
        for kind in (2, 5, 6, 7):
            g2.shared(kind)
        keep(3, gbuf).start()
        down.step(5)
        up.step(0)
        tiles(4, 256, low_tile)
        down.step(6)
        up.step(1)

    summed(s1, dense_part, beside=beside_dense)
    up.step(2)
    mid, dmid, dact = v["mid"], v["dmid"], v["dact"]
    total_d = sum_d.total()
    mid[...] = dot_o(total_d, pick(pk, "dense_out")) + bias_d[...] + xs[...].astype(F32)
    down.wait()

    def grad_act(rows):
        dact[rows] = dot_t(gbuf[rows], v["wn"][...]) + dot_o(v["low_g"][:, rows], pick(pk, "down_in"))

    def grad_acts(i, carry):
        grad_act(pl.ds(pl.multiple_of(i * 256, 256), 256))

        @pl.when(i == 1)
        def _():
            up.step(3)

        return carry

    lax.fori_loop(0, 4, grad_acts, 0)
    up.step(4)
    s1.arrive()
    g3 = GroupGather(xbuf, *sems(2))
    for j in ORDER:
        rows = slice(j * 32, (j + 1) * 32)
        mid[rows] = mid[rows] + s1.total(rows)
        xbuf[pl.ds(pl.multiple_of(own * 128 + j * 32, 32), 32)] = layer_norm(mid[rows], gain2[...], shift2[...]).astype(BF16)
        g3.put(j)
    all_d = LowGather(v["sum_d"], *sems(2))
    all_d.start(total_d)
    up.step(5)
    up.step(6)
    up.wait()
    act, dpre = v["act"], v["dpre"]

    def forward(at):
        x = take_pair(xbuf, at)
        lu = dot_t(pick(pk, "up_in"), x).astype(BF16)
        for n, rows in enumerate(row_pair(at)):
            v["low_u"][:, rows] = lu[:, n * 128:n * 128 + 128]

        def run(n, carry):
            cols = pl.ds(pl.multiple_of(n * 256, 256), 256)
            w = pk[:, pl.ds(pl.multiple_of(PICKS["up_out"][0] + n * 256, 128), 256)]
            b = bias[:, pl.ds(pl.multiple_of(n * 256, 256), 256)]
            pre = dot(x, v["wu"][:, cols]) + dot_o(lu, w) + b
            cdf = 0.5 * (1.0 + lax.erf(pre * ROOT_HALF))
            put_pair(act, at, (pre * cdf).astype(BF16), cols)
            slope = cdf + pre * (jnp.exp(-0.5 * pre * pre) * ROOT_TAU)
            put_pair(dpre, at, (take_pair(dact, at, cols) * slope).astype(BF16), cols)
            return carry

        lax.fori_loop(0, 4, run, 0)

    def by_pairs(g, work, beside=None):
        def run(p, carry):
            @pl.when(p == 0)
            def _():
                g.shared(2)

            @pl.when(p == 1)
            def _():
                if beside:
                    beside()
                for j in ORDER:
                    g.near(j)
                g.shared(6)

            @pl.when(p == 2)
            def _():
                g.shared(5)

            @pl.when(p == 3)
            def _():
                for j in ORDER:
                    g.far(j)
                g.shared(7)

            work(lax.rem(z + p + p // 2 - 2 * (p // 3), 4))
            return carry

        lax.fori_loop(0, 4, run, 0)

    by_pairs(g3, forward)
    keep(2, xbuf).start()

    sum_u = LowSum(src.at[1], got.at[1], *sems(2))
    s2 = GroupSum(*[v[n] for n in ("parts", "near", "sent", "half", "full")], *sems(2))
    s1.finish()

    def wide(ref, weight):
        def compute(s, at):
            x = take_pair(ref, at)

            def run(n, carry):
                cols = pl.ds(pl.multiple_of(n * 512, 512), 512)
                put_pair(s.parts, at, dot_t(x, weight[cols]).astype(BF16), cols)
                return carry

            lax.fori_loop(0, 4, run, 0)

        return compute

    keep(2, xbuf).wait()
    g3.finish()
    def low_up():
        src[1] = dot_t(pick(pk, "up_out"), dpre[...]).astype(BF16)
        sum_u.start()

    summed(s2, wide(dpre, v["wu"]), beside=low_up)
    for thing in (joined, dense, down, up, sw):
        thing.finish()
    keep(3, gbuf).wait()
    g2.finish()
    mlp = gbuf

    def forward_down(rows):
        mlp[rows] = dot(act[rows], v["wn"][...]).astype(BF16)

    tiles(4, 256, forward_down)
    src[2] = dot_t(pick(pk, "down_in"), act[...]).astype(BF16)
    total_u = sum_u.total()
    dmid[...] = dot_o(total_u, pick(pk, "up_in"))
    sum_n = LowSum(src.at[2], got.at[2], *sems(2))
    sum_n.start()
    all_u = LowGather(v["sum_u"], *sems(2))
    all_u.start(total_u)
    s2.arrive()
    all_n = LowGather(v["sum_n"], *sems(2))
    all_n.start(sum_n.total())
    g4 = GroupGather(xbuf, *sems(2))
    for j in ORDER:
        rows = slice(j * 32, (j + 1) * 32)
        dmid[rows] = v["gos"][rows].astype(F32) + norm_back(mid[rows], gain2[...], dmid[rows] + s2.total(rows))
        xbuf[pl.ds(pl.multiple_of(own * 128 + j * 32, 32), 32)] = dmid[rows].astype(BF16)
        g4.put(j)
    spread = Spread(split, whole, *sems(11))

    def product(first, count, low, ref):
        for n in range(0, count, 2):
            spread.put(first + n, dot(low[...], ref[:, n * 128:n * 128 + 256]))

    def early_products():
        spread.mark(pk[:8, PICKS["hot"][0]:PICKS["hot"][0] + 128])
        product(2, 8, v["low_u"], dpre)
        product(10, 8, v["low_g"], act)
        all_u.wait()
        product(28, 2, v["sum_u"], v["cols"].at[2])

    grads = c4

    def context(at):
        x = take_pair(xbuf, at)
        ld = dot_t(pick(pk, "dense_out"), x).astype(BF16)
        for n, rows in enumerate(row_pair(at)):
            v["low_d"][:, rows] = ld[:, n * 128:n * 128 + 128]
        value = dot_t(x, v["wd"][...]) + dot_o(ld, pick(pk, "dense_in"))
        value = value.astype(BF16).astype(F32)
        mix = take_pair(ctx, at).astype(F32)
        for h in range(4):
            first = h // 2 * 128
            g = value[:, first:first + 128]
            here = (lane // 64) == h % 2
            d = -jnp.sum(jnp.where(here, g * mix[:, first:first + 128], 0.0), axis=-1, keepdims=True)
            high, middle, lowest = cast_parts(d)
            if h % 2:
                g = jnp.concatenate([g[:, 64:], g[:, :64]], axis=1)
            put_pair(grads.at[h], at, jnp.where(lane < 64, g, jnp.where(lane == 64, high, jnp.where(
                lane == 65, middle, jnp.where(lane == 66, lowest, 0.0)))).astype(BF16))

    by_pairs(g4, context, early_products)
    keep(1, xbuf).start()

    s3 = GroupSum(mlp, *[v[n] for n in ("near2", "sent2", "half2", "full2")], *sems(2))
    for i in range(4):
        s3.give(i)
    def dense_products():
        product(0, 2, v["low_d"], ctx)
        all_d.wait()
        keep(1, xbuf).wait()
        product(26, 2, v["sum_d"], v["cols"].at[1])
        all_n.wait()
        product(30, 2, v["sum_n"], v["cols"].at[3])
        spread.start()

    dense_products()
    hooks_back = {0: s3.far, 1: s3.near_up, 2: s3.near_down, 6: spread.add, 7: spread.deal, 8: s3.pass_on,
                  15: spread.deal_plane}
    dk, dv = v["dact"].at[:, 0:128], v["dact"].at[:, 128:256]

    def head_back(h, carry):
        dk[...] = jnp.zeros_like(dk)
        dv[...] = jnp.zeros_like(dv)
        for i in range(4):
            rows = pl.ds(i * 256, 256)
            q, g = qa[h, rows], grads[h, rows]

            def span(keys, masked):
                k = ka[h, keys]
                score = dot_t(k, q)
                if masked:
                    score = jnp.where(mask, score, MASKED)
                p = jnp.exp(score)
                ds = (p * dot_t(va[h, keys], g)).astype(BF16)
                dk[keys] += dot(ds, q)
                dv[keys] += dot(p.astype(BF16), g)
                return dot_o(k, ds)

            dq = span(rows, True)
            if i:
                dq = dq + span(pl.ds(0, i * 256), False)
            grads[h, rows] = (dq * 0.125).T.astype(BF16)
            for n, hook in hooks_back.items():
                if n % 4 == i:
                    @pl.when(h == n // 4)
                    def _(hook=hook):
                        hook()
        ka[h] = dk[...].astype(BF16)
        va[h] = dv[...].astype(BF16)
        return carry

    lax.fori_loop(0, 4, head_back, 0)
    dfused = v["dfused"]
    for h in (0, 2):
        dfused[:, h * 192:h * 192 + 384] = jnp.concatenate(
            [ref[k, :, :64] for k in (h, h + 1) for ref in (grads, ka, va)], axis=1)

    src[3] = dot_t(pick(pk, "joined_out"), dfused[...]).astype(BF16)
    sum_q = LowSum(src.at[3], got.at[3], *sems(2))
    sum_q.start()
    s4 = GroupSum(*[v[n] for n in ("parts", "near", "sent", "half", "full")], *sems(2))
    s2.finish()
    all_q = LowGather(v["sum_q"], *sems(2))

    def early_low():
        value = sum_q.total()
        all_q.start(value)

    spread2 = LastSpread(split2, whole2, *sems(10))

    def late_products():
        spread2.mark(pk[:8, PICKS["hot"][0]:PICKS["hot"][0] + 128])
        for n in range(0, 6, 2):
            spread2.put(n, dot(v["low_q"][...], dfused[:, n * 128:n * 128 + 256]))

    summed(s4, wide(dfused, v["wj"]), early_low, late_products)
    all_q.wait()
    spread2.put(6, dot(v["sum_q"][...], v["cols"][0]))
    spread2.start()
    layer, mine_grad = v["layer"], v["gos"]
    pairs = [(sub(mine_grad, j), sub(back, j), sub(back, j)) for j in range(4)] + [(layer, out, out)]
    sw2 = Swap(pairs, *sems(3))
    s3.arrive()
    for thing in (g4, s3):
        thing.finish()
    layer[...] = (mid[...] + bias_n[...] + dot_o(v["sum_n"][:, mine_rows], pick(pk, "down_out")) + s3.total()).astype(BF16)
    sw2.start(4)
    spread.share()
    correction = dot_o(v["sum_q"][:, mine_rows], pick(pk, "joined_in"))
    spread2.add()
    spread2.deal()
    s4.arrive()
    for j in ORDER:
        rows = slice(j * 32, (j + 1) * 32)
        value = dmid[rows] + norm_back(xs[rows].astype(F32), gain1[...], correction[rows] + s4.total(rows))
        mine_grad[rows] = value.astype(BF16)
        sw2.start(j)
    spread2.share_groups()
    spread2.line()
    spread.finish()
    spread2.share_line()
    for n in range(5):
        sw2.wait(n)
    spread2.finish()
    for thing in (s4, sw2):
        thing.finish()


SCRATCH = dict(
    lines=((8, 2048), F32), bias=((1, 1024), F32), bias_one=((768,), F32), mine=((16, TRADED), BF16), pk=((16, PICKED), BF16),
    xs=((128, 2048), BF16), xbuf=((1024, 2048), BF16), gbuf=((1024, 2048), BF16), gos=((128, 2048), BF16),
    wj=((2048, 768), BF16), wd=((256, 2048), BF16), wn=((1024, 2048), BF16), wu=((2048, 1024), BF16),
    qa=((4, 1024, 128), BF16), ka=((4, 1024, 128), BF16), va=((4, 1024, 128), BF16), c4=((4, 1024, 128), BF16),
    ctx=((1024, 256), BF16), dfused=((1024, 768), BF16), act=((1024, 1024), BF16),
    dpre=((1024, 1024), BF16), dact=((1024, 1024), F32), mid=((128, 2048), F32), dmid=((128, 2048), F32),
    layer=((128, 2048), BF16), cols=((4, 1024, 256), BF16),
    low_src=((4, 16, 1024), BF16), low_got=((4, 8, 16, 128), BF16),
    low_q=((16, 1024), BF16), low_g=((16, 1024), BF16), low_u=((16, 1024), BF16), low_d=((16, 1024), BF16),
    sum_d=((16, 1024), BF16), sum_u=((16, 1024), BF16), sum_n=((16, 1024), BF16), sum_q=((16, 1024), BF16),
    parts=((1024, 2048), BF16), near=((4, 128, 2048), BF16), sent=((3, 128, 2048), BF16), half=((2, 64, 2048), BF16),
    full=((2, 128, 2048), BF16), near2=((4, 128, 2048), BF16), sent2=((3, 128, 2048), BF16),
    half2=((2, 64, 2048), BF16), full2=((2, 128, 2048), BF16))


def block_call(*args):
    outs = [shape(128, 2048), shape(128, 2048), shape(8, 16, 3, 8, 128), shape(8, 8, 16, 8, 128),
            shape(8, 12, 8, 128), shape(8, 8, 4, 8, 128)]
    low = [DMA((8,)), DMA((8,))]
    sums = [DMA((10,)), DMA((10,))]
    gather = GroupGather.SEMS
    kinds = [DMA((8,)), DMA((8,)), DMA((4,)), *Swap.sems(11), *PlaneGather.SEMS * 4, *gather, *gather, *low, *sums,
             *gather, *low, *low, *sums, *low, *low, *low, *gather, *Spread.SCRATCH, *sums, *low, *sums, *low,
             *LastSpread.SCRATCH, *Swap.sems(5)]
    return pl.pallas_call(
        block_kernel, out_shape=outs, in_specs=specs(pltpu.SMEM, *[ANY] * 22), out_specs=specs(*[ANY] * 6),
        scratch_shapes=[VMEM(*s) for s in SCRATCH.values()] + kinds,
        compiler_params=params(1, 60), name="block")(*args)


def write_kernel(split, whole, split2, whole2, back, layer, *outs):
    joined_out, dense_in, up_out, down_in, *wholes, grad, out = outs
    for ref, count, first in ((dense_in, 2, 0), (up_out, 8, 2), (down_in, 8, 10)):
        for n in range(count):
            for half in (0, 1):
                k = 2 * (first + n) + half
                ref[:, half * 8:half * 8 + 8, n * 128:n * 128 + 128] = split[:, k // 3, k % 3].astype(F32)
    for n in range(6):
        for half in (0, 1):
            joined_out[:, half * 8:half * 8 + 8, n * 128:n * 128 + 128] = split2[:, 2 * n + half].astype(F32)
    for i, ref in enumerate(wholes):
        for t in range(8):
            for n in range(2):
                for half in (0, 1):
                    at = t * 256 + n * 128
                    k = n * 2 + half
                    block_in = whole2[:, t, k] if i == 0 else whole[:, t, i * 4 + k]
                    ref[:, half * 8:half * 8 + 8, at:at + 128] = block_in.astype(F32)
    grad[...] = back[...].astype(F32)
    out[...] = layer[...]


def write_call(split, whole, split2, whole2, back, layer):
    widths = [768, 256, 1024, 1024] + [2048] * 4
    rows = pl.BlockSpec((32, 2048), lambda b: (b, 0))
    return pl.pallas_call(
        write_kernel, grid=(4,),
        out_shape=[shape(8, 16, n, dtype=F32) for n in widths] + [shape(128, 2048, dtype=F32), shape(128, 2048)],
        in_specs=[pl.BlockSpec((2, *n, 8, 128), lambda b, n=n: (b, *[0] * len(n), 0, 0)) for n in ((16, 3), (8, 16), (12,), (8, 4))
                  ] + [rows, rows],
        out_specs=[pl.BlockSpec((2, 16, n), lambda b: (b, 0, 0)) for n in widths] + [rows, rows],
        compiler_params=plain(58), name="write")(split, whole, split2, whole2, back, layer)


def local(tokens, grad_out, adapter_ids, first_gain, first_shift, joined_weight, joined_bias, dense_weight,
          dense_bias, second_gain, second_shift, up_weight, up_bias, down_weight, down_bias, joined_adapt_in,
          joined_adapt_out, dense_adapt_in, dense_adapt_out, up_adapt_in, up_adapt_out, down_adapt_in,
          down_adapt_out):
    turn = lambda a: jnp.swapaxes(a, 1, 2)
    flat = lambda a: a.reshape(128, a.shape[2])
    vectors = [a.reshape(1, -1) for a in (first_gain, first_shift, second_gain, second_shift, dense_bias, down_bias,
                                          up_bias)] + [joined_bias]
    adapters = dict(joined_in=turn(joined_adapt_in), joined_out=joined_adapt_out, dense_in=turn(dense_adapt_in),
                    dense_out=dense_adapt_out, up_in=turn(up_adapt_in), up_out=up_adapt_out,
                    down_in=turn(down_adapt_in), down_out=down_adapt_out)
    back, layer, split, whole, split2, whole2 = block_call(
        adapter_ids, tokens, grad_out, *vectors, *[flat(adapters[n]) for n in SETS], joined_weight, dense_weight,
        down_weight, up_weight)
    joined_out, dense_in, up_out, down_in, joined_in, dense_out, up_in, down_out, grad_tokens, layer_out = write_call(
        split, whole, split2, whole2, back, layer)
    return (layer_out, grad_tokens, turn(joined_in), joined_out, turn(dense_in), dense_out, turn(up_in), up_out,
            turn(down_in), down_out)


def solution(mesh):
    fine = Mesh(mesh.devices.reshape(2, 4, 2, 2, 4), AXES)
    rows, cols = P(FSDP, TP), P(TP, FSDP)
    tok = P((*FSDP, *TP), None)
    last, middle, one = P(None, None, TP), P(None, TP, None), P(TP)
    return jax.shard_map(
        local, mesh=fine,
        in_specs=(tok, tok, P(FSDP), P(), P(), rows, one, cols, P(), P(), P(), rows, one, cols, P(), P(), last,
                  middle, P(), P(), last, middle, P()),
        out_specs=(tok, tok, P(), last, middle, P(), P(), last, middle, P()), check_vma=False)
```

```python
import functools

import jax
import jax.numpy as jnp
from jax import lax
from jax.experimental import pallas as pl
from jax.experimental.pallas import tpu as pltpu
from jax.sharding import Mesh
from jax.sharding import PartitionSpec as P

HEADS = 32
EPSILON = 1e-05
MASKED = -1e30
AXES = ("xl", "y", "c", "xh", "z")
FSDP = ("xl", "y", "c")
TP = ("xh", "z")
PLANE = ("xl", "y", "xh")
MESH_ID = pl.DeviceIdType.MESH
ANY = pl.ANY
VMEM = pltpu.VMEM
DMA = pltpu.SemaphoreType.DMA
F32 = jnp.float32
BF16 = jnp.bfloat16
ORDER = (0, 3, 1, 2)
PICKS = dict(hot=(0, 128), joined_out=(128, 768), up_out=(896, 1024), dense_in=(1920, 256), down_in=(2176, 1024),
             joined_in=(3200, 2048), up_in=(5248, 2048), dense_out=(7296, 2048), down_out=(9344, 2048))
TRADED = 3200
PICKED = 11392


def remote(src, dst, sems, index, device):
    send, recv = sems
    return pltpu.make_async_remote_copy(
        src_ref=src, dst_ref=dst, send_sem=send.at[index], recv_sem=recv.at[index],
        device_id=device, device_id_type=MESH_ID)


def places():
    return tuple(lax.axis_index(a) for a in AXES)


def at_home():
    _, _, c, xh, _ = places()
    return 1 - (xh - c) * (xh - c)


def meet(peers):
    barrier = pltpu.get_barrier_semaphore()
    for p in peers:
        pl.semaphore_signal(barrier, inc=1, device_id=p, device_id_type=MESH_ID)
    pl.semaphore_wait(barrier, len(peers))


def group_peer(n):
    _, _, c, _, z = places()
    return {"c": lax.rem(c + n // 4, 2), "z": lax.rem(z + n % 4, 4)}


def group_peers():
    return [group_peer(n) for n in range(1, 8)]


def diagonal():
    _, _, c, xh, _ = places()
    return {"c": 1 - c, "xh": 1 - xh}


def plane_peers():
    xl, y, c, xh, _ = places()
    peers = []
    for d in range(1, 4):
        for core in (0, 1):
            peers.append({"y": lax.rem(y + d, 4), "c": core})
            x = lax.rem(xh * 2 + xl + d, 4)
            peers.append({"xh": x // 2, "xl": lax.rem(x, 2), "c": core})
    return peers


def block(ref, n, size=128):
    return ref.at[pl.ds(pl.multiple_of(n * size, size), size)]


def loop(count, body, first=0):
    def run(i, carry):
        body(i)
        return carry

    lax.fori_loop(first, count, run, 0)


class GroupGather:
    SEMS = [DMA((8, 4)), DMA((8, 4))]

    def __init__(self, dst, send, recv):
        self.dst, self.sems = dst, (send, recv)
        _, _, self.c, _, self.z = places()
        self.up, self.down, self.other = group_peer(1), group_peer(3), group_peer(4)

    def at(self, core, z, j):
        return self.dst.at[pl.ds(pl.multiple_of((core * 4 + z) * 128 + j * 32, 32), 32)]

    def copy(self, z, j, kind, device):
        ref = self.at(self.c, z, j)
        return remote(ref, ref, self.sems, (kind, j), device)

    def put(self, j):
        self.copy(self.z, j, 0, self.up).start()
        self.copy(self.z, j, 1, self.down).start()
        self.copy(self.z, j, 2, self.other).start()

    def near(self, j):
        below, above = lax.rem(self.z + 3, 4), lax.rem(self.z + 1, 4)
        self.copy(below, j, 0, self.up).wait_recv()
        if j < 2:
            self.copy(below, j, 3, self.up).start()
        self.copy(below, j, 5, self.other).start()
        self.copy(above, j, 1, self.down).wait_recv()
        if j >= 2:
            self.copy(above, j, 4, self.down).start()
        self.copy(above, j, 6, self.other).start()

    def far(self, j):
        opposite = lax.rem(self.z + 2, 4)
        self.copy(opposite, j, 3 if j < 2 else 4, self.up).wait_recv()
        self.copy(opposite, j, 7, self.other).start()

    def shared(self, kind):
        loop(4, lambda j: self.copy(self.z, j, kind, self.other).wait_recv())

    def finish(self):
        def end(j):
            for kind in (0, 1, 2, 3 + j // 2, 5, 6, 7):
                self.copy(self.z, j, kind, self.other).wait_send()

        loop(4, end)


class LowGather:
    SEMS = [DMA((8,)), DMA((8,))]

    def __init__(self, dst, send, recv):
        self.dst, self.sems = dst, (send, recv)
        _, _, c, _, z = places()
        self.own = pl.ds(pl.multiple_of((c * 4 + z) * 128, 128), 128)

    def copy(self, n):
        ref = self.dst.at[:, self.own]
        return remote(ref, ref, self.sems, (n,), group_peer(n))

    def start(self, value):
        self.dst[:, self.own] = value
        loop(8, lambda n: self.copy(n).start(), 1)

    def wait(self):
        loop(8, lambda n: self.copy(n).wait(), 1)


class LowSum:
    SEMS = [DMA((8,)), DMA((8,))]

    def __init__(self, src, got, send, recv):
        self.src, self.got, self.sems = src, got, (send, recv)
        _, _, self.c, _, self.z = places()

    def copy(self, n):
        p = group_peer(n)
        cols = pl.ds(pl.multiple_of((p["c"] * 4 + p["z"]) * 128, 128), 128)
        return remote(self.src.at[:, cols], self.got.at[n], self.sems, (n,), p)

    def start(self):
        loop(8, lambda n: self.copy(n).start(), 1)

    def total(self):
        loop(8, lambda n: self.copy(n).wait(), 1)
        own = pl.ds(pl.multiple_of((self.c * 4 + self.z) * 128, 128), 128)
        out = self.src[:, own].astype(F32)
        for n in range(1, 8):
            out = out + self.got[n].astype(F32)
        return out.astype(BF16)


class PlaneGather:
    SEMS = [DMA((1,)), DMA((41,)), DMA((16, 2))]

    def __init__(self, src, dst, by_rows, local_sem, send, recv):
        self.src, self.dst, self.by_rows, self.local_sem, self.sems = src, dst, by_rows, local_sem, (send, recv)
        self.xl, self.y, self.c, self.xh, _ = places()
        self.x = self.xh * 2 + self.xl
        self.home = at_home()
        r = lax.rem(self.x - 2 * self.c + 4, 4)
        self.odd = 1 - lax.rem(r, 2)
        self.even = lax.rem(r, 2)
        self.away = lax.rem(r - self.odd + 4, 4)

    def whole(self, xl, y, core):
        k = (xl * 4 + y) * 2 + core
        if self.by_rows:
            return block(self.dst, k)
        return self.dst.at[:, pl.ds(pl.multiple_of(k * 128, 128), 128)]

    def half(self, ref, h):
        n = ref.shape[0] // 2
        return ref.at[pl.ds(pl.multiple_of(h * n, n), n)]

    def copy(self, place, h, n, device, src=None):
        xl, y, core = place
        send, recv = self.sems
        dst = self.half(self.whole(*place), h)
        return pltpu.make_async_remote_copy(
            src_ref=dst if src is None else self.half(src, h), dst_ref=dst, send_sem=send.at[n],
            recv_sem=recv.at[(xl * 4 + y) * 2 + core, h], device_id=device, device_id_type=MESH_ID)

    def arrived(self, place, h):
        self.copy(place, h, 0, {"c": 1 - self.c}).wait_recv()

    def arrived_whole(self, place):
        loop(2, lambda h: self.arrived(place, h))

    def chip(self, dx, dy, core):
        x = lax.rem(self.x + dx, 4)
        return {"xh": x // 2, "xl": lax.rem(x, 2), "y": lax.rem(self.y + dy, 4), "c": core}

    def both_ways(self, place, n, along_x, along_y, core, src=None):
        def send(i):
            d = 1 + 2 * lax.rem(i, 2)
            h = lax.rem(i + i // 2, 2)
            self.copy(place, h, n + i, self.chip(along_x * d, along_y * d, core), src).start()

        loop(4, send)

    def local(self):
        return pltpu.make_async_copy(self.src, self.whole(self.xl, self.y, self.c), self.local_sem.at[0])

    def start(self):
        place = (self.xl, self.y, self.c)

        @pl.when(self.home == 1)
        def _():
            self.local().start()

        self.both_ways(place, 0, 1 - self.c, self.c, self.xh, self.src)

        @pl.when(self.home == 0)
        def _():
            loop(2, lambda h: self.copy(place, h, 39 + h, {"c": 1 - self.c}, self.src).start())

    def row(self, d):
        return lax.rem(self.y + d, 4)

    def along_y(self, e):
        self.both_ways((e, self.y, 0), 4 + 4 * e, 0, 1, self.c)

    def along_x(self, d):
        self.both_ways((self.xl, self.row(d), 1), 23 + 4 * d, 1, 0, self.c)

    def step(self, n):
        if n == 0:
            @pl.when(self.home == 1)
            def _():
                self.local().wait()
                self.arrived_whole((self.xl, self.y, 1 - self.c))
                self.along_y(self.xl)
                self.along_x(0)
        elif n == 1:
            place, h = (self.odd, self.y, 0), self.away // 2
            self.arrived(place, h)
            self.copy(place, h, 12, self.chip(self.away, 0, self.c)).start()

            @pl.when(self.home == 1)
            def _():
                def pass_y(k):
                    place = (self.xl, self.row(3 - 2 * k), 1)
                    self.arrived(place, k)
                    self.copy(place, k, 21 + k, self.chip(0, 1 + 2 * k, self.c)).start()

                loop(2, pass_y)
        elif n == 2:
            self.arrived((self.odd, self.y, 0), 1 - self.away // 2)
            self.along_y(self.odd)

            @pl.when(self.home == 1)
            def _():
                def spread(k):
                    self.arrived((self.xl, self.row(3 - 2 * k), 1), 1 - k)
                    self.along_x(3 - 2 * k)

                loop(2, spread)
        elif n == 3:
            @pl.when(self.home == 0)
            def _():
                self.arrived_whole((self.even, self.y, 0))
                self.along_y(self.even)

            @pl.when(self.home == 1)
            def _():
                self.arrived_whole((self.xl, self.row(2), 1))
                self.along_x(2)
        elif n == 4:
            def pass_on(i):
                e, k = i // 2, lax.rem(i, 2)
                place = (e, self.row(3 - 2 * k), 0)
                self.arrived(place, k)
                self.copy(place, k, 13 + i, self.chip(0, 1 + 2 * k, self.c)).start()

            loop(4, pass_on)
        else:
            def pass_on(i):
                k = i * (3 if n == 5 else 1) + (n - 5)
                place, h = (self.odd, self.row(k), 1), self.away // 2
                self.arrived(place, h)
                self.copy(place, h, 17 + k, self.chip(self.away, 0, self.c)).start()

            loop(2, pass_on)

    def wait(self):
        def rows(e):
            loop(2, lambda k: self.arrived((e, self.row(3 - 2 * k), 0), 1 - k))
            self.arrived_whole((e, self.row(2), 0))

        loop(2, rows)
        loop(4, lambda y: self.arrived((self.odd, y, 1), 1 - self.away // 2))

        @pl.when(self.home == 0)
        def _():
            loop(4, lambda y: self.arrived_whole((self.even, y, 1)))

    def finish(self):
        sent = lambda n: self.copy((0, 0, 0), 0, n, {"c": 1 - self.c}).wait_send()
        loop(21, sent)

        @pl.when(self.home == 1)
        def _():
            loop(39, sent, 21)

        @pl.when(self.home == 0)
        def _():
            loop(41, sent, 39)


class GroupSum:
    NAMES = ("far_up", "far_down", "up_high", "down_low", "up_low", "down_high")
    SCRATCH = [VMEM((1024, 2048), BF16), VMEM((4, 128, 2048), BF16), VMEM((3, 128, 2048), BF16),
               VMEM((2, 64, 2048), BF16), VMEM((2, 128, 2048), BF16), DMA((10,)), DMA((10,))]

    def __init__(self, parts, near, sent, half, full, send, recv):
        self.parts, self.near, self.sent, self.half, self.full, self.sems = parts, near, sent, half, full, (send, recv)
        _, _, self.c, _, self.z = places()
        self.up, self.down, self.other = group_peer(1), group_peer(3), group_peer(4)
        self.order = [lax.rem(self.z + d, 4) for d in (2, 1, 3, 0)]

    def part(self, core, i):
        return block(self.parts, core * 4 + self.order[i])

    def given(self, i):
        return remote(self.part(1 - self.c, i), self.near.at[i], self.sems, (i,), self.other)

    def give_from(self, i, at):
        remote(block(self.parts, (1 - self.c) * 4 + at), self.near.at[i], self.sems, (i,), self.other).start()

    def give(self, i):
        self.given(i).start()

    def pair(self, i, rows=slice(None)):
        return self.part(self.c, i)[rows].astype(F32) + self.near[i, rows].astype(F32)

    def piece(self, name):
        low, high = pl.ds(0, 64), pl.ds(64, 64)
        n = self.NAMES.index(name)
        src = (self.sent.at[0, low], self.sent.at[0, high], self.sent.at[1, high], self.sent.at[2, low],
               self.sent.at[1, low], self.sent.at[2, high])[n]
        dst = (self.half.at[0], self.half.at[1], self.full.at[0, high], self.full.at[1, low],
               self.full.at[0, low], self.full.at[1, high])[n]
        return remote(src, dst, self.sems, (4 + n,), (self.up, self.down)[n % 2])

    def far(self):
        self.given(0).wait_recv()
        self.sent[0] = self.pair(0).astype(BF16)
        self.piece("far_up").start()
        self.piece("far_down").start()

    def near_up(self):
        self.given(1).wait_recv()
        self.sent[1, pl.ds(64, 64)] = self.pair(1, pl.ds(64, 64)).astype(BF16)
        self.piece("up_high").start()

    def near_down(self):
        self.given(2).wait_recv()
        self.sent[2, pl.ds(0, 64)] = self.pair(2, pl.ds(0, 64)).astype(BF16)
        self.piece("down_low").start()

    def pass_on(self):
        low, high = pl.ds(0, 64), pl.ds(64, 64)
        self.piece("far_up").wait_recv()
        self.sent[1, low] = (self.pair(1, low) + self.half[0].astype(F32)).astype(BF16)
        self.piece("up_low").start()
        self.piece("far_down").wait_recv()
        self.sent[2, high] = (self.pair(2, high) + self.half[1].astype(F32)).astype(BF16)
        self.piece("down_high").start()

    def arrive(self):
        self.given(3).wait_recv()
        for name in ("up_high", "down_low", "up_low", "down_high"):
            self.piece(name).wait_recv()

    def total(self, rows=slice(None)):
        return self.pair(3, rows) + self.full[0, rows].astype(F32) + self.full[1, rows].astype(F32)

    def finish(self):
        for name in self.NAMES:
            self.piece(name).wait_send()
        for i in range(4):
            self.given(i).wait_send()


def params(cid, mib):
    return pltpu.CompilerParams(collective_id=cid, has_side_effects=True, vmem_limit_bytes=mib << 20)


def plain(mib):
    return pltpu.CompilerParams(vmem_limit_bytes=mib << 20)


def shape(*dims, dtype=BF16):
    return jax.ShapeDtypeStruct(dims, dtype)


def specs(*spaces):
    return [pl.BlockSpec(memory_space=s) for s in spaces]


def layer_norm(rows_in, gain, shift):
    row_mean = jnp.mean(rows_in, axis=-1, keepdims=True)
    centered = rows_in - row_mean
    variance = jnp.mean(centered * centered, axis=-1, keepdims=True)
    return centered * lax.rsqrt(variance + EPSILON) * gain + shift


def norm_back(rows_in, gain, grad):
    row_mean = jnp.mean(rows_in, axis=-1, keepdims=True)
    centered = rows_in - row_mean
    inverse = lax.rsqrt(jnp.mean(centered * centered, axis=-1, keepdims=True) + EPSILON)
    n = centered * inverse
    e = gain * grad
    return (e - jnp.mean(e, axis=-1, keepdims=True) - n * jnp.mean(e * n, axis=-1, keepdims=True)) * inverse


def dot(a, b, dims=((1,), (0,))):
    return lax.dot_general(a, b, (dims, ((), ())), preferred_element_type=F32)


def dot_t(a, b):
    return dot(a, b, ((1,), (1,)))


def dot_o(a, b):
    return dot(a, b, ((0,), (0,)))


def tiles(count, size, body):
    def run(i, carry):
        body(pl.ds(pl.multiple_of(i * size, size), size))
        return carry

    lax.fori_loop(0, count, run, 0)


def split_refs(refs, *counts):
    refs, out = list(refs), []
    for n in counts:
        out.append(refs[:n])
        refs = refs[n:]
    return (*out, refs)


def pick(ref, name):
    first, n = PICKS[name]
    return ref[:, pl.ds(first, n)]


def row_pair(z):
    return (pl.ds(pl.multiple_of(z * 128, 128), 128), pl.ds(pl.multiple_of(512 + z * 128, 128), 128))


def take_pair(ref, z, cols=slice(None)):
    a, b = row_pair(z)
    return jnp.concatenate([ref[a, cols], ref[b, cols]], axis=0)


def put_pair(ref, z, value, cols=slice(None)):
    a, b = row_pair(z)
    ref[a, cols] = value[:128]
    ref[b, cols] = value[128:]


class Swap:
    def __init__(self, pairs, local, send, recv):
        self.pairs, self.local, self.sems, self.home = pairs, local, (send, recv), at_home()

    def near_copy(self, n):
        src, _, dst = self.pairs[n]
        return pltpu.make_async_copy(src, dst, self.local.at[n])

    def far_copy(self, n):
        src, dst, _ = self.pairs[n]
        return remote(src, dst, self.sems, (n,), diagonal())

    def start(self, n):
        @pl.when(self.home == 1)
        def _():
            self.near_copy(n).start()

        @pl.when(self.home == 0)
        def _():
            self.far_copy(n).start()

    def wait(self, n):
        @pl.when(self.home == 1)
        def _():
            self.near_copy(n).wait()

        @pl.when(self.home == 0)
        def _():
            self.far_copy(n).wait_recv()

    def finish(self):
        @pl.when(self.home == 0)
        def _():
            for n in range(len(self.pairs)):
                self.far_copy(n).wait_send()

    @staticmethod
    def sems(n):
        return [DMA((n,)), DMA((n,)), DMA((n,))]


class Spread:
    SCRATCH = [VMEM((16, 5, 8, 128), BF16), VMEM((16, 5, 8, 128), BF16), VMEM((8, 3, 8, 128), BF16),
               VMEM((8, 8, 128), BF16), DMA((16,)), DMA((16,)), DMA((9,)), DMA((16,)), DMA((20,)), DMA((20,)), DMA((2,))]

    def __init__(self, split, whole, send, got, part, full, one_send, one_recv, two_send, two_recv, send3, recv3, local):
        self.split, self.whole, self.send, self.got, self.part, self.full = split, whole, send, got, part, full
        self.one, self.two, self.three, self.local = (one_send, one_recv), (two_send, two_recv), (send3, recv3), local
        self.xl, self.y, self.c, self.xh, self.z = places()
        self.q = (self.xh * 2 + self.xl) * 4 + self.y
        self.home = at_home()

    def put(self, n, value):
        for m in range(4):
            k = 2 * n + m
            where = (k // 3, k % 3) if k < 48 else (k - 48, 3)
            row, col = m % 2 * 8, m // 2 * 128
            self.send[where] = value[row:row + 8, col:col + 128].astype(BF16)

    def mark(self, hot):
        for j in range(16):
            self.send[j, 4] = hot

    def chip(self, n):
        q = lax.rem(self.q + n, 16)
        x = q // 4
        return q, {"xh": x // 2, "xl": lax.rem(x, 2), "y": lax.rem(q, 4)}

    def to_owner(self, n):
        q, device = self.chip(n)
        return remote(self.send.at[q], self.got.at[n], self.one, (n,), device)

    def start(self):
        loop(16, lambda n: self.to_owner(n).start(), 1)

    def add(self):
        self.got[0] = self.send[self.q]
        loop(16, lambda n: self.to_owner(n).wait_recv(), 1)
        for b in range(8):
            def more(n, total, b=b):
                return total + self.got[n, 0:4].astype(F32) * self.got[n, 4].astype(F32)[b:b + 1]

            total = lax.fori_loop(0, 16, more, jnp.zeros((4, 8, 128), F32)).astype(BF16)
            self.part[b] = total[:3]
            self.full[b] = total[3]

    def copy_to_groups(self, slot, i):
        device = {"xh": self.c, "xl": lax.rem(self.xl + i // 4, 2), "y": lax.rem(self.y + lax.rem(i, 4), 4)}
        send, recv = self.two
        return pltpu.make_async_remote_copy(
            src_ref=self.part, dst_ref=self.split.at[:, slot], send_sem=send.at[i],
            recv_sem=recv.at[self.q], device_id=device, device_id_type=MESH_ID)

    def split_copy(self, i):
        return self.copy_to_groups(self.q, i)

    def split_own(self):
        return pltpu.make_async_copy(self.part, self.split.at[:, self.q], self.local.at[0])

    def whole_own(self):
        return pltpu.make_async_copy(self.full, self.whole.at[:, self.c * 4 + self.z, self.q], self.local.at[1])

    def line_copies(self):
        where = self.whole.at[:, self.c * 4 + self.z, self.q]
        return [remote(self.full, where, self.three, (d,), {"z": lax.rem(self.z + d, 4)}) for d in (1, 2, 3)]

    def plane_copy(self, n):
        where = self.whole.at[:, pl.ds(self.c * 4, 4), self.q]
        return remote(where, where, self.three, (4 + n,), self.chip(n)[1])

    def shared_whole(self):
        where = self.whole.at[:, pl.ds(self.c * 4, 4)]
        return remote(where, where, self.three, (0,), {"c": 1 - self.c})

    def shared_split(self):
        send, recv = self.two
        return pltpu.make_async_remote_copy(
            src_ref=self.split, dst_ref=self.split, send_sem=send.at[8], recv_sem=recv.at[0],
            device_id={"c": 1 - self.c}, device_id_type=MESH_ID)

    def deal_groups(self):
        @pl.when(self.home == 1)
        def _():
            self.split_own().start()

        @pl.when(self.home == 0)
        def _():
            self.split_copy(0).start()

        loop(8, lambda i: self.split_copy(i).start(), 1)

    def deal(self):
        self.whole_own().start()
        for copy in self.line_copies():
            copy.start()
        self.deal_groups()

    def deal_plane(self):
        self.whole_own().wait()
        for copy in self.line_copies():
            copy.wait_recv()
        loop(16, lambda n: self.plane_copy(n).start(), 1)

    def wait_groups(self, count):
        send, recv = self.two
        def wait(q):
            @pl.when(self.q != q)
            def _():
                pltpu.make_async_remote_copy(
                    src_ref=self.part, dst_ref=self.split.at[:, q], send_sem=send.at[0], recv_sem=recv.at[q],
                    device_id={"c": 1 - self.c}, device_id_type=MESH_ID).wait_recv()

        loop(count, wait)

    def share(self):
        @pl.when(self.home == 1)
        def _():
            self.split_own().wait()
            self.wait_groups(16)
            self.shared_split().start()

        loop(16, lambda n: self.plane_copy(n).wait_recv(), 1)
        self.shared_whole().start()

    def finish_shares(self):
        self.shared_whole().wait()

        @pl.when(self.home == 1)
        def _():
            self.shared_split().wait_send()

        @pl.when(self.home == 0)
        def _():
            self.shared_split().wait_recv()

    def finish_groups(self):
        @pl.when(self.home == 0)
        def _():
            self.split_copy(0).wait_send()

        loop(8, lambda i: self.split_copy(i).wait_send(), 1)

    def finish(self):
        self.finish_shares()
        self.finish_groups()
        for copy in self.line_copies():
            copy.wait_send()

        def end(n):
            self.plane_copy(n).wait_send()
            self.to_owner(n).wait_send()

        loop(16, end, 1)


class LastSpread(Spread):
    SCRATCH = [VMEM((16, 2, 8, 128), BF16), VMEM((16, 2, 8, 128), BF16), VMEM((8, 8, 128), BF16),
               DMA((16,)), DMA((16,)), DMA((9,)), DMA((16,)), DMA((20,)), DMA((20,)), DMA((2,))]

    def __init__(self, split, whole, send, got, part, *sems):
        super().__init__(split, whole, send, got, part, part, *sems)

    def put(self, n, value):
        for m in range(4):
            row, col = m % 2 * 8, m // 2 * 128
            self.send[2 * n + m, 0] = value[row:row + 8, col:col + 128].astype(BF16)

    def mark(self, hot):
        for j in range(16):
            self.send[j, 1] = hot

    def add(self):
        self.got[0] = self.send[self.q]
        loop(16, lambda n: self.to_owner(n).wait_recv(), 1)
        for b in range(8):
            def more(n, total, b=b):
                return total + self.got[n, 0].astype(F32) * self.got[n, 1].astype(F32)[b:b + 1]

            self.part[b] = lax.fori_loop(0, 16, more, jnp.zeros((8, 128), F32)).astype(BF16)

    def split_copy(self, i):
        return self.copy_to_groups(lax.rem(self.q, 12), i)

    def split_own(self):
        return pltpu.make_async_copy(self.part, self.split.at[:, lax.rem(self.q, 12)], self.local.at[0])

    def late(self):
        return lax.rem(self.q, 4)

    def whole_own(self):
        return pltpu.make_async_copy(self.part, self.whole.at[:, self.c * 4 + self.z, self.late()], self.local.at[1])

    def line_copies(self):
        where = self.whole.at[:, self.c * 4 + self.z]
        return [remote(where, where, self.three, (d,), {"z": lax.rem(self.z + d, 4)}) for d in (1, 2, 3)]

    def plane_copy(self, n):
        where = self.whole.at[:, self.c * 4 + self.z, self.late()]
        return remote(self.part, where, self.three, (4 + n,), self.chip(n)[1])

    def deal(self):
        @pl.when(self.q >= 12)
        def _():
            self.whole_own().start()
            loop(16, lambda n: self.plane_copy(n).start(), 1)

        @pl.when(self.q < 12)
        def _():
            self.deal_groups()

    def share_groups(self):
        @pl.when(self.home == 1)
        def _():
            @pl.when(self.q < 12)
            def _():
                self.split_own().wait()

            self.wait_groups(12)
            self.shared_split().start()

    def line(self):
        @pl.when(self.q >= 12)
        def _():
            self.whole_own().wait()

        def late(n):
            @pl.when(lax.rem(self.q - n + 16, 16) >= 12)
            def _():
                self.plane_copy(n).wait_recv()

        loop(16, late, 1)

        for copy in self.line_copies():
            copy.start()

    def share_line(self):
        for copy in self.line_copies():
            copy.wait_recv()
        self.shared_whole().start()

    def finish(self):
        self.finish_shares()

        @pl.when(self.q < 12)
        def _():
            self.finish_groups()

        @pl.when(self.q >= 12)
        def _():
            loop(16, lambda n: self.plane_copy(n).wait_send(), 1)

        for copy in self.line_copies():
            copy.wait_send()
        loop(16, lambda n: self.to_owner(n).wait_send(), 1)


def far_peers():
    xl, y, _, xh, _ = places()
    peers = []
    for d in range(1, 4):
        x = lax.rem(xh * 2 + xl + d, 4)
        for e in range(1, 4):
            peers.append({"xh": x // 2, "xl": lax.rem(x, 2), "y": lax.rem(y + e, 4)})
    return peers


ROOT_HALF = 0.7071067811865476
ROOT_TAU = 0.3989422804014327
SETS = dict(joined_in=(0, 0), up_in=(128, 0), dense_out=(256, 0), down_out=(384, 0), up_out=(512, 0),
            down_in=(512, 1024), joined_out=(640, 0), dense_in=(640, 768))


def cast_parts(value):
    high = value.astype(BF16).astype(F32)
    middle = (value - high).astype(BF16).astype(F32)
    return high, middle, value - high - middle


def block_kernel(*refs):
    (ids, tokens, go, *vectors), adapters, shards, outs, scratch = split_refs(refs, 11, 8, 4, 6)
    back, out, split, whole, split2, whole2 = outs
    names = list(SCRATCH)
    v = dict(zip(names, scratch))
    rest = list(scratch[len(names):])

    def sems(n):
        taken = rest[:n]
        del rest[:n]
        return taken

    load_sem, vector_sem, copy_sem = sems(3)
    xl, y, c, xh, z = places()
    own = c * 4 + z
    mine_rows = pl.ds(pl.multiple_of(own * 128, 128), 128)
    there_rows = (1 - c) * 4 + z
    gain1, shift1, gain2, shift2, bias_d, bias_n = (v["lines"].at[n:n + 1] for n in range(6))
    pk, xs, xbuf, gbuf = v["pk"], v["xs"], v["xbuf"], v["gbuf"]
    sets = v["parts"]
    loads = {}
    for n, (name, ref) in enumerate(zip(SETS, adapters)):
        row, col = SETS[name]
        loads[name] = pltpu.make_async_copy(ref, sets.at[pl.ds(row, 128), pl.ds(col, ref.shape[1])], load_sem.at[n])
        loads[name].start()
    lines = [pltpu.make_async_copy(ref, v["lines"].at[n:n + 1], vector_sem.at[n]) for n, ref in enumerate(vectors[:6])]
    for line in lines:
        line.start()
    meet(plane_peers() + group_peers() + far_peers())

    bias = v["bias"]
    mine = v["mine"]
    piece = lambda who, j: gbuf.at[pl.ds(pl.multiple_of(who * 128 + j * 32, 32), 32)]
    sub = lambda ref, j: ref.at[pl.ds(j * 32, 32)]
    pairs = [(sub(tokens, j), sub(xs, j), sub(xs, j)) for j in range(4)]
    pairs += [(m, p, p) for m, p in ((mine, pk.at[:, :TRADED]), (vectors[7], v["bias_one"]), (vectors[6], bias))]
    pairs += [(sub(go, j), piece(there_rows, j), piece(own, j)) for j in range(4)]
    sw = Swap(pairs, *sems(3))
    for j in ORDER:
        sw.start(j)
    joined = PlaneGather(shards[0], v["wj"], True, *sems(3))
    dense = PlaneGather(shards[1], v["wd"], False, *sems(3))
    down = PlaneGather(shards[2], v["wn"], False, *sems(3))
    up = PlaneGather(shards[3], v["wu"], True, *sems(3))
    joined.start()
    set_id = ids[0]
    for name in ("joined_out", "up_out", "dense_in", "down_in"):
        (row, col), (first, n) = SETS[name], PICKS[name]
        loads[name].wait()
        chosen = sets[row:row + 16, col:col + n]
        for k in range(1, 8):
            chosen = jnp.where(set_id == k, sets[row + k * 16:row + k * 16 + 16, col:col + n], chosen)
        mine[:, first:first + n] = chosen
    first, n = PICKS["hot"]
    mine[:, first:first + n] = jnp.where(lax.broadcasted_iota(jnp.int32, (16, 128), 0) == set_id, 1.0, 0.0).astype(BF16)
    for n in (4, 5, 6):
        sw.start(n)
    for line in lines:
        line.wait()
    g1 = GroupGather(xbuf, *sems(2))
    for j in ORDER:
        sw.wait(j)
        x1 = layer_norm(xs[j * 32:(j + 1) * 32].astype(F32), gain1[...], shift1[...])
        xbuf[pl.ds(pl.multiple_of(own * 128 + j * 32, 32), 32)] = x1.astype(BF16)
        g1.put(j)
    dense.start()
    joined.step(0)
    joined.step(1)
    g1.near(0)
    joined.step(2)
    g1.near(3)
    joined.step(3)
    g1.near(1)
    joined.step(4)
    g1.near(2)
    joined.step(5)
    joined.step(6)
    for j in ORDER:
        sw.start(7 + j)
    dense.step(0)
    dense.step(1)
    down.start()
    sw.wait(4)
    for name in ("joined_in", "up_in", "dense_out", "down_out"):
        (row, col), (first, n) = SETS[name], PICKS[name]
        loads[name].wait()
        chosen = jnp.zeros((16, n), F32)
        for k in range(8):
            chosen = chosen + sets[row + k * 16:row + k * 16 + 16, col:col + n].astype(F32) * pk[k:k + 1, 0:1].astype(F32)
        pk[:, first:first + n] = chosen.astype(BF16)

    def low_pair(at):
        low = dot_t(pick(pk, "joined_in"), take_pair(xbuf, at)).astype(BF16)
        for n, rows in enumerate(row_pair(at)):
            v["low_q"][:, rows] = low[:, n * 128:n * 128 + 128]

    g1.shared(2)
    low_pair(z)
    for j in ORDER:
        g1.far(j)
    g1.shared(5)
    low_pair(lax.rem(z + 3, 4))
    g1.shared(6)
    low_pair(lax.rem(z + 1, 4))
    g1.shared(7)
    low_pair(lax.rem(z + 2, 4))
    g2 = GroupGather(gbuf, *sems(2))
    for n in (5, 6):
        sw.wait(n)
    joined.wait()

    lane = lax.broadcasted_iota(jnp.int32, (256, 128), 1)
    row = lax.broadcasted_iota(jnp.int32, (256, 128), 0)
    qa, ka, va = v["qa"], v["ka"], v["va"]

    def project(i, carry):
        rows = pl.ds(pl.multiple_of(i * 256, 256), 256)
        acc = dot(xbuf[rows], v["wj"][...]) + dot_o(v["low_q"][:, rows], pick(pk, "joined_out")) + v["bias_one"][...].reshape(1, 768)
        b = acc.astype(BF16).astype(F32)
        position = (i * 256 + row).astype(F32) * 0.125
        ones = jnp.where(lane < 67, 1.0, 0.0)
        for h in range(4):
            slope = jnp.exp2((own * 4 + h + 1).astype(F32) * (-8.0 / HEADS) + jnp.zeros((1, 128), F32))
            high, middle, lowest = cast_parts(position * slope)
            tail = jnp.where(lane == 64, high, jnp.where(lane == 65, middle, jnp.where(lane == 66, lowest, jnp.where(
                lane < 70, 1.0, 0.0))))
            at = h * 192
            qa[h, rows] = jnp.where(lane < 64, b[:, at:at + 128] * 0.125, ones).astype(BF16)
            ka[h, rows] = jnp.where(lane < 64, b[:, at + 64:at + 192], tail).astype(BF16)
            value = jnp.concatenate([b[:, at + 128:at + 192], b[:, at:at + 64]], axis=1)
            va[h, rows] = jnp.where(lane < 64, value, ones).astype(BF16)
        return carry

    lax.fori_loop(0, 4, project, 0)
    own_cols = pl.ds(pl.multiple_of(own * 256, 256), 256)
    keep = lambda n, ref: pltpu.make_async_copy(ref.at[:, own_cols], v["cols"].at[n], copy_sem.at[n])
    keep(0, xbuf).start()
    for j in ORDER:
        sw.wait(7 + j)
        g2.put(j)

    hooks = [lambda: dense.step(2), lambda: down.step(0), lambda: (dense.step(3), down.step(1)), lambda: g2.near(0), lambda: dense.step(4),
             lambda: g2.near(3), lambda: down.step(2), lambda: g2.near(1), lambda: (dense.step(5), dense.step(6)),
             lambda: g2.near(2), lambda: up.start(), lambda: down.step(3), lambda: (g2.far(0), g2.far(3)),
             lambda: None, lambda: (g2.far(1), g2.far(2)), lambda: down.step(4)]
    mask = lax.broadcasted_iota(jnp.int32, (256, 256), 0) <= lax.broadcasted_iota(jnp.int32, (256, 256), 1)
    line = lax.broadcasted_iota(jnp.int32, (128, 256), 0)
    c4 = v["c4"]

    def head(h, carry):
        for i in range(4):
            rows = pl.ds(i * 256, 256)
            q = qa[h, rows]
            last = jnp.where(mask, dot_t(ka[h, rows], q), MASKED)
            top = jnp.max(last, axis=0, keepdims=True)
            if i:
                before = dot_t(ka[h, pl.ds(0, i * 256)], q)
                top = jnp.maximum(top, jnp.max(before, axis=0, keepdims=True))
            mix = dot_o(va[h, rows], jnp.exp(last - top).astype(BF16))
            if i:
                mix = mix + dot_o(va[h, pl.ds(0, i * 256)], jnp.exp(before - top).astype(BF16))
            total = mix[64:65]
            high, middle, lowest = cast_parts(-(top + jnp.log(total)))
            mix = jnp.where(line == 67, high, jnp.where(line == 68, middle, jnp.where(
                line == 69, lowest, mix / total)))
            turned = mix.T
            c4[h, rows] = turned.astype(BF16)
            qa[h, rows] = jnp.where(lane < 67, q.astype(F32), jnp.where(lane < 70, turned, 0.0)).astype(BF16)
            for k in range(4):
                @pl.when(h == k)
                def _(k=k, i=i):
                    hooks[k * 4 + i]()
        return carry

    lax.fori_loop(0, 4, head, 0)
    ctx = v["ctx"]
    for h in (0, 2):
        ctx[:, h * 64:h * 64 + 128] = jnp.concatenate([c4[h, :, :64], c4[h + 1, :, :64]], axis=1)

    v["gos"][...] = gbuf[mine_rows]

    src, got = v["low_src"], v["low_got"]
    src[0] = dot_t(pick(pk, "dense_in"), ctx[...]).astype(BF16)
    sum_d = LowSum(src.at[0], got.at[0], *sems(2))
    sum_d.start()
    s1 = GroupSum(*[v[n] for n in ("parts", "near", "sent", "half", "full")], *sems(2))
    dense.wait()
    keep(0, xbuf).wait()
    g1.finish()

    def summed(s, compute, before=lambda: None, beside=lambda: None):
        def part(i, carry):
            compute(s, lax.rem(z + 2 - i + 3 * (i // 2) - 2 * (i // 3) + 4, 4))
            s.give_from(i, lax.rem(z + 2 - i + 3 * (i // 2) - 2 * (i // 3) + 4, 4))

            @pl.when(i == 1)
            def _():
                before()
                s.far()

            @pl.when(i == 2)
            def _():
                s.near_up()

            return carry

        lax.fori_loop(0, 4, part, 0)
        s.near_down()
        beside()
        s.pass_on()

    def dense_part(s, at):
        put_pair(s.parts, at, dot(take_pair(ctx, at), v["wd"][...]).astype(BF16))

    def low_tile(rows):
        v["low_g"][:, rows] = dot_t(pick(pk, "down_out"), gbuf[rows]).astype(BF16)

    def beside_dense():
        for kind in (2, 5, 6, 7):
            g2.shared(kind)
        keep(3, gbuf).start()
        down.step(5)
        up.step(0)
        tiles(4, 256, low_tile)
        down.step(6)
        up.step(1)

    summed(s1, dense_part, beside=beside_dense)
    up.step(2)
    mid, dmid, dact = v["mid"], v["dmid"], v["dact"]
    total_d = sum_d.total()
    mid[...] = dot_o(total_d, pick(pk, "dense_out")) + bias_d[...] + xs[...].astype(F32)
    down.wait()

    def grad_act(rows):
        dact[rows] = dot_t(gbuf[rows], v["wn"][...]) + dot_o(v["low_g"][:, rows], pick(pk, "down_in"))

    def grad_acts(i, carry):
        grad_act(pl.ds(pl.multiple_of(i * 256, 256), 256))

        @pl.when(i == 1)
        def _():
            up.step(3)

        return carry

    lax.fori_loop(0, 4, grad_acts, 0)
    up.step(4)
    s1.arrive()
    g3 = GroupGather(xbuf, *sems(2))
    for j in ORDER:
        rows = slice(j * 32, (j + 1) * 32)
        mid[rows] = mid[rows] + s1.total(rows)
        xbuf[pl.ds(pl.multiple_of(own * 128 + j * 32, 32), 32)] = layer_norm(mid[rows], gain2[...], shift2[...]).astype(BF16)
        g3.put(j)
    all_d = LowGather(v["sum_d"], *sems(2))
    all_d.start(total_d)
    up.step(5)
    up.step(6)
    up.wait()
    act, dpre = v["act"], v["dpre"]

    def forward(at):
        x = take_pair(xbuf, at)
        lu = dot_t(pick(pk, "up_in"), x).astype(BF16)
        for n, rows in enumerate(row_pair(at)):
            v["low_u"][:, rows] = lu[:, n * 128:n * 128 + 128]

        def run(n, carry):
            cols = pl.ds(pl.multiple_of(n * 256, 256), 256)
            w = pk[:, pl.ds(pl.multiple_of(PICKS["up_out"][0] + n * 256, 128), 256)]
            b = bias[:, pl.ds(pl.multiple_of(n * 256, 256), 256)]
            pre = dot(x, v["wu"][:, cols]) + dot_o(lu, w) + b
            cdf = 0.5 * (1.0 + lax.erf(pre * ROOT_HALF))
            put_pair(act, at, (pre * cdf).astype(BF16), cols)
            slope = cdf + pre * (jnp.exp(-0.5 * pre * pre) * ROOT_TAU)
            put_pair(dpre, at, (take_pair(dact, at, cols) * slope).astype(BF16), cols)
            return carry

        lax.fori_loop(0, 4, run, 0)

    def by_pairs(g, work, beside=None):
        def run(p, carry):
            @pl.when(p == 0)
            def _():
                g.shared(2)
                if not beside:
                    g.near(0)
                    g.near(3)

            @pl.when(p == 1)
            def _():
                if beside:
                    beside()
                    g.near(0)
                    g.near(3)
                g.near(1)
                g.near(2)
                g.shared(6)

            @pl.when(p == 2)
            def _():
                g.shared(5)

            @pl.when(p == 3)
            def _():
                for j in ORDER:
                    g.far(j)
                g.shared(7)

            work(lax.rem(z + p + p // 2 - 2 * (p // 3), 4))
            return carry

        lax.fori_loop(0, 4, run, 0)

    by_pairs(g3, forward)
    keep(2, xbuf).start()

    sum_u = LowSum(src.at[1], got.at[1], *sems(2))
    s2 = GroupSum(*[v[n] for n in ("parts", "near", "sent", "half", "full")], *sems(2))
    s1.finish()

    def wide(ref, weight):
        def compute(s, at):
            x = take_pair(ref, at)

            def run(n, carry):
                cols = pl.ds(pl.multiple_of(n * 512, 512), 512)
                put_pair(s.parts, at, dot_t(x, weight[cols]).astype(BF16), cols)
                return carry

            lax.fori_loop(0, 4, run, 0)

        return compute

    keep(2, xbuf).wait()
    g3.finish()
    def low_up():
        src[1] = dot_t(pick(pk, "up_out"), dpre[...]).astype(BF16)
        sum_u.start()

    summed(s2, wide(dpre, v["wu"]), beside=low_up)
    for thing in (joined, dense, down, up, sw):
        thing.finish()
    keep(3, gbuf).wait()
    g2.finish()
    mlp = gbuf

    def forward_down(rows):
        mlp[rows] = dot(act[rows], v["wn"][...]).astype(BF16)

    src[2] = dot_t(pick(pk, "down_in"), act[...]).astype(BF16)
    sum_n = LowSum(src.at[2], got.at[2], *sems(2))
    sum_n.start()
    tiles(4, 256, forward_down)
    total_u = sum_u.total()
    dmid[...] = dot_o(total_u, pick(pk, "up_in"))
    all_u = LowGather(v["sum_u"], *sems(2))
    all_u.start(total_u)
    s2.arrive()
    all_n = LowGather(v["sum_n"], *sems(2))
    g4 = GroupGather(xbuf, *sems(2))
    for j in ORDER:
        rows = slice(j * 32, (j + 1) * 32)
        dmid[rows] = v["gos"][rows].astype(F32) + norm_back(mid[rows], gain2[...], dmid[rows] + s2.total(rows))
        xbuf[pl.ds(pl.multiple_of(own * 128 + j * 32, 32), 32)] = dmid[rows].astype(BF16)
        g4.put(j)
    spread = Spread(split, whole, *sems(11))

    def product(first, count, low, ref):
        for n in range(0, count, 2):
            spread.put(first + n, dot(low[...], ref[:, n * 128:n * 128 + 256]))

    def early_products():
        all_n.start(sum_n.total())
        spread.mark(pk[:8, PICKS["hot"][0]:PICKS["hot"][0] + 128])
        product(2, 8, v["low_u"], dpre)
        product(10, 8, v["low_g"], act)
        all_u.wait()
        product(28, 2, v["sum_u"], v["cols"].at[2])

    grads = c4

    def context(at):
        x = take_pair(xbuf, at)
        ld = dot_t(pick(pk, "dense_out"), x).astype(BF16)
        for n, rows in enumerate(row_pair(at)):
            v["low_d"][:, rows] = ld[:, n * 128:n * 128 + 128]
        value = dot_t(x, v["wd"][...]) + dot_o(ld, pick(pk, "dense_in"))
        value = value.astype(BF16).astype(F32)
        mix = take_pair(ctx, at).astype(F32)
        for h in range(4):
            first = h // 2 * 128
            g = value[:, first:first + 128]
            here = (lane // 64) == h % 2
            d = -jnp.sum(jnp.where(here, g * mix[:, first:first + 128], 0.0), axis=-1, keepdims=True)
            high, middle, lowest = cast_parts(d)
            if h % 2:
                g = jnp.concatenate([g[:, 64:], g[:, :64]], axis=1)
            put_pair(grads.at[h], at, jnp.where(lane < 64, g, jnp.where(lane == 64, high, jnp.where(
                lane == 65, middle, jnp.where(lane == 66, lowest, 0.0)))).astype(BF16))

    by_pairs(g4, context, early_products)
    keep(1, xbuf).start()

    s3 = GroupSum(mlp, *[v[n] for n in ("near2", "sent2", "half2", "full2")], *sems(2))
    for i in range(4):
        s3.give(i)
    def dense_products():
        product(0, 2, v["low_d"], ctx)
        all_d.wait()
        keep(1, xbuf).wait()
        product(26, 2, v["sum_d"], v["cols"].at[1])
        all_n.wait()
        product(30, 2, v["sum_n"], v["cols"].at[3])
        spread.start()

    dense_products()
    hooks_back = {0: s3.far, 1: s3.near_up, 2: s3.near_down, 6: spread.add, 7: spread.deal, 8: s3.pass_on,
                  15: spread.deal_plane}
    dk, dv = v["dact"].at[:, 0:128], v["dact"].at[:, 128:256]

    def head_back(h, carry):
        dk[...] = jnp.zeros_like(dk)
        dv[...] = jnp.zeros_like(dv)
        for i in range(4):
            rows = pl.ds(i * 256, 256)
            q, g = qa[h, rows], grads[h, rows]

            def span(keys, masked):
                k = ka[h, keys]
                score = dot_t(k, q)
                if masked:
                    score = jnp.where(mask, score, MASKED)
                p = jnp.exp(score)
                ds = (p * dot_t(va[h, keys], g)).astype(BF16)
                dk[keys] += dot(ds, q)
                dv[keys] += dot(p.astype(BF16), g)
                return dot_o(k, ds)

            dq = span(rows, True)
            if i:
                dq = dq + span(pl.ds(0, i * 256), False)
            grads[h, rows] = (dq * 0.125).T.astype(BF16)
            for n, hook in hooks_back.items():
                if n % 4 == i:
                    @pl.when(h == n // 4)
                    def _(hook=hook):
                        hook()
        ka[h] = dk[...].astype(BF16)
        va[h] = dv[...].astype(BF16)
        return carry

    lax.fori_loop(0, 4, head_back, 0)
    dfused = v["dfused"]
    for h in (0, 2):
        dfused[:, h * 192:h * 192 + 384] = jnp.concatenate(
            [ref[k, :, :64] for k in (h, h + 1) for ref in (grads, ka, va)], axis=1)

    src[3] = dot_t(pick(pk, "joined_out"), dfused[...]).astype(BF16)
    sum_q = LowSum(src.at[3], got.at[3], *sems(2))
    sum_q.start()
    s4 = GroupSum(*[v[n] for n in ("parts", "near", "sent", "half", "full")], *sems(2))
    s2.finish()
    all_q = LowGather(v["sum_q"], *sems(2))

    def early_low():
        value = sum_q.total()
        all_q.start(value)

    spread2 = LastSpread(split2, whole2, *sems(10))

    def late_products():
        spread2.mark(pk[:8, PICKS["hot"][0]:PICKS["hot"][0] + 128])
        for n in range(0, 6, 2):
            spread2.put(n, dot(v["low_q"][...], dfused[:, n * 128:n * 128 + 256]))

    summed(s4, wide(dfused, v["wj"]), early_low, late_products)
    all_q.wait()
    spread2.put(6, dot(v["sum_q"][...], v["cols"][0]))
    spread2.start()
    layer, mine_grad = v["layer"], v["gos"]
    pairs = [(sub(mine_grad, j), sub(back, j), sub(back, j)) for j in range(4)] + [(layer, out, out)]
    sw2 = Swap(pairs, *sems(3))
    s3.arrive()
    for thing in (g4, s3):
        thing.finish()
    layer[...] = (mid[...] + bias_n[...] + dot_o(v["sum_n"][:, mine_rows], pick(pk, "down_out")) + s3.total()).astype(BF16)
    sw2.start(4)
    spread.share()
    correction = dot_o(v["sum_q"][:, mine_rows], pick(pk, "joined_in"))
    spread2.add()
    spread2.deal()
    s4.arrive()
    for j in ORDER:
        rows = slice(j * 32, (j + 1) * 32)
        value = dmid[rows] + norm_back(xs[rows].astype(F32), gain1[...], correction[rows] + s4.total(rows))
        mine_grad[rows] = value.astype(BF16)
        sw2.start(j)
        if j == 3:
            spread2.line()
    spread2.share_groups()
    spread.finish()
    spread2.share_line()
    for n in range(5):
        sw2.wait(n)
    spread2.finish()
    for thing in (s4, sw2):
        thing.finish()


SCRATCH = dict(
    lines=((8, 2048), F32), bias=((1, 1024), F32), bias_one=((768,), F32), mine=((16, TRADED), BF16), pk=((16, PICKED), BF16),
    xs=((128, 2048), BF16), xbuf=((1024, 2048), BF16), gbuf=((1024, 2048), BF16), gos=((128, 2048), BF16),
    wj=((2048, 768), BF16), wd=((256, 2048), BF16), wn=((1024, 2048), BF16), wu=((2048, 1024), BF16),
    qa=((4, 1024, 128), BF16), ka=((4, 1024, 128), BF16), va=((4, 1024, 128), BF16), c4=((4, 1024, 128), BF16),
    ctx=((1024, 256), BF16), dfused=((1024, 768), BF16), act=((1024, 1024), BF16),
    dpre=((1024, 1024), BF16), dact=((1024, 1024), F32), mid=((128, 2048), F32), dmid=((128, 2048), F32),
    layer=((128, 2048), BF16), cols=((4, 1024, 256), BF16),
    low_src=((4, 16, 1024), BF16), low_got=((4, 8, 16, 128), BF16),
    low_q=((16, 1024), BF16), low_g=((16, 1024), BF16), low_u=((16, 1024), BF16), low_d=((16, 1024), BF16),
    sum_d=((16, 1024), BF16), sum_u=((16, 1024), BF16), sum_n=((16, 1024), BF16), sum_q=((16, 1024), BF16),
    parts=((1024, 2048), BF16), near=((4, 128, 2048), BF16), sent=((3, 128, 2048), BF16), half=((2, 64, 2048), BF16),
    full=((2, 128, 2048), BF16), near2=((4, 128, 2048), BF16), sent2=((3, 128, 2048), BF16),
    half2=((2, 64, 2048), BF16), full2=((2, 128, 2048), BF16))


def block_call(*args):
    outs = [shape(128, 2048), shape(128, 2048), shape(8, 16, 3, 8, 128), shape(8, 8, 16, 8, 128),
            shape(8, 12, 8, 128), shape(8, 8, 4, 8, 128)]
    low = [DMA((8,)), DMA((8,))]
    sums = [DMA((10,)), DMA((10,))]
    gather = GroupGather.SEMS
    kinds = [DMA((8,)), DMA((8,)), DMA((4,)), *Swap.sems(11), *PlaneGather.SEMS * 4, *gather, *gather, *low, *sums,
             *gather, *low, *low, *sums, *low, *low, *low, *gather, *Spread.SCRATCH, *sums, *low, *sums, *low,
             *LastSpread.SCRATCH, *Swap.sems(5)]
    return pl.pallas_call(
        block_kernel, out_shape=outs, in_specs=specs(pltpu.SMEM, *[ANY] * 22), out_specs=specs(*[ANY] * 6),
        scratch_shapes=[VMEM(*s) for s in SCRATCH.values()] + kinds,
        compiler_params=params(1, 60), name="block")(*args)


def write_kernel(split, whole, split2, whole2, back, layer, *outs):
    joined_out, dense_in, up_out, down_in, *wholes, grad, out = outs
    for ref, count, first in ((dense_in, 2, 0), (up_out, 8, 2), (down_in, 8, 10)):
        for n in range(count):
            for half in (0, 1):
                k = 2 * (first + n) + half
                ref[:, half * 8:half * 8 + 8, n * 128:n * 128 + 128] = split[:, k // 3, k % 3].astype(F32)
    for n in range(6):
        for half in (0, 1):
            joined_out[:, half * 8:half * 8 + 8, n * 128:n * 128 + 128] = split2[:, 2 * n + half].astype(F32)
    for i, ref in enumerate(wholes):
        for t in range(8):
            for n in range(2):
                for half in (0, 1):
                    at = t * 256 + n * 128
                    k = n * 2 + half
                    block_in = whole2[:, t, k] if i == 0 else whole[:, t, i * 4 + k]
                    ref[:, half * 8:half * 8 + 8, at:at + 128] = block_in.astype(F32)
    grad[...] = back[...].astype(F32)
    out[...] = layer[...]


def write_call(split, whole, split2, whole2, back, layer):
    widths = [768, 256, 1024, 1024] + [2048] * 4
    rows = pl.BlockSpec((64, 2048), lambda b: (b, 0))
    return pl.pallas_call(
        write_kernel, grid=(2,),
        out_shape=[shape(8, 16, n, dtype=F32) for n in widths] + [shape(128, 2048, dtype=F32), shape(128, 2048)],
        in_specs=[pl.BlockSpec((4, *n, 8, 128), lambda b, n=n: (b, *[0] * len(n), 0, 0)) for n in ((16, 3), (8, 16), (12,), (8, 4))
                  ] + [rows, rows],
        out_specs=[pl.BlockSpec((4, 16, n), lambda b: (b, 0, 0)) for n in widths] + [rows, rows],
        compiler_params=plain(58), name="write")(split, whole, split2, whole2, back, layer)


def local(tokens, grad_out, adapter_ids, first_gain, first_shift, joined_weight, joined_bias, dense_weight,
          dense_bias, second_gain, second_shift, up_weight, up_bias, down_weight, down_bias, joined_adapt_in,
          joined_adapt_out, dense_adapt_in, dense_adapt_out, up_adapt_in, up_adapt_out, down_adapt_in,
          down_adapt_out):
    turn = lambda a: jnp.swapaxes(a, 1, 2)
    flat = lambda a: a.reshape(128, a.shape[2])
    vectors = [a.reshape(1, -1) for a in (first_gain, first_shift, second_gain, second_shift, dense_bias, down_bias,
                                          up_bias)] + [joined_bias]
    adapters = dict(joined_in=turn(joined_adapt_in), joined_out=joined_adapt_out, dense_in=turn(dense_adapt_in),
                    dense_out=dense_adapt_out, up_in=turn(up_adapt_in), up_out=up_adapt_out,
                    down_in=turn(down_adapt_in), down_out=down_adapt_out)
    back, layer, split, whole, split2, whole2 = block_call(
        adapter_ids, tokens, grad_out, *vectors, *[flat(adapters[n]) for n in SETS], joined_weight, dense_weight,
        down_weight, up_weight)
    joined_out, dense_in, up_out, down_in, joined_in, dense_out, up_in, down_out, grad_tokens, layer_out = write_call(
        split, whole, split2, whole2, back, layer)
    return (layer_out, grad_tokens, turn(joined_in), joined_out, turn(dense_in), dense_out, turn(up_in), up_out,
            turn(down_in), down_out)


def solution(mesh):
    fine = Mesh(mesh.devices.reshape(2, 4, 2, 2, 4), AXES)
    rows, cols = P(FSDP, TP), P(TP, FSDP)
    tok = P((*FSDP, *TP), None)
    last, middle, one = P(None, None, TP), P(None, TP, None), P(TP)
    return jax.shard_map(
        local, mesh=fine,
        in_specs=(tok, tok, P(FSDP), P(), P(), rows, one, cols, P(), P(), P(), rows, one, cols, P(), P(), last,
                  middle, P(), P(), last, middle, P()),
        out_specs=(tok, tok, P(), last, middle, P(), P(), last, middle, P()), check_vma=False)
```

```python
import functools

import jax
import jax.numpy as jnp
from jax import lax
from jax.experimental import pallas as pl
from jax.experimental.pallas import tpu as pltpu
from jax.sharding import Mesh
from jax.sharding import PartitionSpec as P

HEADS = 32
EPSILON = 1e-05
MASKED = -1e30
AXES = ("xl", "y", "c", "xh", "z")
FSDP = ("xl", "y", "c")
TP = ("xh", "z")
PLANE = ("xl", "y", "xh")
MESH_ID = pl.DeviceIdType.MESH
ANY = pl.ANY
VMEM = pltpu.VMEM
DMA = pltpu.SemaphoreType.DMA
F32 = jnp.float32
BF16 = jnp.bfloat16
ORDER = (0, 3, 1, 2)
PICKS = dict(hot=(0, 128), joined_out=(128, 768), up_out=(896, 1024), dense_in=(1920, 256), down_in=(2176, 1024),
             joined_in=(3200, 2048), up_in=(5248, 2048), dense_out=(7296, 2048), down_out=(9344, 2048))
TRADED = 3200
PICKED = 11392


def remote(src, dst, sems, index, device):
    send, recv = sems
    return pltpu.make_async_remote_copy(
        src_ref=src, dst_ref=dst, send_sem=send.at[index], recv_sem=recv.at[index],
        device_id=device, device_id_type=MESH_ID)


def places():
    return tuple(lax.axis_index(a) for a in AXES)


def at_home():
    _, _, c, xh, _ = places()
    return 1 - (xh - c) * (xh - c)


def meet(peers):
    barrier = pltpu.get_barrier_semaphore()
    for p in peers:
        pl.semaphore_signal(barrier, inc=1, device_id=p, device_id_type=MESH_ID)
    pl.semaphore_wait(barrier, len(peers))


def group_peer(n):
    _, _, c, _, z = places()
    return {"c": lax.rem(c + n // 4, 2), "z": lax.rem(z + n % 4, 4)}


def group_peers():
    return [group_peer(n) for n in range(1, 8)]


def diagonal():
    _, _, c, xh, _ = places()
    return {"c": 1 - c, "xh": 1 - xh}


def plane_peers():
    xl, y, c, xh, _ = places()
    peers = []
    for d in range(1, 4):
        for core in (0, 1):
            peers.append({"y": lax.rem(y + d, 4), "c": core})
            x = lax.rem(xh * 2 + xl + d, 4)
            peers.append({"xh": x // 2, "xl": lax.rem(x, 2), "c": core})
    return peers


def block(ref, n, size=128):
    return ref.at[pl.ds(pl.multiple_of(n * size, size), size)]


def loop(count, body, first=0):
    def run(i, carry):
        body(i)
        return carry

    lax.fori_loop(first, count, run, 0)


class GroupGather:
    SEMS = [DMA((8, 4)), DMA((8, 4))]

    def __init__(self, dst, send, recv):
        self.dst, self.sems = dst, (send, recv)
        _, _, self.c, _, self.z = places()
        self.up, self.down, self.other = group_peer(1), group_peer(3), group_peer(4)

    def at(self, core, z, j):
        return self.dst.at[pl.ds(pl.multiple_of((core * 4 + z) * 128 + j * 32, 32), 32)]

    def copy(self, z, j, kind, device):
        ref = self.at(self.c, z, j)
        return remote(ref, ref, self.sems, (kind, j), device)

    def put(self, j):
        self.copy(self.z, j, 0, self.up).start()
        self.copy(self.z, j, 1, self.down).start()
        self.copy(self.z, j, 2, self.other).start()

    def near(self, j):
        below, above = lax.rem(self.z + 3, 4), lax.rem(self.z + 1, 4)
        self.copy(below, j, 0, self.up).wait_recv()
        if j < 2:
            self.copy(below, j, 3, self.up).start()
        self.copy(below, j, 5, self.other).start()
        self.copy(above, j, 1, self.down).wait_recv()
        if j >= 2:
            self.copy(above, j, 4, self.down).start()
        self.copy(above, j, 6, self.other).start()

    def far(self, j):
        opposite = lax.rem(self.z + 2, 4)
        self.copy(opposite, j, 3 if j < 2 else 4, self.up).wait_recv()
        self.copy(opposite, j, 7, self.other).start()

    def shared(self, kind):
        loop(4, lambda j: self.copy(self.z, j, kind, self.other).wait_recv())

    def finish(self):
        def end(j):
            for kind in (0, 1, 2, 3 + j // 2, 5, 6, 7):
                self.copy(self.z, j, kind, self.other).wait_send()

        loop(4, end)


class LowGather:
    SEMS = [DMA((8,)), DMA((8,))]

    def __init__(self, dst, send, recv):
        self.dst, self.sems = dst, (send, recv)
        _, _, c, _, z = places()
        self.own = pl.ds(pl.multiple_of((c * 4 + z) * 128, 128), 128)

    def copy(self, n):
        ref = self.dst.at[:, self.own]
        return remote(ref, ref, self.sems, (n,), group_peer(n))

    def start(self, value):
        self.dst[:, self.own] = value
        loop(8, lambda n: self.copy(n).start(), 1)

    def wait(self):
        loop(8, lambda n: self.copy(n).wait(), 1)


class LowSum:
    SEMS = [DMA((8,)), DMA((8,))]

    def __init__(self, src, got, send, recv):
        self.src, self.got, self.sems = src, got, (send, recv)
        _, _, self.c, _, self.z = places()

    def copy(self, n):
        p = group_peer(n)
        cols = pl.ds(pl.multiple_of((p["c"] * 4 + p["z"]) * 128, 128), 128)
        return remote(self.src.at[:, cols], self.got.at[n], self.sems, (n,), p)

    def start(self):
        loop(8, lambda n: self.copy(n).start(), 1)

    def total(self):
        loop(8, lambda n: self.copy(n).wait(), 1)
        own = pl.ds(pl.multiple_of((self.c * 4 + self.z) * 128, 128), 128)
        out = self.src[:, own].astype(F32)
        for n in range(1, 8):
            out = out + self.got[n].astype(F32)
        return out.astype(BF16)


class PlaneGather:
    SEMS = [DMA((1,)), DMA((41,)), DMA((16, 2))]

    def __init__(self, src, dst, by_rows, local_sem, send, recv):
        self.src, self.dst, self.by_rows, self.local_sem, self.sems = src, dst, by_rows, local_sem, (send, recv)
        self.xl, self.y, self.c, self.xh, _ = places()
        self.x = self.xh * 2 + self.xl
        self.home = at_home()
        r = lax.rem(self.x - 2 * self.c + 4, 4)
        self.odd = 1 - lax.rem(r, 2)
        self.even = lax.rem(r, 2)
        self.away = lax.rem(r - self.odd + 4, 4)

    def whole(self, xl, y, core):
        k = (xl * 4 + y) * 2 + core
        if self.by_rows:
            return block(self.dst, k)
        return self.dst.at[:, pl.ds(pl.multiple_of(k * 128, 128), 128)]

    def half(self, ref, h):
        n = ref.shape[0] // 2
        return ref.at[pl.ds(pl.multiple_of(h * n, n), n)]

    def copy(self, place, h, n, device, src=None):
        xl, y, core = place
        send, recv = self.sems
        dst = self.half(self.whole(*place), h)
        return pltpu.make_async_remote_copy(
            src_ref=dst if src is None else self.half(src, h), dst_ref=dst, send_sem=send.at[n],
            recv_sem=recv.at[(xl * 4 + y) * 2 + core, h], device_id=device, device_id_type=MESH_ID)

    def arrived(self, place, h):
        self.copy(place, h, 0, {"c": 1 - self.c}).wait_recv()

    def arrived_whole(self, place):
        loop(2, lambda h: self.arrived(place, h))

    def chip(self, dx, dy, core):
        x = lax.rem(self.x + dx, 4)
        return {"xh": x // 2, "xl": lax.rem(x, 2), "y": lax.rem(self.y + dy, 4), "c": core}

    def both_ways(self, place, n, along_x, along_y, core, src=None):
        def send(i):
            d = 1 + 2 * lax.rem(i, 2)
            h = lax.rem(i + i // 2, 2)
            self.copy(place, h, n + i, self.chip(along_x * d, along_y * d, core), src).start()

        loop(4, send)

    def local(self):
        return pltpu.make_async_copy(self.src, self.whole(self.xl, self.y, self.c), self.local_sem.at[0])

    def start(self):
        place = (self.xl, self.y, self.c)

        @pl.when(self.home == 1)
        def _():
            self.local().start()

        self.both_ways(place, 0, 1 - self.c, self.c, self.xh, self.src)

        @pl.when(self.home == 0)
        def _():
            loop(2, lambda h: self.copy(place, h, 39 + h, {"c": 1 - self.c}, self.src).start())

    def row(self, d):
        return lax.rem(self.y + d, 4)

    def along_y(self, e):
        self.both_ways((e, self.y, 0), 4 + 4 * e, 0, 1, self.c)

    def along_x(self, d):
        self.both_ways((self.xl, self.row(d), 1), 23 + 4 * d, 1, 0, self.c)

    def step(self, n):
        if n == 0:
            @pl.when(self.home == 1)
            def _():
                self.local().wait()
                self.arrived_whole((self.xl, self.y, 1 - self.c))
                self.along_y(self.xl)
                self.along_x(0)
        elif n == 1:
            place, h = (self.odd, self.y, 0), self.away // 2
            self.arrived(place, h)
            self.copy(place, h, 12, self.chip(self.away, 0, self.c)).start()

            @pl.when(self.home == 1)
            def _():
                def pass_y(k):
                    place = (self.xl, self.row(3 - 2 * k), 1)
                    self.arrived(place, k)
                    self.copy(place, k, 21 + k, self.chip(0, 1 + 2 * k, self.c)).start()

                loop(2, pass_y)
        elif n == 2:
            self.arrived((self.odd, self.y, 0), 1 - self.away // 2)
            self.along_y(self.odd)

            @pl.when(self.home == 1)
            def _():
                def spread(k):
                    self.arrived((self.xl, self.row(3 - 2 * k), 1), 1 - k)
                    self.along_x(3 - 2 * k)

                loop(2, spread)
        elif n == 3:
            @pl.when(self.home == 0)
            def _():
                self.arrived_whole((self.even, self.y, 0))
                self.along_y(self.even)

            @pl.when(self.home == 1)
            def _():
                self.arrived_whole((self.xl, self.row(2), 1))
                self.along_x(2)
        elif n == 4:
            def pass_on(i):
                e, k = i // 2, lax.rem(i, 2)
                place = (e, self.row(3 - 2 * k), 0)
                self.arrived(place, k)
                self.copy(place, k, 13 + i, self.chip(0, 1 + 2 * k, self.c)).start()

            loop(4, pass_on)
        else:
            def pass_on(i):
                k = i * (3 if n == 5 else 1) + (n - 5)
                place, h = (self.odd, self.row(k), 1), self.away // 2
                self.arrived(place, h)
                self.copy(place, h, 17 + k, self.chip(self.away, 0, self.c)).start()

            loop(2, pass_on)

    def wait(self):
        def rows(e):
            loop(2, lambda k: self.arrived((e, self.row(3 - 2 * k), 0), 1 - k))
            self.arrived_whole((e, self.row(2), 0))

        loop(2, rows)
        loop(4, lambda y: self.arrived((self.odd, y, 1), 1 - self.away // 2))

        @pl.when(self.home == 0)
        def _():
            loop(4, lambda y: self.arrived_whole((self.even, y, 1)))

    def finish(self):
        sent = lambda n: self.copy((0, 0, 0), 0, n, {"c": 1 - self.c}).wait_send()
        loop(21, sent)

        @pl.when(self.home == 1)
        def _():
            loop(39, sent, 21)

        @pl.when(self.home == 0)
        def _():
            loop(41, sent, 39)


class GroupSum:
    NAMES = ("far_up", "far_down", "up_high", "down_low", "up_low", "down_high")
    SCRATCH = [VMEM((1024, 2048), BF16), VMEM((4, 128, 2048), BF16), VMEM((3, 128, 2048), BF16),
               VMEM((2, 64, 2048), BF16), VMEM((2, 128, 2048), BF16), DMA((10,)), DMA((10,))]

    def __init__(self, parts, near, sent, half, full, send, recv):
        self.parts, self.near, self.sent, self.half, self.full, self.sems = parts, near, sent, half, full, (send, recv)
        _, _, self.c, _, self.z = places()
        self.up, self.down, self.other = group_peer(1), group_peer(3), group_peer(4)
        self.order = [lax.rem(self.z + d, 4) for d in (2, 1, 3, 0)]

    def part(self, core, i):
        return block(self.parts, core * 4 + self.order[i])

    def given(self, i):
        return remote(self.part(1 - self.c, i), self.near.at[i], self.sems, (i,), self.other)

    def give_from(self, i, at):
        remote(block(self.parts, (1 - self.c) * 4 + at), self.near.at[i], self.sems, (i,), self.other).start()

    def give(self, i):
        self.given(i).start()

    def pair(self, i, rows=slice(None)):
        return self.part(self.c, i)[rows].astype(F32) + self.near[i, rows].astype(F32)

    def piece(self, name):
        low, high = pl.ds(0, 64), pl.ds(64, 64)
        n = self.NAMES.index(name)
        src = (self.sent.at[0, low], self.sent.at[0, high], self.sent.at[1, high], self.sent.at[2, low],
               self.sent.at[1, low], self.sent.at[2, high])[n]
        dst = (self.half.at[0], self.half.at[1], self.full.at[0, high], self.full.at[1, low],
               self.full.at[0, low], self.full.at[1, high])[n]
        return remote(src, dst, self.sems, (4 + n,), (self.up, self.down)[n % 2])

    def far(self):
        self.given(0).wait_recv()
        self.sent[0] = self.pair(0).astype(BF16)
        self.piece("far_up").start()
        self.piece("far_down").start()

    def near_up(self):
        self.given(1).wait_recv()
        self.sent[1, pl.ds(64, 64)] = self.pair(1, pl.ds(64, 64)).astype(BF16)
        self.piece("up_high").start()

    def near_down(self):
        self.given(2).wait_recv()
        self.sent[2, pl.ds(0, 64)] = self.pair(2, pl.ds(0, 64)).astype(BF16)
        self.piece("down_low").start()

    def pass_on(self):
        low, high = pl.ds(0, 64), pl.ds(64, 64)
        self.piece("far_up").wait_recv()
        self.sent[1, low] = (self.pair(1, low) + self.half[0].astype(F32)).astype(BF16)
        self.piece("up_low").start()
        self.piece("far_down").wait_recv()
        self.sent[2, high] = (self.pair(2, high) + self.half[1].astype(F32)).astype(BF16)
        self.piece("down_high").start()

    def arrive(self):
        self.given(3).wait_recv()
        for name in ("up_high", "down_low", "up_low", "down_high"):
            self.piece(name).wait_recv()

    def total(self, rows=slice(None)):
        return self.pair(3, rows) + self.full[0, rows].astype(F32) + self.full[1, rows].astype(F32)

    def finish(self):
        for name in self.NAMES:
            self.piece(name).wait_send()
        for i in range(4):
            self.given(i).wait_send()


def params(cid, mib):
    return pltpu.CompilerParams(collective_id=cid, has_side_effects=True, vmem_limit_bytes=mib << 20)


def plain(mib):
    return pltpu.CompilerParams(vmem_limit_bytes=mib << 20)


def shape(*dims, dtype=BF16):
    return jax.ShapeDtypeStruct(dims, dtype)


def specs(*spaces):
    return [pl.BlockSpec(memory_space=s) for s in spaces]


def layer_norm(rows_in, gain, shift):
    row_mean = jnp.mean(rows_in, axis=-1, keepdims=True)
    centered = rows_in - row_mean
    variance = jnp.mean(centered * centered, axis=-1, keepdims=True)
    return centered * lax.rsqrt(variance + EPSILON) * gain + shift


def norm_back(rows_in, gain, grad):
    row_mean = jnp.mean(rows_in, axis=-1, keepdims=True)
    centered = rows_in - row_mean
    inverse = lax.rsqrt(jnp.mean(centered * centered, axis=-1, keepdims=True) + EPSILON)
    n = centered * inverse
    e = gain * grad
    return (e - jnp.mean(e, axis=-1, keepdims=True) - n * jnp.mean(e * n, axis=-1, keepdims=True)) * inverse


def dot(a, b, dims=((1,), (0,))):
    return lax.dot_general(a, b, (dims, ((), ())), preferred_element_type=F32)


def dot_t(a, b):
    return dot(a, b, ((1,), (1,)))


def dot_o(a, b):
    return dot(a, b, ((0,), (0,)))


def tiles(count, size, body):
    def run(i, carry):
        body(pl.ds(pl.multiple_of(i * size, size), size))
        return carry

    lax.fori_loop(0, count, run, 0)


def split_refs(refs, *counts):
    refs, out = list(refs), []
    for n in counts:
        out.append(refs[:n])
        refs = refs[n:]
    return (*out, refs)


def pick(ref, name):
    first, n = PICKS[name]
    return ref[:, pl.ds(first, n)]


def row_pair(z):
    return (pl.ds(pl.multiple_of(z * 128, 128), 128), pl.ds(pl.multiple_of(512 + z * 128, 128), 128))


def take_pair(ref, z, cols=slice(None)):
    a, b = row_pair(z)
    return jnp.concatenate([ref[a, cols], ref[b, cols]], axis=0)


def put_pair(ref, z, value, cols=slice(None)):
    a, b = row_pair(z)
    ref[a, cols] = value[:128]
    ref[b, cols] = value[128:]


class Swap:
    def __init__(self, pairs, local, send, recv):
        self.pairs, self.local, self.sems, self.home = pairs, local, (send, recv), at_home()

    def near_copy(self, n):
        src, _, dst = self.pairs[n]
        return pltpu.make_async_copy(src, dst, self.local.at[n])

    def far_copy(self, n):
        src, dst, _ = self.pairs[n]
        return remote(src, dst, self.sems, (n,), diagonal())

    def start(self, n):
        @pl.when(self.home == 1)
        def _():
            self.near_copy(n).start()

        @pl.when(self.home == 0)
        def _():
            self.far_copy(n).start()

    def wait(self, n):
        @pl.when(self.home == 1)
        def _():
            self.near_copy(n).wait()

        @pl.when(self.home == 0)
        def _():
            self.far_copy(n).wait_recv()

    def finish(self):
        @pl.when(self.home == 0)
        def _():
            for n in range(len(self.pairs)):
                self.far_copy(n).wait_send()

    @staticmethod
    def sems(n):
        return [DMA((n,)), DMA((n,)), DMA((n,))]


class Spread:
    SCRATCH = [VMEM((16, 5, 8, 128), BF16), VMEM((16, 5, 8, 128), BF16), VMEM((8, 3, 8, 128), BF16),
               VMEM((8, 8, 128), BF16), DMA((16,)), DMA((16,)), DMA((9,)), DMA((16,)), DMA((20,)), DMA((20,)), DMA((2,))]

    def __init__(self, split, whole, send, got, part, full, one_send, one_recv, two_send, two_recv, send3, recv3, local):
        self.split, self.whole, self.send, self.got, self.part, self.full = split, whole, send, got, part, full
        self.one, self.two, self.three, self.local = (one_send, one_recv), (two_send, two_recv), (send3, recv3), local
        self.xl, self.y, self.c, self.xh, self.z = places()
        self.q = (self.xh * 2 + self.xl) * 4 + self.y
        self.home = at_home()

    def put(self, n, value):
        for m in range(4):
            k = 2 * n + m
            where = (k // 3, k % 3) if k < 48 else (k - 48, 3)
            row, col = m % 2 * 8, m // 2 * 128
            self.send[where] = value[row:row + 8, col:col + 128].astype(BF16)

    def mark(self, hot):
        for j in range(16):
            self.send[j, 4] = hot

    def chip(self, n):
        q = lax.rem(self.q + n, 16)
        x = q // 4
        return q, {"xh": x // 2, "xl": lax.rem(x, 2), "y": lax.rem(q, 4)}

    def to_owner(self, n):
        q, device = self.chip(n)
        return remote(self.send.at[q], self.got.at[n], self.one, (n,), device)

    def start(self):
        loop(16, lambda n: self.to_owner(n).start(), 1)

    def add(self):
        self.got[0] = self.send[self.q]
        loop(16, lambda n: self.to_owner(n).wait_recv(), 1)
        for b in range(8):
            def more(n, total, b=b):
                return total + self.got[n, 0:4].astype(F32) * self.got[n, 4].astype(F32)[b:b + 1]

            total = lax.fori_loop(0, 16, more, jnp.zeros((4, 8, 128), F32)).astype(BF16)
            self.part[b] = total[:3]
            self.full[b] = total[3]

    def copy_to_groups(self, slot, i):
        device = {"xh": self.c, "xl": lax.rem(self.xl + i // 4, 2), "y": lax.rem(self.y + lax.rem(i, 4), 4)}
        send, recv = self.two
        return pltpu.make_async_remote_copy(
            src_ref=self.part, dst_ref=self.split.at[:, slot], send_sem=send.at[i],
            recv_sem=recv.at[self.q], device_id=device, device_id_type=MESH_ID)

    def split_copy(self, i):
        return self.copy_to_groups(self.q, i)

    def split_own(self):
        return pltpu.make_async_copy(self.part, self.split.at[:, self.q], self.local.at[0])

    def whole_own(self):
        return pltpu.make_async_copy(self.full, self.whole.at[:, self.c * 4 + self.z, self.q], self.local.at[1])

    def line_copies(self):
        where = self.whole.at[:, self.c * 4 + self.z, self.q]
        return [remote(self.full, where, self.three, (d,), {"z": lax.rem(self.z + d, 4)}) for d in (1, 2, 3)]

    def plane_copy(self, n):
        where = self.whole.at[:, pl.ds(self.c * 4, 4), self.q]
        return remote(where, where, self.three, (4 + n,), self.chip(n)[1])

    def shared_whole(self):
        where = self.whole.at[:, pl.ds(self.c * 4, 4)]
        return remote(where, where, self.three, (0,), {"c": 1 - self.c})

    def shared_split(self):
        send, recv = self.two
        return pltpu.make_async_remote_copy(
            src_ref=self.split, dst_ref=self.split, send_sem=send.at[8], recv_sem=recv.at[0],
            device_id={"c": 1 - self.c}, device_id_type=MESH_ID)

    def deal_groups(self):
        @pl.when(self.home == 1)
        def _():
            self.split_own().start()

        @pl.when(self.home == 0)
        def _():
            self.split_copy(0).start()

        loop(8, lambda i: self.split_copy(i).start(), 1)

    def deal(self):
        self.whole_own().start()
        for copy in self.line_copies():
            copy.start()
        self.deal_groups()

    def deal_plane(self):
        self.whole_own().wait()
        for copy in self.line_copies():
            copy.wait_recv()
        loop(16, lambda n: self.plane_copy(n).start(), 1)

    def wait_groups(self, count):
        send, recv = self.two
        def wait(q):
            @pl.when(self.q != q)
            def _():
                pltpu.make_async_remote_copy(
                    src_ref=self.part, dst_ref=self.split.at[:, q], send_sem=send.at[0], recv_sem=recv.at[q],
                    device_id={"c": 1 - self.c}, device_id_type=MESH_ID).wait_recv()

        loop(count, wait)

    def share(self):
        @pl.when(self.home == 1)
        def _():
            self.split_own().wait()
            self.wait_groups(16)
            self.shared_split().start()

        loop(16, lambda n: self.plane_copy(n).wait_recv(), 1)
        self.shared_whole().start()

    def finish_shares(self):
        self.shared_whole().wait()

        @pl.when(self.home == 1)
        def _():
            self.shared_split().wait_send()

        @pl.when(self.home == 0)
        def _():
            self.shared_split().wait_recv()

    def finish_groups(self):
        @pl.when(self.home == 0)
        def _():
            self.split_copy(0).wait_send()

        loop(8, lambda i: self.split_copy(i).wait_send(), 1)

    def finish(self):
        self.finish_shares()
        self.finish_groups()
        for copy in self.line_copies():
            copy.wait_send()

        def end(n):
            self.plane_copy(n).wait_send()
            self.to_owner(n).wait_send()

        loop(16, end, 1)


class LastSpread(Spread):
    SCRATCH = [VMEM((16, 2, 8, 128), BF16), VMEM((16, 2, 8, 128), BF16), VMEM((8, 8, 128), BF16),
               DMA((16,)), DMA((16,)), DMA((9,)), DMA((16,)), DMA((20,)), DMA((20,)), DMA((2,))]

    def __init__(self, split, whole, send, got, part, *sems):
        super().__init__(split, whole, send, got, part, part, *sems)

    def put(self, n, value):
        for m in range(4):
            row, col = m % 2 * 8, m // 2 * 128
            self.send[2 * n + m, 0] = value[row:row + 8, col:col + 128].astype(BF16)

    def mark(self, hot):
        for j in range(16):
            self.send[j, 1] = hot

    def add(self):
        self.got[0] = self.send[self.q]
        loop(16, lambda n: self.to_owner(n).wait_recv(), 1)
        for b in range(8):
            def more(n, total, b=b):
                return total + self.got[n, 0].astype(F32) * self.got[n, 1].astype(F32)[b:b + 1]

            self.part[b] = lax.fori_loop(0, 16, more, jnp.zeros((8, 128), F32)).astype(BF16)

    def split_copy(self, i):
        return self.copy_to_groups(lax.rem(self.q, 12), i)

    def split_own(self):
        return pltpu.make_async_copy(self.part, self.split.at[:, lax.rem(self.q, 12)], self.local.at[0])

    def late(self):
        return lax.rem(self.q, 4)

    def whole_own(self):
        return pltpu.make_async_copy(self.part, self.whole.at[:, self.c * 4 + self.z, self.late()], self.local.at[1])

    def line_copies(self):
        where = self.whole.at[:, self.c * 4 + self.z]
        return [remote(where, where, self.three, (d,), {"z": lax.rem(self.z + d, 4)}) for d in (1, 2, 3)]

    def plane_copy(self, n):
        where = self.whole.at[:, self.c * 4 + self.z, self.late()]
        return remote(self.part, where, self.three, (4 + n,), self.chip(n)[1])

    def deal(self):
        @pl.when(self.q >= 12)
        def _():
            self.whole_own().start()
            loop(16, lambda n: self.plane_copy(n).start(), 1)

        @pl.when(self.q < 12)
        def _():
            self.deal_groups()

    def share_groups(self):
        @pl.when(self.home == 1)
        def _():
            @pl.when(self.q < 12)
            def _():
                self.split_own().wait()

            self.wait_groups(12)
            self.shared_split().start()

    def line(self):
        @pl.when(self.q >= 12)
        def _():
            self.whole_own().wait()

        def late(n):
            @pl.when(lax.rem(self.q - n + 16, 16) >= 12)
            def _():
                self.plane_copy(n).wait_recv()

        loop(16, late, 1)

        for copy in self.line_copies():
            copy.start()

    def share_line(self):
        for copy in self.line_copies():
            copy.wait_recv()
        self.shared_whole().start()

    def finish(self):
        self.finish_shares()

        @pl.when(self.q < 12)
        def _():
            self.finish_groups()

        @pl.when(self.q >= 12)
        def _():
            loop(16, lambda n: self.plane_copy(n).wait_send(), 1)

        for copy in self.line_copies():
            copy.wait_send()
        loop(16, lambda n: self.to_owner(n).wait_send(), 1)


def far_peers():
    xl, y, _, xh, _ = places()
    peers = []
    for d in range(1, 4):
        x = lax.rem(xh * 2 + xl + d, 4)
        for e in range(1, 4):
            peers.append({"xh": x // 2, "xl": lax.rem(x, 2), "y": lax.rem(y + e, 4)})
    return peers


ROOT_HALF = 0.7071067811865476
ROOT_TAU = 0.3989422804014327
SETS = dict(joined_in=(0, 0), up_in=(128, 0), dense_out=(256, 0), down_out=(384, 0), up_out=(512, 0),
            down_in=(512, 1024), joined_out=(640, 0), dense_in=(640, 768))


def cast_parts(value):
    high = value.astype(BF16).astype(F32)
    middle = (value - high).astype(BF16).astype(F32)
    return high, middle, value - high - middle


def block_kernel(*refs):
    (ids, tokens, go, *vectors), adapters, shards, outs, scratch = split_refs(refs, 11, 8, 4, 6)
    back, out, split, whole, split2, whole2 = outs
    names = list(SCRATCH)
    v = dict(zip(names, scratch))
    rest = list(scratch[len(names):])

    def sems(n):
        taken = rest[:n]
        del rest[:n]
        return taken

    load_sem, vector_sem, copy_sem = sems(3)
    xl, y, c, xh, z = places()
    own = c * 4 + z
    mine_rows = pl.ds(pl.multiple_of(own * 128, 128), 128)
    there_rows = (1 - c) * 4 + z
    gain1, shift1, gain2, shift2, bias_d, bias_n = (v["lines"].at[n:n + 1] for n in range(6))
    pk, xs, xbuf, gbuf = v["pk"], v["xs"], v["xbuf"], v["gbuf"]
    sets = v["parts"]
    loads = {}
    for n, (name, ref) in enumerate(zip(SETS, adapters)):
        row, col = SETS[name]
        loads[name] = pltpu.make_async_copy(ref, sets.at[pl.ds(row, 128), pl.ds(col, ref.shape[1])], load_sem.at[n])
        loads[name].start()
    lines = [pltpu.make_async_copy(ref, v["lines"].at[n:n + 1], vector_sem.at[n]) for n, ref in enumerate(vectors[:6])]
    for line in lines:
        line.start()
    meet(plane_peers() + group_peers() + far_peers())

    bias = v["bias"]
    mine = v["mine"]
    piece = lambda who, j: gbuf.at[pl.ds(pl.multiple_of(who * 128 + j * 32, 32), 32)]
    sub = lambda ref, j: ref.at[pl.ds(j * 32, 32)]
    pairs = [(sub(tokens, j), sub(xs, j), sub(xs, j)) for j in range(4)]
    pairs += [(m, p, p) for m, p in ((mine, pk.at[:, :TRADED]), (vectors[7], v["bias_one"]), (vectors[6], bias))]
    pairs += [(sub(go, j), piece(there_rows, j), piece(own, j)) for j in range(4)]
    sw = Swap(pairs, *sems(3))
    for j in ORDER:
        sw.start(j)
    joined = PlaneGather(shards[0], v["wj"], True, *sems(3))
    dense = PlaneGather(shards[1], v["wd"], False, *sems(3))
    down = PlaneGather(shards[2], v["wn"], False, *sems(3))
    up = PlaneGather(shards[3], v["wu"], True, *sems(3))
    joined.start()
    set_id = ids[0]
    for name in ("joined_out", "up_out", "dense_in", "down_in"):
        (row, col), (first, n) = SETS[name], PICKS[name]
        loads[name].wait()
        chosen = sets[row:row + 16, col:col + n]
        for k in range(1, 8):
            chosen = jnp.where(set_id == k, sets[row + k * 16:row + k * 16 + 16, col:col + n], chosen)
        mine[:, first:first + n] = chosen
    first, n = PICKS["hot"]
    mine[:, first:first + n] = jnp.where(lax.broadcasted_iota(jnp.int32, (16, 128), 0) == set_id, 1.0, 0.0).astype(BF16)
    for n in (4, 5, 6):
        sw.start(n)
    for line in lines:
        line.wait()
    g1 = GroupGather(xbuf, *sems(2))
    for j in ORDER:
        sw.wait(j)
        x1 = layer_norm(xs[j * 32:(j + 1) * 32].astype(F32), gain1[...], shift1[...])
        xbuf[pl.ds(pl.multiple_of(own * 128 + j * 32, 32), 32)] = x1.astype(BF16)
        g1.put(j)
    dense.start()
    joined.step(0)
    joined.step(1)
    g1.near(0)
    joined.step(2)
    g1.near(3)
    joined.step(3)
    g1.near(1)
    joined.step(4)
    g1.near(2)
    joined.step(5)
    joined.step(6)
    for j in ORDER:
        sw.start(7 + j)
    dense.step(0)
    dense.step(1)
    down.start()
    sw.wait(4)
    for name in ("joined_in", "up_in", "dense_out", "down_out"):
        (row, col), (first, n) = SETS[name], PICKS[name]
        loads[name].wait()
        chosen = jnp.zeros((16, n), F32)
        for k in range(8):
            chosen = chosen + sets[row + k * 16:row + k * 16 + 16, col:col + n].astype(F32) * pk[k:k + 1, 0:1].astype(F32)
        pk[:, first:first + n] = chosen.astype(BF16)

    def low_pair(at):
        low = dot_t(pick(pk, "joined_in"), take_pair(xbuf, at)).astype(BF16)
        for n, rows in enumerate(row_pair(at)):
            v["low_q"][:, rows] = low[:, n * 128:n * 128 + 128]

    g1.shared(2)
    low_pair(z)
    for j in ORDER:
        g1.far(j)
    g1.shared(5)
    low_pair(lax.rem(z + 3, 4))
    g1.shared(6)
    low_pair(lax.rem(z + 1, 4))
    for n in (5, 6):
        sw.wait(n)
    joined.wait()
    g1.shared(7)
    low_pair(lax.rem(z + 2, 4))
    g2 = GroupGather(gbuf, *sems(2))

    lane = lax.broadcasted_iota(jnp.int32, (256, 128), 1)
    row = lax.broadcasted_iota(jnp.int32, (256, 128), 0)
    qa, ka, va = v["qa"], v["ka"], v["va"]

    def project(i, carry):
        rows = pl.ds(pl.multiple_of(i * 256, 256), 256)
        acc = dot(xbuf[rows], v["wj"][...]) + dot_o(v["low_q"][:, rows], pick(pk, "joined_out")) + v["bias_one"][...].reshape(1, 768)
        b = acc.astype(BF16).astype(F32)
        position = (i * 256 + row).astype(F32) * 0.125
        ones = jnp.where(lane < 67, 1.0, 0.0)
        for h in range(4):
            slope = jnp.exp2((own * 4 + h + 1).astype(F32) * (-8.0 / HEADS) + jnp.zeros((1, 128), F32))
            high, middle, lowest = cast_parts(position * slope)
            tail = jnp.where(lane == 64, high, jnp.where(lane == 65, middle, jnp.where(lane == 66, lowest, jnp.where(
                lane < 70, 1.0, 0.0))))
            at = h * 192
            qa[h, rows] = jnp.where(lane < 64, b[:, at:at + 128] * 0.125, ones).astype(BF16)
            ka[h, rows] = jnp.where(lane < 64, b[:, at + 64:at + 192], tail).astype(BF16)
            value = jnp.concatenate([b[:, at + 128:at + 192], b[:, at:at + 64]], axis=1)
            va[h, rows] = jnp.where(lane < 64, value, ones).astype(BF16)
        return carry

    lax.fori_loop(0, 4, project, 0)
    own_cols = pl.ds(pl.multiple_of(own * 256, 256), 256)
    keep = lambda n, ref: pltpu.make_async_copy(ref.at[:, own_cols], v["cols"].at[n], copy_sem.at[n])
    keep(0, xbuf).start()
    for j in ORDER:
        sw.wait(7 + j)
        g2.put(j)

    hooks = [lambda: dense.step(2), lambda: down.step(0), lambda: (dense.step(3), down.step(1)), lambda: g2.near(0), lambda: dense.step(4),
             lambda: g2.near(3), lambda: down.step(2), lambda: g2.near(1), lambda: (dense.step(5), dense.step(6)),
             lambda: g2.near(2), lambda: up.start(), lambda: down.step(3), lambda: (g2.far(0), g2.far(3)),
             lambda: None, lambda: (g2.far(1), g2.far(2)), lambda: down.step(4)]
    mask = lax.broadcasted_iota(jnp.int32, (256, 256), 0) <= lax.broadcasted_iota(jnp.int32, (256, 256), 1)
    line = lax.broadcasted_iota(jnp.int32, (128, 256), 0)
    c4 = v["c4"]

    def head(h, carry):
        for i in range(4):
            rows = pl.ds(i * 256, 256)
            q = qa[h, rows]
            last = jnp.where(mask, dot_t(ka[h, rows], q), MASKED)
            top = jnp.max(last, axis=0, keepdims=True)
            if i:
                before = dot_t(ka[h, pl.ds(0, i * 256)], q)
                top = jnp.maximum(top, jnp.max(before, axis=0, keepdims=True))
            mix = dot_o(va[h, rows], jnp.exp(last - top).astype(BF16))
            if i:
                mix = mix + dot_o(va[h, pl.ds(0, i * 256)], jnp.exp(before - top).astype(BF16))
            total = mix[64:65]
            high, middle, lowest = cast_parts(-(top + jnp.log(total)))
            mix = jnp.where(line == 67, high, jnp.where(line == 68, middle, jnp.where(
                line == 69, lowest, mix / total)))
            turned = mix.T
            c4[h, rows] = turned.astype(BF16)
            qa[h, rows] = jnp.where(lane < 67, q.astype(F32), jnp.where(lane < 70, turned, 0.0)).astype(BF16)
            for k in range(4):
                @pl.when(h == k)
                def _(k=k, i=i):
                    hooks[k * 4 + i]()
        return carry

    lax.fori_loop(0, 4, head, 0)
    ctx = v["ctx"]
    for h in (0, 2):
        ctx[:, h * 64:h * 64 + 128] = jnp.concatenate([c4[h, :, :64], c4[h + 1, :, :64]], axis=1)

    v["gos"][...] = gbuf[mine_rows]

    src, got = v["low_src"], v["low_got"]
    src[0] = dot_t(pick(pk, "dense_in"), ctx[...]).astype(BF16)
    sum_d = LowSum(src.at[0], got.at[0], *sems(2))
    sum_d.start()
    s1 = GroupSum(*[v[n] for n in ("parts", "near", "sent", "half", "full")], *sems(2))
    dense.wait()
    keep(0, xbuf).wait()
    g1.finish()

    def summed(s, compute, before=lambda: None, beside=lambda: None):
        def part(i, carry):
            compute(s, lax.rem(z + 2 - i + 3 * (i // 2) - 2 * (i // 3) + 4, 4))
            s.give_from(i, lax.rem(z + 2 - i + 3 * (i // 2) - 2 * (i // 3) + 4, 4))

            @pl.when(i == 1)
            def _():
                before()
                s.far()

            @pl.when(i == 2)
            def _():
                s.near_up()

            return carry

        lax.fori_loop(0, 4, part, 0)
        s.near_down()
        beside()
        s.pass_on()

    def dense_part(s, at):
        put_pair(s.parts, at, dot(take_pair(ctx, at), v["wd"][...]).astype(BF16))

    def low_tile(rows):
        v["low_g"][:, rows] = dot_t(pick(pk, "down_out"), gbuf[rows]).astype(BF16)

    def beside_dense():
        for kind in (2, 5, 6, 7):
            g2.shared(kind)
        keep(3, gbuf).start()
        down.step(5)
        up.step(0)
        tiles(4, 256, low_tile)
        down.step(6)
        up.step(1)

    summed(s1, dense_part, beside=beside_dense)
    up.step(2)
    mid, dmid, dact = v["mid"], v["dmid"], v["dact"]
    total_d = sum_d.total()
    mid[...] = dot_o(total_d, pick(pk, "dense_out")) + bias_d[...] + xs[...].astype(F32)
    down.wait()

    def grad_act(rows):
        dact[rows] = dot_t(gbuf[rows], v["wn"][...]) + dot_o(v["low_g"][:, rows], pick(pk, "down_in"))

    def grad_acts(i, carry):
        grad_act(pl.ds(pl.multiple_of(i * 256, 256), 256))

        @pl.when(i == 1)
        def _():
            up.step(3)

        return carry

    lax.fori_loop(0, 4, grad_acts, 0)
    up.step(4)
    s1.arrive()
    g3 = GroupGather(xbuf, *sems(2))
    for j in ORDER:
        rows = slice(j * 32, (j + 1) * 32)
        mid[rows] = mid[rows] + s1.total(rows)
        xbuf[pl.ds(pl.multiple_of(own * 128 + j * 32, 32), 32)] = layer_norm(mid[rows], gain2[...], shift2[...]).astype(BF16)
        g3.put(j)
    all_d = LowGather(v["sum_d"], *sems(2))
    all_d.start(total_d)
    up.step(5)
    up.step(6)
    up.wait()
    act, dpre = v["act"], v["dpre"]

    def forward(at):
        x = take_pair(xbuf, at)
        lu = dot_t(pick(pk, "up_in"), x).astype(BF16)
        for n, rows in enumerate(row_pair(at)):
            v["low_u"][:, rows] = lu[:, n * 128:n * 128 + 128]

        def run(n, carry):
            cols = pl.ds(pl.multiple_of(n * 256, 256), 256)
            w = pk[:, pl.ds(pl.multiple_of(PICKS["up_out"][0] + n * 256, 128), 256)]
            b = bias[:, pl.ds(pl.multiple_of(n * 256, 256), 256)]
            pre = dot(x, v["wu"][:, cols]) + dot_o(lu, w) + b
            cdf = 0.5 * (1.0 + lax.erf(pre * ROOT_HALF))
            put_pair(act, at, (pre * cdf).astype(BF16), cols)
            slope = cdf + pre * (jnp.exp(-0.5 * pre * pre) * ROOT_TAU)
            put_pair(dpre, at, (take_pair(dact, at, cols) * slope).astype(BF16), cols)
            return carry

        lax.fori_loop(0, 4, run, 0)

    def by_pairs(g, work, beside=None):
        def run(p, carry):
            @pl.when(p == 0)
            def _():
                g.shared(2)
                if not beside:
                    g.near(0)
                    g.near(3)

            @pl.when(p == 1)
            def _():
                if beside:
                    beside()
                    g.near(0)
                    g.near(3)
                g.near(1)
                g.near(2)
                g.shared(6)

            @pl.when(p == 2)
            def _():
                g.shared(5)

            @pl.when(p == 3)
            def _():
                for j in ORDER:
                    g.far(j)
                g.shared(7)

            work(lax.rem(z + p + p // 2 - 2 * (p // 3), 4))
            return carry

        lax.fori_loop(0, 4, run, 0)

    by_pairs(g3, forward)
    keep(2, xbuf).start()

    sum_u = LowSum(src.at[1], got.at[1], *sems(2))
    s2 = GroupSum(*[v[n] for n in ("parts", "near", "sent", "half", "full")], *sems(2))
    s1.finish()

    def wide(ref, weight):
        def compute(s, at):
            x = take_pair(ref, at)

            def run(n, carry):
                cols = pl.ds(pl.multiple_of(n * 512, 512), 512)
                put_pair(s.parts, at, dot_t(x, weight[cols]).astype(BF16), cols)
                return carry

            lax.fori_loop(0, 4, run, 0)

        return compute

    keep(2, xbuf).wait()
    g3.finish()
    def low_up():
        src[1] = dot_t(pick(pk, "up_out"), dpre[...]).astype(BF16)
        sum_u.start()

    summed(s2, wide(dpre, v["wu"]), beside=low_up)
    for thing in (joined, dense, down, up, sw):
        thing.finish()
    keep(3, gbuf).wait()
    g2.finish()
    mlp = gbuf

    def forward_down(rows):
        mlp[rows] = dot(act[rows], v["wn"][...]).astype(BF16)

    src[2] = dot_t(pick(pk, "down_in"), act[...]).astype(BF16)
    sum_n = LowSum(src.at[2], got.at[2], *sems(2))
    sum_n.start()
    tiles(4, 256, forward_down)
    total_u = sum_u.total()
    dmid[...] = dot_o(total_u, pick(pk, "up_in"))
    all_u = LowGather(v["sum_u"], *sems(2))
    all_u.start(total_u)
    s2.arrive()
    all_n = LowGather(v["sum_n"], *sems(2))
    g4 = GroupGather(xbuf, *sems(2))
    for j in ORDER:
        rows = slice(j * 32, (j + 1) * 32)
        dmid[rows] = v["gos"][rows].astype(F32) + norm_back(mid[rows], gain2[...], dmid[rows] + s2.total(rows))
        xbuf[pl.ds(pl.multiple_of(own * 128 + j * 32, 32), 32)] = dmid[rows].astype(BF16)
        g4.put(j)
    spread = Spread(split, whole, *sems(11))

    def product(first, count, low, ref):
        for n in range(0, count, 2):
            spread.put(first + n, dot(low[...], ref[:, n * 128:n * 128 + 256]))

    def early_products():
        all_n.start(sum_n.total())
        spread.mark(pk[:8, PICKS["hot"][0]:PICKS["hot"][0] + 128])
        product(2, 8, v["low_u"], dpre)
        product(10, 8, v["low_g"], act)
        all_u.wait()
        product(28, 2, v["sum_u"], v["cols"].at[2])

    grads = c4

    def context(at):
        x = take_pair(xbuf, at)
        ld = dot_t(pick(pk, "dense_out"), x).astype(BF16)
        for n, rows in enumerate(row_pair(at)):
            v["low_d"][:, rows] = ld[:, n * 128:n * 128 + 128]
        value = dot_t(x, v["wd"][...]) + dot_o(ld, pick(pk, "dense_in"))
        value = value.astype(BF16).astype(F32)
        mix = take_pair(ctx, at).astype(F32)
        for h in range(4):
            first = h // 2 * 128
            g = value[:, first:first + 128]
            here = (lane // 64) == h % 2
            d = -jnp.sum(jnp.where(here, g * mix[:, first:first + 128], 0.0), axis=-1, keepdims=True)
            high, middle, lowest = cast_parts(d)
            if h % 2:
                g = jnp.concatenate([g[:, 64:], g[:, :64]], axis=1)
            put_pair(grads.at[h], at, jnp.where(lane < 64, g, jnp.where(lane == 64, high, jnp.where(
                lane == 65, middle, jnp.where(lane == 66, lowest, 0.0)))).astype(BF16))

    by_pairs(g4, context, early_products)
    keep(1, xbuf).start()

    s3 = GroupSum(mlp, *[v[n] for n in ("near2", "sent2", "half2", "full2")], *sems(2))
    for i in range(4):
        s3.give(i)
    def dense_products():
        product(0, 2, v["low_d"], ctx)
        all_d.wait()
        keep(1, xbuf).wait()
        product(26, 2, v["sum_d"], v["cols"].at[1])
        all_n.wait()
        product(30, 2, v["sum_n"], v["cols"].at[3])
        spread.start()

    dense_products()
    hooks_back = {0: s3.far, 1: s3.near_up, 2: s3.near_down, 6: spread.add, 7: spread.deal, 8: s3.pass_on,
                  15: spread.deal_plane}
    dk, dv = v["dact"].at[:, 0:128], v["dact"].at[:, 128:256]

    def head_back(h, carry):
        dk[...] = jnp.zeros_like(dk)
        dv[...] = jnp.zeros_like(dv)
        for i in range(4):
            rows = pl.ds(i * 256, 256)
            q, g = qa[h, rows], grads[h, rows]

            def span(keys, masked):
                k = ka[h, keys]
                score = dot_t(k, q)
                if masked:
                    score = jnp.where(mask, score, MASKED)
                p = jnp.exp(score)
                ds = (p * dot_t(va[h, keys], g)).astype(BF16)
                dk[keys] += dot(ds, q)
                dv[keys] += dot(p.astype(BF16), g)
                return dot_o(k, ds)

            dq = span(rows, True)
            if i:
                dq = dq + span(pl.ds(0, i * 256), False)
            grads[h, rows] = (dq * 0.125).T.astype(BF16)
            for n, hook in hooks_back.items():
                if n % 4 == i:
                    @pl.when(h == n // 4)
                    def _(hook=hook):
                        hook()
        ka[h] = dk[...].astype(BF16)
        va[h] = dv[...].astype(BF16)
        return carry

    lax.fori_loop(0, 4, head_back, 0)
    dfused = v["dfused"]
    for h in (0, 2):
        dfused[:, h * 192:h * 192 + 384] = jnp.concatenate(
            [ref[k, :, :64] for k in (h, h + 1) for ref in (grads, ka, va)], axis=1)

    src[3] = dot_t(pick(pk, "joined_out"), dfused[...]).astype(BF16)
    sum_q = LowSum(src.at[3], got.at[3], *sems(2))
    sum_q.start()
    s4 = GroupSum(*[v[n] for n in ("parts", "near", "sent", "half", "full")], *sems(2))
    s2.finish()
    all_q = LowGather(v["sum_q"], *sems(2))

    def early_low():
        value = sum_q.total()
        all_q.start(value)

    spread2 = LastSpread(split2, whole2, *sems(10))

    def late_products():
        spread2.mark(pk[:8, PICKS["hot"][0]:PICKS["hot"][0] + 128])
        for n in range(0, 6, 2):
            spread2.put(n, dot(v["low_q"][...], dfused[:, n * 128:n * 128 + 256]))

    summed(s4, wide(dfused, v["wj"]), early_low, late_products)
    all_q.wait()
    spread2.put(6, dot(v["sum_q"][...], v["cols"][0]))
    spread2.start()
    layer, mine_grad = v["layer"], v["gos"]
    pairs = [(sub(mine_grad, j), sub(back, j), sub(back, j)) for j in range(4)] + [(layer, out, out)]
    sw2 = Swap(pairs, *sems(3))
    s3.arrive()
    for thing in (g4, s3):
        thing.finish()
    layer[...] = (mid[...] + bias_n[...] + dot_o(v["sum_n"][:, mine_rows], pick(pk, "down_out")) + s3.total()).astype(BF16)
    sw2.start(4)
    spread.share()
    correction = dot_o(v["sum_q"][:, mine_rows], pick(pk, "joined_in"))
    spread2.add()
    spread2.deal()
    s4.arrive()
    for j in ORDER:
        rows = slice(j * 32, (j + 1) * 32)
        value = dmid[rows] + norm_back(xs[rows].astype(F32), gain1[...], correction[rows] + s4.total(rows))
        mine_grad[rows] = value.astype(BF16)
        sw2.start(j)
        if j == 3:
            spread2.line()
    spread2.share_groups()
    spread.finish()
    spread2.share_line()
    for n in range(5):
        sw2.wait(n)
    spread2.finish()
    for thing in (s4, sw2):
        thing.finish()


SCRATCH = dict(
    lines=((8, 2048), F32), bias=((1, 1024), F32), bias_one=((768,), F32), mine=((16, TRADED), BF16), pk=((16, PICKED), BF16),
    xs=((128, 2048), BF16), xbuf=((1024, 2048), BF16), gbuf=((1024, 2048), BF16), gos=((128, 2048), BF16),
    wj=((2048, 768), BF16), wd=((256, 2048), BF16), wn=((1024, 2048), BF16), wu=((2048, 1024), BF16),
    qa=((4, 1024, 128), BF16), ka=((4, 1024, 128), BF16), va=((4, 1024, 128), BF16), c4=((4, 1024, 128), BF16),
    ctx=((1024, 256), BF16), dfused=((1024, 768), BF16), act=((1024, 1024), BF16),
    dpre=((1024, 1024), BF16), dact=((1024, 1024), F32), mid=((128, 2048), F32), dmid=((128, 2048), F32),
    layer=((128, 2048), BF16), cols=((4, 1024, 256), BF16),
    low_src=((4, 16, 1024), BF16), low_got=((4, 8, 16, 128), BF16),
    low_q=((16, 1024), BF16), low_g=((16, 1024), BF16), low_u=((16, 1024), BF16), low_d=((16, 1024), BF16),
    sum_d=((16, 1024), BF16), sum_u=((16, 1024), BF16), sum_n=((16, 1024), BF16), sum_q=((16, 1024), BF16),
    parts=((1024, 2048), BF16), near=((4, 128, 2048), BF16), sent=((3, 128, 2048), BF16), half=((2, 64, 2048), BF16),
    full=((2, 128, 2048), BF16), near2=((4, 128, 2048), BF16), sent2=((3, 128, 2048), BF16),
    half2=((2, 64, 2048), BF16), full2=((2, 128, 2048), BF16))


def block_call(*args):
    outs = [shape(128, 2048), shape(128, 2048), shape(8, 16, 3, 8, 128), shape(8, 8, 16, 8, 128),
            shape(8, 12, 8, 128), shape(8, 8, 4, 8, 128)]
    low = [DMA((8,)), DMA((8,))]
    sums = [DMA((10,)), DMA((10,))]
    gather = GroupGather.SEMS
    kinds = [DMA((8,)), DMA((8,)), DMA((4,)), *Swap.sems(11), *PlaneGather.SEMS * 4, *gather, *gather, *low, *sums,
             *gather, *low, *low, *sums, *low, *low, *low, *gather, *Spread.SCRATCH, *sums, *low, *sums, *low,
             *LastSpread.SCRATCH, *Swap.sems(5)]
    return pl.pallas_call(
        block_kernel, out_shape=outs, in_specs=specs(pltpu.SMEM, *[ANY] * 22), out_specs=specs(*[ANY] * 6),
        scratch_shapes=[VMEM(*s) for s in SCRATCH.values()] + kinds,
        compiler_params=params(1, 60), name="block")(*args)


def write_kernel(split, whole, split2, whole2, back, layer, *outs):
    joined_out, dense_in, up_out, down_in, *wholes, grad, out = outs
    for ref, count, first in ((dense_in, 2, 0), (up_out, 8, 2), (down_in, 8, 10)):
        for n in range(count):
            for half in (0, 1):
                k = 2 * (first + n) + half
                ref[:, half * 8:half * 8 + 8, n * 128:n * 128 + 128] = split[:, k // 3, k % 3].astype(F32)
    for n in range(6):
        for half in (0, 1):
            joined_out[:, half * 8:half * 8 + 8, n * 128:n * 128 + 128] = split2[:, 2 * n + half].astype(F32)
    for i, ref in enumerate(wholes):
        for t in range(8):
            for n in range(2):
                for half in (0, 1):
                    at = t * 256 + n * 128
                    k = n * 2 + half
                    block_in = whole2[:, t, k] if i == 0 else whole[:, t, i * 4 + k]
                    ref[:, half * 8:half * 8 + 8, at:at + 128] = block_in.astype(F32)
    grad[...] = back[...].astype(F32)
    out[...] = layer[...]


def write_call(split, whole, split2, whole2, back, layer):
    widths = [768, 256, 1024, 1024] + [2048] * 4
    rows = pl.BlockSpec((64, 2048), lambda b: (b, 0))
    return pl.pallas_call(
        write_kernel, grid=(2,),
        out_shape=[shape(8, 16, n, dtype=F32) for n in widths] + [shape(128, 2048, dtype=F32), shape(128, 2048)],
        in_specs=[pl.BlockSpec((4, *n, 8, 128), lambda b, n=n: (b, *[0] * len(n), 0, 0)) for n in ((16, 3), (8, 16), (12,), (8, 4))
                  ] + [rows, rows],
        out_specs=[pl.BlockSpec((4, 16, n), lambda b: (b, 0, 0)) for n in widths] + [rows, rows],
        compiler_params=plain(58), name="write")(split, whole, split2, whole2, back, layer)


def local(tokens, grad_out, adapter_ids, first_gain, first_shift, joined_weight, joined_bias, dense_weight,
          dense_bias, second_gain, second_shift, up_weight, up_bias, down_weight, down_bias, joined_adapt_in,
          joined_adapt_out, dense_adapt_in, dense_adapt_out, up_adapt_in, up_adapt_out, down_adapt_in,
          down_adapt_out):
    turn = lambda a: jnp.swapaxes(a, 1, 2)
    flat = lambda a: a.reshape(128, a.shape[2])
    vectors = [a.reshape(1, -1) for a in (first_gain, first_shift, second_gain, second_shift, dense_bias, down_bias,
                                          up_bias)] + [joined_bias]
    adapters = dict(joined_in=turn(joined_adapt_in), joined_out=joined_adapt_out, dense_in=turn(dense_adapt_in),
                    dense_out=dense_adapt_out, up_in=turn(up_adapt_in), up_out=up_adapt_out,
                    down_in=turn(down_adapt_in), down_out=down_adapt_out)
    back, layer, split, whole, split2, whole2 = block_call(
        adapter_ids, tokens, grad_out, *vectors, *[flat(adapters[n]) for n in SETS], joined_weight, dense_weight,
        down_weight, up_weight)
    joined_out, dense_in, up_out, down_in, joined_in, dense_out, up_in, down_out, grad_tokens, layer_out = write_call(
        split, whole, split2, whole2, back, layer)
    return (layer_out, grad_tokens, turn(joined_in), joined_out, turn(dense_in), dense_out, turn(up_in), up_out,
            turn(down_in), down_out)


def solution(mesh):
    fine = Mesh(mesh.devices.reshape(2, 4, 2, 2, 4), AXES)
    rows, cols = P(FSDP, TP), P(TP, FSDP)
    tok = P((*FSDP, *TP), None)
    last, middle, one = P(None, None, TP), P(None, TP, None), P(TP)
    return jax.shard_map(
        local, mesh=fine,
        in_specs=(tok, tok, P(FSDP), P(), P(), rows, one, cols, P(), P(), P(), rows, one, cols, P(), P(), last,
                  middle, P(), P(), last, middle, P()),
        out_specs=(tok, tok, P(), last, middle, P(), P(), last, middle, P()), check_vma=False)
```
